32 devices in a mesh: row: 4 (over y, x), col: 8 (over z, core).
Axes of the slice: x: 2, y: 2, z: 4, core: 2. Of those that a mesh axis runs over, the one named last changes fastest.
Arguments:
- text: bfloat16 [32, 2, 502, 768], P(('row', 'col')), may hold values from -6 to 6
- memory: bfloat16 [32, 10, 768], P(('row', 'col')), may hold values from -6 to 6
- tail_lengths: int32 [32], P(('row', 'col')), may hold values from 125 to 502, as said below
- picture_starts: int32 [32, 2], P(('row', 'col')), may hold values from 0 to 246, as said below
- grad_out: bfloat16 [32, 2, 522, 768], P(('row', 'col')), may hold values from -6 to 6
- query_weight: bfloat16 [768, 768], P('row', 'col'), may hold values from -0.21875 to 0.21875
- key_weight: bfloat16 [768, 768], P('row', 'col'), may hold values from -0.21875 to 0.21875
- value_weight: bfloat16 [768, 768], P('row', 'col'), may hold values from -0.21875 to 0.21875
- out_weight: bfloat16 [768, 768], P('row', 'col'), may hold values from -2.5 to 2.5
- up_weight: bfloat16 [768, 3072], P('row', 'col'), may hold values from -0.21875 to 0.21875
- down_weight: bfloat16 [3072, 768], P('row', 'col'), may hold values from -0.109375 to 0.109375
- query_bias: bfloat16 [768], P('col'), may hold values from -4 to 4
- value_bias: bfloat16 [768], P('col'), may hold values from -4 to 4
- out_bias: bfloat16 [768], P('col'), may hold values from -4 to 4
- attention_gain: bfloat16 [768], P('col'), may hold values from 0.5 to 1.5
- attention_shift: bfloat16 [768], P('col'), may hold values from -4 to 4
- up_bias: bfloat16 [3072], P('col'), may hold values from -4 to 4
- down_bias: bfloat16 [768], P('col'), may hold values from -4 to 4
- output_gain: bfloat16 [768], P('col'), may hold values from 0.5 to 1.5
- output_shift: bfloat16 [768], P('col'), may hold values from -4 to 4
Outputs:
- layer_output: bfloat16 [32, 2, 522, 768], P(('row', 'col'))
- text_grad: bfloat16 [32, 2, 502, 768], P(('row', 'col'))
- memory_grad: bfloat16 [32, 10, 768], P(('row', 'col'))
- query_weight_grad: float32 [768, 768], P('row', 'col')
- key_weight_grad: float32 [768, 768], P('row', 'col')
- value_weight_grad: float32 [768, 768], P('row', 'col')
- out_weight_grad: float32 [768, 768], P('row', 'col')
- up_weight_grad: float32 [768, 3072], P('row', 'col')
- down_weight_grad: float32 [3072, 768], P('row', 'col')
- query_bias_grad: float32 [768], P('col')
- value_bias_grad: float32 [768], P('col')
- out_bias_grad: float32 [768], P('col')
- attention_gain_grad: float32 [768], P('col')
- attention_shift_grad: float32 [768], P('col')
- up_bias_grad: float32 [3072], P('col')
- down_bias_grad: float32 [768], P('col')
- output_gain_grad: float32 [768], P('col')
- output_shift_grad: float32 [768], P('col')
The draws below stay inside these ranges and needn't reach their ends.
Inputs may be any that keep to these rules, and one draw needn't show every extreme that they name: `tail_lengths`: valid text positions of each sequence's second segment; some sequence has 502 and some 502 // 4. `picture_starts`: start of each segment's picture span among its 502 text positions; the span of 256 tokens ends inside them.
All inputs are finite; a program needn't handle non-finite values.
Results may differ from the reference program's by a relative error of at most 0.02.
Values may be sent and summed in bfloat16 or wider, within the bound.
A program may use at most 192 MiB of HBM per device.

```python
import jax
import jax.numpy as jnp
from jax import lax

D = 768
HEADS = 12
HEAD_DIM = 64
FF = 3072
MEMORY = 10
TEXT = 502
PICTURE = 256
SEG_ROWS = 522
SEQS = 32


def draw_tail_lengths(key, part):
    first, second = jax.random.split(key)
    lengths = jax.random.randint(first, (SEQS,), TEXT // 4, TEXT + 1)
    place = jax.random.randint(second, (), 0, SEQS)
    lengths = lengths.at[place].set(TEXT)
    return lengths.at[(place + 1) % SEQS].set(TEXT // 4).astype(jnp.int32)


def draw_picture_starts(key, part):
    first, second = jax.random.split(jax.random.fold_in(key, 7))
    starts = jax.random.randint(first, (SEQS, 2), 0, TEXT - PICTURE + 1)
    place = jax.random.randint(second, (), 0, SEQS)
    starts = starts.at[place, 0].set(0)
    return starts.at[(place + 1) % SEQS, 1].set(TEXT - PICTURE).astype(jnp.int32)


def with_spikes(drawn, stream_key, source, target, parts, factor):
    def block_of(dim):
        return (jnp.arange(drawn.shape[dim]) // (drawn.shape[dim] // parts)).reshape((-1,) + (1,) * (drawn.ndim - 1 - dim))

    first = jax.random.permutation(stream_key, parts)[block_of(target)]
    far = (block_of(target) + parts // 2) % parts
    return jnp.where((block_of(source) == first) | (block_of(source) == far), factor * drawn, drawn)


def levels(key, shape, shards, low, high):
    factor_of, own = 1.0, jax.random.fold_in(key, 6)
    for axis_at, parts in shards:
        heights = jnp.exp(jax.random.uniform(jax.random.fold_in(own, axis_at), (parts,), jnp.float32, low / len(shards), high / len(shards)))
        factor_of = factor_of * jnp.repeat(heights, shape[axis_at] // parts).reshape([-1 if axis == axis_at else 1 for axis in range(len(shape))])
    return factor_of


def gaussian(rng, extent, width, limit, pieces=(), kind=jnp.bfloat16):
    level = levels(rng, extent, pieces, -0.22, 0.18) if pieces else 1.0
    array = jax.random.normal(rng, extent, jnp.float32) * width * level
    return jnp.minimum(jnp.maximum(array, -limit), limit).astype(kind)


def bell_draw_with(own_key, extent, width, reach, pieces, heavy, dtype=jnp.bfloat16):
    array = width * jax.random.normal(own_key, extent, jnp.float32)
    if pieces:
        array = array * levels(own_key, extent, pieces, -0.22, 0.18)
    return jnp.clip(with_spikes(array, jax.random.fold_in(own_key, 3), *heavy), -reach, reach).astype(dtype)


def setup_inputs(seed: int = 0) -> dict:
    key_list = jax.random.split(jax.random.key(seed), 21)
    return {
        "text": bell_draw_with(key_list[0], (SEQS, 2, TEXT, D), 1.0, 6.0, ((0, 32),), (0, 3, 32, 2.75)),
        "memory": gaussian(key_list[1], (SEQS, MEMORY, D), 1.0, 6.0, ((0, 32),)),
        "tail_lengths": draw_tail_lengths(jax.random.fold_in(key_list[20], 71), 0),
        "picture_starts": draw_picture_starts(jax.random.fold_in(key_list[20], 71), 0),
        "grad_out": bell_draw_with(key_list[4], (SEQS, 2, SEG_ROWS, D), 1.0, 6.0, ((0, 32),), (0, 3, 32, 2.75)),
        "query_weight": gaussian(key_list[5], (D, D), D ** -0.5, 0.21875, ((0, 4), (1, 8))),
        "key_weight": gaussian(key_list[6], (D, D), D ** -0.5, 0.21875, ((0, 4), (1, 8))),
        "value_weight": gaussian(key_list[7], (D, D), D ** -0.5, 0.21875, ((0, 4), (1, 8))),
        "out_weight": gaussian(key_list[8], (D, D), (max(D // 128, 1)) ** -0.5, 2.5, ((0, 4), (1, 8))),
        "up_weight": gaussian(key_list[9], (D, FF), D ** -0.5, 0.21875, ((0, 4), (1, 8))),
        "down_weight": gaussian(key_list[10], (FF, D), FF ** -0.5, 0.109375, ((0, 4), (1, 8))),
        "query_bias": gaussian(key_list[11], (D,), 0.3, 4.0, ((0, 8),)),
        "value_bias": gaussian(key_list[12], (D,), 0.3, 4.0, ((0, 8),)),
        "out_bias": gaussian(key_list[13], (D,), 0.3, 4.0, ((0, 8),)),
        "attention_gain": jnp.clip(1.0 + 0.1 * jax.random.normal(key_list[14], (D,), jnp.float32), 0.5, 1.5).astype(jnp.bfloat16),
        "attention_shift": gaussian(key_list[15], (D,), 0.3, 4.0, ((0, 8),)),
        "up_bias": gaussian(key_list[16], (FF,), 0.3, 4.0, ((0, 8),)),
        "down_bias": gaussian(key_list[17], (D,), 0.3, 4.0, ((0, 8),)),
        "output_gain": jnp.clip(1.0 + 0.1 * jax.random.normal(key_list[18], (D,), jnp.float32), 0.5, 1.5).astype(jnp.bfloat16),
        "output_shift": gaussian(key_list[19], (D,), 0.3, 4.0, ((0, 8),)),
    }


@jax.custom_vjp
def low(v):
    return lax.optimization_barrier(v.astype(jnp.bfloat16)).astype(jnp.float32)

@jax.custom_vjp
def low_back(v):
    return v

def low_keep(v):
    return (low(v), None)

def low_pass(kept, grad):
    return (grad,)

def back_keep(v):
    return (v, None)

def back_low(kept, grad):
    return (low(grad),)
low.defvjp(low_keep, low_pass)
low_back.defvjp(back_keep, back_low)
epsilon = 1e-06
masked_score = -1e+30

def narrow_both(inputs):
    return low_back(low(inputs))

def layer_norm(inputs, gain, shift):
    center = lax.optimization_barrier(jnp.mean(inputs, axis=-1, keepdims=True))
    centred = inputs - center
    spread = lax.optimization_barrier(jnp.mean(centred * centred, axis=-1, keepdims=True))
    return centred * lax.rsqrt(spread + epsilon) * gain + shift

def gelu_exact(inputs):
    return jax.nn.gelu(inputs, approximate=False)

def allowed_pairs(length, start):
    place = jnp.arange(SEG_ROWS)
    offset = place - MEMORY
    is_text = (offset >= 0) & (offset < TEXT)
    usable = jnp.logical_not(is_text & (offset >= length))
    picture = is_text & (offset >= start) & (offset < start + PICTURE)
    causal = place[None, :] <= place[:, None]
    inside = picture[:, None] & picture[None, :]
    return usable[None, :] & (causal | inside)

def project(left, right):
    return jnp.dot(left, right, precision=lax.Precision.HIGHEST, preferred_element_type=jnp.float32)

def attend(query, keys, values, allowed):
    query_heads = query.reshape(SEG_ROWS, HEADS, HEAD_DIM)
    key_heads = keys.reshape(SEG_ROWS, HEADS, HEAD_DIM)
    value_heads = values.reshape(SEG_ROWS, HEADS, HEAD_DIM)
    scores = jnp.einsum('qhd,khd->hqk', query_heads, key_heads, precision=lax.Precision.HIGHEST) * HEAD_DIM ** (-0.5)
    scores = jnp.where(allowed[None], low_back(scores), masked_score)
    probs = low(jax.nn.softmax(scores, axis=-1))
    mixed = jnp.einsum('hqk,khd->qhd', probs, value_heads, precision=lax.Precision.HIGHEST)
    return mixed.reshape(SEG_ROWS, HEADS * HEAD_DIM)

def segment_forward(inputs, length, start, weights):
    query_weight, key_weight, value_weight, out_weight, up_weight, down_weight, query_bias, value_bias, out_bias, attention_gain, attention_shift, up_bias, down_bias, output_gain, output_shift = weights
    narrow_in = low(inputs)
    query = narrow_both(project(narrow_in, query_weight) + query_bias)
    keys = narrow_both(project(narrow_in, key_weight))
    values = narrow_both(project(narrow_in, value_weight) + value_bias)
    mixed = narrow_both(attend(query, keys, values, allowed_pairs(length, start)))
    branch = low_back(project(mixed, out_weight) + out_bias)
    hidden = layer_norm(inputs + branch, attention_gain, attention_shift)
    upward = low_back(project(low(hidden), up_weight) + up_bias)
    activated = low(gelu_exact(upward))
    downward = low_back(project(activated, down_weight) + down_bias)
    return layer_norm(hidden + downward, output_gain, output_shift)

def sequence_forward(weights, seq_text, seq_memory, length, starts):
    carried = seq_memory
    results = []
    for segment in range(2):
        inputs = jnp.concatenate([carried, seq_text[segment], carried], axis=0)
        seg_length = TEXT if segment == 0 else length
        result = segment_forward(inputs, seg_length, starts[segment], weights)
        results.append(result)
        carried = result[MEMORY + TEXT:]
    return jnp.stack(results)

def reference(text, memory, tail_lengths, picture_starts, grad_out, query_weight, key_weight, value_weight, out_weight, up_weight, down_weight, query_bias, value_bias, out_bias, attention_gain, attention_shift, up_bias, down_bias, output_gain, output_shift):
    weights = tuple((item.astype(jnp.float32) for item in (query_weight, key_weight, value_weight, out_weight, up_weight, down_weight, query_bias, value_bias, out_bias, attention_gain, attention_shift, up_bias, down_bias, output_gain, output_shift)))

    def one_sequence(totals, items):
        seq_text, seq_memory, length, starts, cotangent = items

        def forward(weights_now, text_now, memory_now):
            return sequence_forward(weights_now, text_now, memory_now, length, starts)
        result, pullback = jax.vjp(forward, weights, seq_text.astype(jnp.float32), seq_memory.astype(jnp.float32))
        weight_grads, seq_text_grad, seq_memory_grad = pullback(cotangent.astype(jnp.float32))
        totals = jax.tree.map(jnp.add, totals, weight_grads)
        return (totals, (result.astype(jnp.bfloat16), seq_text_grad.astype(jnp.bfloat16), seq_memory_grad.astype(jnp.bfloat16)))
    zeros = jax.tree.map(jnp.zeros_like, weights)
    totals, (outputs, text_grads, memory_grads) = lax.scan(one_sequence, zeros, (text, memory, tail_lengths, picture_starts, grad_out))
    return (outputs, text_grads, memory_grads, totals[0], totals[1], totals[2], totals[3], totals[4], totals[5], totals[6], totals[7], totals[8], totals[9], totals[10], totals[11], totals[12], totals[13], totals[14])
```

```python
import functools

import jax
import jax.numpy as jnp
from jax import lax
from jax.experimental import pallas as pl
from jax.experimental.pallas import tpu as pltpu
from jax.sharding import PartitionSpec as P

HEADS = 12
HEAD_DIM = 64
MEMORY = 10
TEXT = 502
PICTURE = 256
SEG_ROWS = 522
ROWS = 528
KEYS = 640
QUAD = 256
F32 = jnp.float32
BF16 = jnp.bfloat16

EPSILON = 1e-06
MASKED = -1e30
LOG2E = 1.4426950408889634

ERFC_SLOPE = 0.4 * 0.7071067811865476
ERFC_POLY = (0.22562816739082336, 0.2265406847000122, 0.20122945308685303, 0.19582846760749817, 0.07433333992958069, 0.09543049335479736, 0.07776277512311935, -0.1374378800392151, 0.040684547275304794)


def nn(left, right):
    return lax.dot_general(left, right, (((1,), (0,)), ((), ())), preferred_element_type=F32)


def nt(left, right):
    return lax.dot_general(left, right, (((1,), (1,)), ((), ())), preferred_element_type=F32)


def norm_forward(inputs, gain, shift):
    center = jnp.mean(inputs, axis=-1, keepdims=True)
    centred = inputs - center
    spread = jnp.mean(centred * centred, axis=-1, keepdims=True)
    inverse = lax.rsqrt(spread + EPSILON)
    normed = centred * inverse
    return normed * gain + shift, normed, inverse


def norm_backward(grad, normed, inverse, gain):
    scaled = grad * gain
    first = jnp.mean(scaled, axis=-1, keepdims=True)
    second = jnp.mean(scaled * normed, axis=-1, keepdims=True)
    return (scaled - first - normed * second) * inverse


def column_sum(values):
    return jnp.sum(values, axis=0, keepdims=True)


def gelu_pair(upward):
    size = jnp.abs(upward)
    t = 1.0 / (1.0 + ERFC_SLOPE * size)
    poly = jnp.full_like(t, ERFC_POLY[-1])
    for coefficient in ERFC_POLY[-2::-1]:
        poly = poly * t + coefficient
    bell = jnp.exp2(upward * upward * (-0.5 * LOG2E))
    tail = 0.5 * bell * t * poly
    phi = jnp.where(upward < 0.0, tail, 1.0 - tail)
    return upward * phi, phi + upward * (bell * 0.3989422804014327)


def attention_forward_kernel(
    info, x, wq, wk, wv, wo, vq, vv, vo, gain, shift,
    q_out, k_out, v_out, e_out, total_out, mixed_out, hidden_out, normed_out, inverse_out,
    narrow, bias, k_pad, v_pad, branch,
):
    step = pl.program_id(0)

    @pl.when(step == 0)
    def _():
        narrow[...] = x[...].astype(BF16)
        branch[...] = jnp.zeros_like(branch)
        total_out[...] = jnp.ones_like(total_out)
        k_pad[...] = jnp.zeros_like(k_pad)
        v_pad[...] = jnp.zeros_like(v_pad)
        length, start = info[0], info[1]
        row = lax.broadcasted_iota(jnp.int32, (ROWS, KEYS), 0)
        col = lax.broadcasted_iota(jnp.int32, (ROWS, KEYS), 1)
        low, high = start + MEMORY, start + MEMORY + PICTURE
        text = (col >= MEMORY) & (col < MEMORY + TEXT)
        usable = jnp.logical_not(text & (col >= MEMORY + length)) & (col < SEG_ROWS)
        inside = (row >= low) & (row < high) & (col >= low) & (col < high)
        allowed = usable & ((col <= row) | inside)
        bias[...] = jnp.where(allowed, 0.0, MASKED)

    xb = narrow[...]
    q = ((nt(xb, wq[...]) + vq[...]).astype(BF16).astype(F32) * HEAD_DIM**-0.5).astype(BF16)
    q_out[...] = q
    k_pad[:ROWS, :] = nt(xb, wk[...]).astype(BF16)
    v_pad[:ROWS, :] = (nt(xb, wv[...]) + vv[...]).astype(BF16)
    k_out[...] = k_pad[:ROWS, :]
    v_out[...] = v_pad[:ROWS, :]
    lane = lax.broadcasted_iota(jnp.int32, (ROWS, 128), 1)
    totals = total_out[...]
    for pair in range(2):
        at = slice(128 * pair, 128 * pair + 128)
        halves = []
        for half in range(2):
            mine = (lane < HEAD_DIM) if half == 0 else (lane >= HEAD_DIM)
            qm = jnp.where(mine, q_out[:, at], jnp.zeros((), BF16))
            scores = nt(qm, k_pad[:, at]) + bias[...]
            peak = jnp.max(scores, axis=-1, keepdims=True)
            expos = jnp.exp2((scores - peak) * LOG2E)
            total = jnp.sum(expos, axis=-1, keepdims=True)
            narrow_e = expos.astype(BF16)
            e_out[2 * pair + half] = narrow_e
            totals = jnp.where(lane == step * 4 + 2 * pair + half, total, totals)
            halves.append(nn(narrow_e, v_pad[:, at]) / total)
        mixed_out[:, at] = jnp.where(lane < HEAD_DIM, halves[0], halves[1]).astype(BF16)
    total_out[...] = totals
    branch[...] += nt(mixed_out[...], wo[...])

    @pl.when(step == pl.num_programs(0) - 1)
    def _():
        hidden, normed, inverse = norm_forward(
            x[...] + (branch[...] + vo[...]), gain[...], shift[...]
        )
        hidden_out[...] = hidden
        normed_out[...] = normed
        inverse_out[...] = jnp.broadcast_to(inverse, inverse_out.shape)


def whole(shape):
    return pl.BlockSpec(shape, lambda i: (0,) * len(shape))


def params(limit=58):
    return pltpu.CompilerParams(
        dimension_semantics=("arbitrary",), vmem_limit_bytes=limit * 1024 * 1024
    )


def attention_forward(info, x, weights):
    width = x.shape[1]
    steps = width // QUAD
    row_block = pl.BlockSpec((QUAD, width), lambda i: (i, 0))
    col_block = pl.BlockSpec((width, QUAD), lambda i: (0, i))
    bias_block = pl.BlockSpec((1, QUAD), lambda i: (0, i))
    rows_block = pl.BlockSpec((ROWS, QUAD), lambda i: (0, i))
    vector = whole((1, width))
    full = whole((ROWS, width))
    stats = whole((ROWS, 128))
    shape = jax.ShapeDtypeStruct
    return pl.pallas_call(
        attention_forward_kernel,
        grid=(steps,),
        in_specs=[
            pl.BlockSpec(memory_space=pltpu.SMEM),
            full, row_block, row_block, row_block, col_block,
            bias_block, bias_block, vector, vector, vector,
        ],
        out_specs=[
            rows_block, rows_block, rows_block,
            pl.BlockSpec((4, ROWS, KEYS), lambda i: (i, 0, 0)),
            stats, rows_block, full, full, stats,
        ],
        out_shape=[
            shape((ROWS, width), BF16), shape((ROWS, width), BF16), shape((ROWS, width), BF16),
            shape((HEADS, ROWS, KEYS), BF16),
            shape((ROWS, 128), F32), shape((ROWS, width), BF16),
            shape((ROWS, width), F32), shape((ROWS, width), F32), shape((ROWS, 128), F32),
        ],
        scratch_shapes=[
            pltpu.VMEM((ROWS, width), BF16),
            pltpu.VMEM((ROWS, KEYS), F32),
            pltpu.VMEM((KEYS, QUAD), BF16),
            pltpu.VMEM((KEYS, QUAD), BF16),
            pltpu.VMEM((ROWS, width), F32),
        ],
        compiler_params=params(),
        name="attention_forward",
    )(
        info, x, weights["q"], weights["k"], weights["v"], weights["o"],
        weights["vq"], weights["vv"], weights["vo"], weights["ag"], weights["as"],
    )


def feed_forward_kernel(
    hidden, wu, wd, vu, vd, gain, shift, act_out, slope_out, y_out, normed_out, inverse_out,
    narrow, total,
):
    step = pl.program_id(0)

    @pl.when(step == 0)
    def _():
        narrow[...] = hidden[...].astype(BF16)
        total[...] = jnp.zeros_like(total)

    upward = nt(narrow[...], wu[...]) + vu[...]
    act, slope = gelu_pair(upward)
    act_out[...] = act.astype(BF16)
    slope_out[...] = slope.astype(BF16)
    total[...] += nt(act_out[...], wd[...])

    @pl.when(step == pl.num_programs(0) - 1)
    def _():
        y, normed, inverse = norm_forward(
            hidden[...] + (total[...] + vd[...]), gain[...], shift[...]
        )
        y_out[...] = y
        normed_out[...] = normed
        inverse_out[...] = jnp.broadcast_to(inverse, inverse_out.shape)


UNITS = 512


def feed_forward(hidden, weights):
    width = hidden.shape[1]
    units = weights["u"].shape[0]
    vector = whole((1, width))
    full = whole((ROWS, width))
    block = pl.BlockSpec((ROWS, UNITS), lambda i: (0, i))
    shape = jax.ShapeDtypeStruct
    return pl.pallas_call(
        feed_forward_kernel,
        grid=(units // UNITS,),
        in_specs=[
            full,
            pl.BlockSpec((UNITS, width), lambda i: (i, 0)),
            pl.BlockSpec((width, UNITS), lambda i: (0, i)),
            pl.BlockSpec((1, UNITS), lambda i: (0, i)),
            vector, vector, vector,
        ],
        out_specs=[block, block, full, full, whole((ROWS, 128))],
        out_shape=[
            shape((ROWS, units), BF16), shape((ROWS, units), BF16),
            shape((ROWS, width), F32), shape((ROWS, width), F32), shape((ROWS, 128), F32),
        ],
        scratch_shapes=[pltpu.VMEM((ROWS, width), BF16), pltpu.VMEM((ROWS, width), F32)],
        compiler_params=params(),
        name="feed_forward",
    )(
        hidden, weights["u"], weights["d"], weights["vu"], weights["vd"],
        weights["og"], weights["os"],
    )


def feed_backward_kernel(
    dy, normed2, inverse2, normed1, inverse1, slope, wd, wu, wo, gain2, gain1,
    gd_out, gu_out, gb_out, dfirst_out, gm_out, vu_out, sums_out,
    dsecond, dhidden,
):
    step = pl.program_id(0)

    @pl.when(step == 0)
    def _():
        grad, normed = dy[...], normed2[...]
        sums_out[0:1, :] = column_sum(grad * normed)
        sums_out[1:2, :] = column_sum(grad)
        second = norm_backward(grad, normed, inverse2[:, 0:1], gain2[...])
        dsecond[...] = second
        narrow = second.astype(BF16)
        gd_out[...] = narrow
        sums_out[2:3, :] = column_sum(narrow.astype(F32))
        dhidden[...] = jnp.zeros_like(dhidden)

    up = (nn(gd_out[...], wd[...]) * slope[...].astype(F32)).astype(BF16)
    gu_out[...] = up
    vu_out[...] = column_sum(up.astype(F32))
    dhidden[...] += nn(up, wu[...])

    @pl.when(step == pl.num_programs(0) - 1)
    def _():
        grad, normed = dhidden[...] + dsecond[...], normed1[...]
        sums_out[3:4, :] = column_sum(grad * normed)
        sums_out[4:5, :] = column_sum(grad)
        first = norm_backward(grad, normed, inverse1[:, 0:1], gain1[...])
        dfirst_out[...] = first
        narrow = first.astype(BF16)
        gb_out[...] = narrow
        sums_out[5:6, :] = column_sum(narrow.astype(F32))
        sums_out[6:8, :] = jnp.zeros((2, narrow.shape[1]), F32)
        gm_out[...] = nn(narrow, wo[...]).astype(BF16)


def feed_backward(dy, saved, weights):
    width = dy.shape[1]
    units = weights["u"].shape[0]
    vector = whole((1, width))
    full = whole((ROWS, width))
    stats = whole((ROWS, 128))
    block = pl.BlockSpec((ROWS, UNITS), lambda i: (0, i))
    shape = jax.ShapeDtypeStruct
    return pl.pallas_call(
        feed_backward_kernel,
        grid=(units // UNITS,),
        in_specs=[
            full, full, stats, full, stats, block,
            pl.BlockSpec((width, UNITS), lambda i: (0, i)),
            pl.BlockSpec((UNITS, width), lambda i: (i, 0)),
            whole((width, width)), vector, vector,
        ],
        out_specs=[
            full, block, full, full, full,
            pl.BlockSpec((1, UNITS), lambda i: (0, i)), whole((8, width)),
        ],
        out_shape=[
            shape((ROWS, width), BF16), shape((ROWS, units), BF16), shape((ROWS, width), BF16),
            shape((ROWS, width), F32), shape((ROWS, width), BF16),
            shape((1, units), F32), shape((8, width), F32),
        ],
        scratch_shapes=[pltpu.VMEM((ROWS, width), F32), pltpu.VMEM((ROWS, width), F32)],
        compiler_params=params(),
        name="feed_backward",
    )(
        dy, saved["normed2"], saved["inverse2"], saved["normed1"], saved["inverse1"],
        saved["slope"], weights["d"], weights["u"], weights["o"], weights["og"], weights["ag"],
    )


def attention_backward_kernel(
    q, k, v, e, total, mixed, gm, dfirst, wq, wk, wv,
    gq_out, gk_out, gv_out, dx_out, vq_out, vv_out,
    k_pad, v_pad,
):
    step = pl.program_id(0)

    @pl.when(step == 0)
    def _():
        dx_out[...] = dfirst[...]
        k_pad[...] = jnp.zeros_like(k_pad)
        v_pad[...] = jnp.zeros_like(v_pad)

    k_pad[:ROWS, :] = k[...]
    v_pad[:ROWS, :] = v[...]
    lane = lax.broadcasted_iota(jnp.int32, (ROWS, 128), 1)
    for pair in range(2):
        at = slice(128 * pair, 128 * pair + 128)
        grad = gm[:, at].astype(F32)
        product = grad * mixed[:, at].astype(F32)
        totals = total[...]
        rates, inners = [], []
        for half in range(2):
            mine = (lane < HEAD_DIM) if half == 0 else (lane >= HEAD_DIM)
            head = step * 4 + 2 * pair + half
            rate = 1.0 / jnp.sum(jnp.where(lane == head, totals, 0.0), axis=-1, keepdims=True)
            rates.append(rate)
            inners.append(jnp.sum(jnp.where(mine, product, 0.0), axis=-1, keepdims=True) * rate)
        scaled = (grad * jnp.where(lane < HEAD_DIM, rates[0], rates[1])).astype(BF16)
        scaled_t = scaled.T
        query_t = q[:, at].T
        gq, gk, gv = [], [], []
        for half in range(2):
            mine = (lane < HEAD_DIM) if half == 0 else (lane >= HEAD_DIM)
            rows = slice(HEAD_DIM * half, HEAD_DIM * half + HEAD_DIM)
            gmm = jnp.where(mine, scaled, jnp.zeros((), BF16))
            dp = nt(gmm, v_pad[:, at])
            narrow_e = e[2 * pair + half]
            ds = (narrow_e.astype(F32) * (dp - inners[half])).astype(BF16)
            gq.append(nn(ds, k_pad[:, at]))
            gk.append(nn(query_t[rows, :], ds))
            gv.append(nn(scaled_t[rows, :], narrow_e))
        gq_pair = jnp.where(lane < HEAD_DIM, gq[0], gq[1]) * HEAD_DIM**-0.5
        gq_out[:, at] = gq_pair.astype(BF16)
        gk_out[:, at] = jnp.concatenate(gk, axis=0).T[:ROWS].astype(BF16)
        gv_out[:, at] = jnp.concatenate(gv, axis=0).T[:ROWS].astype(BF16)
    vq_out[...] = column_sum(gq_out[...].astype(F32))
    vv_out[...] = column_sum(gv_out[...].astype(F32))
    dx_out[...] += (
        nn(gq_out[...], wq[...]) + nn(gk_out[...], wk[...]) + nn(gv_out[...], wv[...])
    )


def attention_backward(saved, gm, dfirst, weights):
    width = dfirst.shape[1]
    row_block = pl.BlockSpec((QUAD, width), lambda i: (i, 0))
    rows_block = pl.BlockSpec((ROWS, QUAD), lambda i: (0, i))
    full = whole((ROWS, width))
    sums = pl.BlockSpec((1, QUAD), lambda i: (0, i))
    shape = jax.ShapeDtypeStruct
    return pl.pallas_call(
        attention_backward_kernel,
        grid=(width // QUAD,),
        in_specs=[
            rows_block, rows_block, rows_block,
            pl.BlockSpec((4, ROWS, KEYS), lambda i: (i, 0, 0)),
            whole((ROWS, 128)), rows_block, rows_block, full, row_block, row_block, row_block,
        ],
        out_specs=[rows_block, rows_block, rows_block, full, sums, sums],
        out_shape=[
            shape((ROWS, width), BF16), shape((ROWS, width), BF16), shape((ROWS, width), BF16),
            shape((ROWS, width), F32), shape((1, width), F32), shape((1, width), F32),
        ],
        scratch_shapes=[pltpu.VMEM((KEYS, QUAD), BF16), pltpu.VMEM((KEYS, QUAD), BF16)],
        compiler_params=params(),
        name="attention_backward",
    )(
        saved["q"], saved["k"], saved["v"], saved["e"], saved["total"], saved["mixed"],
        gm, dfirst, weights["q"], weights["k"], weights["v"],
    )


def gather_all(part):
    return lax.all_gather(part, ("row", "col"), axis=0, tiled=False)


def fetch(arguments):
    matrices, vectors = arguments[:6], arguments[6:]
    rows, cols = lax.axis_size("row"), lax.axis_size("col")
    depth, across = matrices[0].shape
    width = depth * rows
    names = ("q", "k", "v", "o")
    square = jnp.concatenate([item.T for item in matrices[:4]], axis=1)
    upper = matrices[4].T.reshape(4, across, depth).transpose(1, 0, 2).reshape(across, 4 * depth)
    lower = matrices[5].T
    line = jnp.concatenate(vectors)
    extra = -(-line.shape[0] // (4 * depth))
    extra += -(across + extra) % 16
    line = jnp.pad(line, (0, extra * 4 * depth - line.shape[0])).reshape(extra, 4 * depth)
    first = gather_all(jnp.concatenate([square, line], axis=0))
    second = gather_all(upper)
    third = gather_all(lower)
    whole_square = (
        first[:, :across].reshape(rows, cols, across, 4, depth)
        .transpose(3, 1, 2, 0, 4).reshape(4, width, width)
    )
    weights = {name: whole_square[at] for at, name in enumerate(names)}
    weights["u"] = (
        second.reshape(rows, cols, across, 4, depth)
        .transpose(1, 3, 2, 0, 4).reshape(4 * width, width)
    )
    weights["d"] = third.reshape(rows, cols, across, 4 * depth).transpose(1, 2, 0, 3).reshape(width, 4 * width)
    lines = first[:cols, across:].reshape(cols, -1).astype(F32)
    at = 0
    for name, item in zip(("vq", "vv", "vo", "ag", "as", "vu", "vd", "og", "os"), vectors):
        weights[name] = lines[:, at : at + item.shape[0]].reshape(1, -1)
        at += item.shape[0]
    return weights


def scatter_all(terms):
    return lax.psum_scatter(terms, ("row", "col"), scatter_dimension=0, tiled=False)


def product_t(left, right):
    return jnp.einsum("rd,re->de", left, right, preferred_element_type=F32).astype(BF16)


def solution_body(
    text, memory, tail_lengths, picture_starts, grad_out, *parameters
):
    rows, cols = lax.axis_size("row"), lax.axis_size("col")
    depth, across = parameters[0].shape
    width = depth * rows
    weights = fetch(parameters)
    full_length = jnp.full((1,), TEXT, jnp.int32)
    pad = jnp.zeros((ROWS - SEG_ROWS, width), F32)

    def forward(edge, words, length, start):
        info = jnp.concatenate([length, start])
        x = jnp.concatenate([edge, words.astype(F32), edge, pad], axis=0)
        q, k, v, e, total, mixed, hidden, normed1, inverse1 = attention_forward(info, x, weights)
        act, slope, y, normed2, inverse2 = feed_forward(hidden, weights)
        saved = dict(
            x=x.astype(BF16), q=q, k=k, v=v, e=e, total=total, mixed=mixed, hidden=hidden.astype(BF16),
            normed1=normed1, inverse1=inverse1, act=act, slope=slope, normed2=normed2, inverse2=inverse2,
        )
        return y, saved

    y1, saved1 = forward(memory[0].astype(F32), text[0, 0], full_length, picture_starts[:, 0])
    y2, saved2 = forward(y1[MEMORY + TEXT : SEG_ROWS], text[0, 1], tail_lengths, picture_starts[:, 1])
    layer_output = jnp.stack([y1[:SEG_ROWS], y2[:SEG_ROWS]]).astype(BF16)[None]

    def backward(dy, saved):
        gd, gu, gb, dfirst, gm, vu, sums = feed_backward(dy, saved, weights)
        gq, gk, gv, dx, vq, vv = attention_backward(saved, gm, dfirst, weights)
        return dx, dict(gd=gd, gu=gu, gb=gb, gq=gq, gk=gk, gv=gv, vu=vu, sums=sums, vq=vq, vv=vv)

    cotangent = jnp.pad(grad_out[0].astype(F32), ((0, 0), (0, ROWS - SEG_ROWS), (0, 0)))
    dx2, grads2 = backward(cotangent[1], saved2)
    edge = dx2[:MEMORY] + dx2[MEMORY + TEXT : SEG_ROWS]
    dy1 = cotangent[0].at[MEMORY + TEXT : SEG_ROWS].add(edge)
    dx1, grads1 = backward(dy1, saved1)
    memory_grad = (dx1[:MEMORY] + dx1[MEMORY + TEXT : SEG_ROWS]).astype(BF16)[None]
    text_grad = jnp.stack(
        [dx1[MEMORY : MEMORY + TEXT], dx2[MEMORY : MEMORY + TEXT]]
    ).astype(BF16)[None]

    def both(name):
        return jnp.concatenate([grads1[name], grads2[name]], axis=0)

    def kept(name):
        return jnp.concatenate([saved1[name], saved2[name]], axis=0)

    lower = product_t(both("gd"), kept("act"))
    lower = lower.reshape(cols, across, rows, 4 * depth).transpose(2, 0, 1, 3)
    lower = scatter_all(lower.reshape(rows * cols, across, 4 * depth))
    upper = product_t(both("gu"), kept("hidden"))
    upper = upper.reshape(cols, 4, across, rows, depth).transpose(3, 0, 2, 1, 4)
    upper = scatter_all(upper.reshape(rows * cols, across, 4 * depth))
    xb = kept("x")
    square = jnp.stack(
        [
            product_t(both("gq"), xb), product_t(both("gk"), xb), product_t(both("gv"), xb),
            product_t(both("gb"), kept("mixed")),
        ]
    )
    square = square.reshape(4, cols, across, rows, depth).transpose(3, 1, 2, 0, 4)
    sums = grads1["sums"] + grads2["sums"]
    vectors = (
        grads1["vq"] + grads2["vq"], grads1["vv"] + grads2["vv"], sums[5], sums[3], sums[4],
        grads1["vu"] + grads2["vu"], sums[2], sums[0], sums[1],
    )
    lines = jnp.concatenate([item.reshape(cols, -1) for item in vectors], axis=1)
    count = lines.shape[1]
    extra = -(-count // (4 * depth))
    extra += -(across + extra) % 16
    lines = jnp.pad(lines, ((0, 0), (0, extra * 4 * depth - count))).astype(BF16)
    lines = jnp.broadcast_to(lines.reshape(1, cols, extra, 4 * depth), (rows, cols, extra, 4 * depth))
    square = jnp.concatenate([square.reshape(rows, cols, across, 4 * depth), lines], axis=2)
    square = scatter_all(square.reshape(rows * cols, across + extra, 4 * depth))
    own = square[:across].astype(F32).reshape(across, 4, depth)
    line = square[across:].astype(F32).reshape(-1)
    result = [own[:, at].T for at in range(4)]
    upper = upper.astype(F32).reshape(across, 4, depth).transpose(2, 1, 0).reshape(depth, 4 * across)
    result += [upper, lower.astype(F32).T]
    at = 0
    for item in vectors:
        size = item.size // cols
        result.append(line[at : at + size])
        at += size
    return (layer_output, text_grad, memory_grad, *result)


def solution(mesh):
    batch, matrix, vector = P(("row", "col")), P("row", "col"), P("col")
    return jax.shard_map(
        solution_body,
        mesh=mesh,
        in_specs=(batch,) * 5 + (matrix,) * 6 + (vector,) * 9,
        out_specs=(batch,) * 3 + (matrix,) * 6 + (vector,) * 9,
        check_vma=False,
    )
```

```python
import functools

import jax
import jax.numpy as jnp
from jax import lax
from jax.experimental import pallas as pl
from jax.experimental.pallas import tpu as pltpu
from jax.sharding import PartitionSpec as P

HEADS = 12
HEAD_DIM = 64
MEMORY = 10
TEXT = 502
PICTURE = 256
SEG_ROWS = 522
ROWS = 528
KEYS = 640
QUAD = 256
UNITS = 512
F32 = jnp.float32
BF16 = jnp.bfloat16

EPSILON = 1e-06
MASKED = -1e30
LOG2E = 1.4426950408889634

ERFC_SLOPE = 0.4 * 0.7071067811865476
ERFC_POLY = (0.22562816739082336, 0.2265406847000122, 0.20122945308685303, 0.19582846760749817, 0.07433333992958069, 0.09543049335479736, 0.07776277512311935, -0.1374378800392151, 0.040684547275304794)


def nn(left, right):
    return lax.dot_general(left, right, (((1,), (0,)), ((), ())), preferred_element_type=F32)


def nt(left, right):
    return lax.dot_general(left, right, (((1,), (1,)), ((), ())), preferred_element_type=F32)


def norm_forward(inputs, gain, shift):
    center = jnp.mean(inputs, axis=-1, keepdims=True)
    centred = inputs - center
    spread = jnp.mean(centred * centred, axis=-1, keepdims=True)
    inverse = lax.rsqrt(spread + EPSILON)
    normed = centred * inverse
    return normed * gain + shift, normed, inverse


def norm_backward(grad, normed, inverse, gain):
    scaled = grad * gain
    first = jnp.mean(scaled, axis=-1, keepdims=True)
    second = jnp.mean(scaled * normed, axis=-1, keepdims=True)
    return (scaled - first - normed * second) * inverse


def column_sum(values):
    return jnp.sum(values, axis=0, keepdims=True)


def gelu_pair(upward):
    size = jnp.abs(upward)
    t = 1.0 / (1.0 + ERFC_SLOPE * size)
    poly = jnp.full_like(t, ERFC_POLY[-1])
    for coefficient in ERFC_POLY[-2::-1]:
        poly = poly * t + coefficient
    bell = jnp.exp2(upward * upward * (-0.5 * LOG2E))
    tail = 0.5 * bell * t * poly
    phi = jnp.where(upward < 0.0, tail, 1.0 - tail)
    return upward * phi, phi + upward * (bell * 0.3989422804014327)


def attention_forward_kernel(
    info, x, wq, wk, wv, wo, vq, vv, vo, gain, shift,
    q_out, k_out, v_out, e_out, total_out, mixed_out, hidden_out, normed_out, inverse_out,
    narrow, narrow_hidden, bias, k_pad, v_pad, branch,
):
    step = pl.program_id(0)

    @pl.when(step == 0)
    def _():
        narrow[...] = x[...].astype(BF16)
        branch[...] = jnp.zeros_like(branch)
        total_out[...] = jnp.ones_like(total_out)
        k_pad[...] = jnp.zeros_like(k_pad)
        v_pad[...] = jnp.zeros_like(v_pad)
        length, start = info[0], info[1]
        row = lax.broadcasted_iota(jnp.int32, (ROWS, KEYS), 0)
        col = lax.broadcasted_iota(jnp.int32, (ROWS, KEYS), 1)
        low, high = start + MEMORY, start + MEMORY + PICTURE
        text = (col >= MEMORY) & (col < MEMORY + TEXT)
        usable = jnp.logical_not(text & (col >= MEMORY + length)) & (col < SEG_ROWS)
        inside = (row >= low) & (row < high) & (col >= low) & (col < high)
        allowed = usable & ((col <= row) | inside)
        bias[...] = jnp.where(allowed, 0.0, MASKED)

    xb = narrow[...]
    q = ((nt(xb, wq[...]) + vq[...]).astype(BF16).astype(F32) * HEAD_DIM**-0.5).astype(BF16)
    q_out[...] = q
    k_pad[:ROWS, :] = nt(xb, wk[...]).astype(BF16)
    v_pad[:ROWS, :] = (nt(xb, wv[...]) + vv[...]).astype(BF16)
    k_out[...] = k_pad[:ROWS, :]
    v_out[...] = v_pad[:ROWS, :]
    lane = lax.broadcasted_iota(jnp.int32, (ROWS, 128), 1)
    totals = total_out[...]
    for pair in range(2):
        at = slice(128 * pair, 128 * pair + 128)
        halves = []
        for half in range(2):
            mine = (lane < HEAD_DIM) if half == 0 else (lane >= HEAD_DIM)
            qm = jnp.where(mine, q_out[:, at], jnp.zeros((), BF16))
            scores = nt(qm, k_pad[:, at]) + bias[...]
            peak = jnp.max(scores, axis=-1, keepdims=True)
            expos = jnp.exp2((scores - peak) * LOG2E)
            total = jnp.sum(expos, axis=-1, keepdims=True)
            narrow_e = expos.astype(BF16)
            e_out[2 * pair + half] = narrow_e
            totals = jnp.where(lane == step * 4 + 2 * pair + half, total, totals)
            halves.append(nn(narrow_e, v_pad[:, at]) / total)
        mixed_out[:, at] = jnp.where(lane < HEAD_DIM, halves[0], halves[1]).astype(BF16)
    total_out[...] = totals
    branch[...] += nt(mixed_out[...], wo[...])

    @pl.when(step == pl.num_programs(0) - 1)
    def _():
        hidden, normed, inverse = norm_forward(
            x[...] + (branch[...] + vo[...]), gain[...], shift[...]
        )
        hidden_out[...] = hidden
        narrow_hidden[...] = hidden.astype(BF16)
        normed_out[...] = normed
        inverse_out[...] = jnp.broadcast_to(inverse, inverse_out.shape)


def whole(shape):
    return pl.BlockSpec(shape, lambda i: (0,) * len(shape))


def params(limit=58):
    return pltpu.CompilerParams(
        dimension_semantics=("arbitrary",), vmem_limit_bytes=limit * 1024 * 1024
    )


def attention_forward(info, x, weights):
    width = x.shape[1]
    steps = width // QUAD
    row_block = pl.BlockSpec((QUAD, width), lambda i: (i, 0))
    col_block = pl.BlockSpec((width, QUAD), lambda i: (0, i))
    bias_block = pl.BlockSpec((1, QUAD), lambda i: (0, i))
    rows_block = pl.BlockSpec((ROWS, QUAD), lambda i: (0, i))
    vector = whole((1, width))
    full = whole((ROWS, width))
    stats = whole((ROWS, 128))
    shape = jax.ShapeDtypeStruct
    return pl.pallas_call(
        attention_forward_kernel,
        grid=(steps,),
        in_specs=[
            pl.BlockSpec(memory_space=pltpu.SMEM),
            full, row_block, row_block, row_block, col_block,
            bias_block, bias_block, vector, vector, vector,
        ],
        out_specs=[
            rows_block, rows_block, rows_block,
            pl.BlockSpec((4, ROWS, KEYS), lambda i: (i, 0, 0)),
            stats, rows_block, full, full, stats, full, full,
        ],
        out_shape=[
            shape((ROWS, width), BF16), shape((ROWS, width), BF16), shape((ROWS, width), BF16),
            shape((HEADS, ROWS, KEYS), BF16),
            shape((ROWS, 128), F32), shape((ROWS, width), BF16),
            shape((ROWS, width), F32), shape((ROWS, width), F32), shape((ROWS, 128), F32),
            shape((ROWS, width), BF16), shape((ROWS, width), BF16),
        ],
        scratch_shapes=[
            pltpu.VMEM((ROWS, KEYS), F32),
            pltpu.VMEM((KEYS, QUAD), BF16),
            pltpu.VMEM((KEYS, QUAD), BF16),
            pltpu.VMEM((ROWS, width), F32),
        ],
        compiler_params=params(),
        name="attention_forward",
    )(
        info, x, weights["q"], weights["k"], weights["v"], weights["o"],
        weights["vq"], weights["vv"], weights["vo"], weights["ag"], weights["as"],
    )


def feed_forward_kernel(
    hidden, narrow, wu, wd, vu, vd, gain, shift, act_out, slope_out, y_out, normed_out, inverse_out,
    total,
):
    step = pl.program_id(0)

    @pl.when(step == 0)
    def _():
        total[...] = jnp.zeros_like(total)

    upward = nn(narrow[...], wu[...]) + vu[...]
    act, slope = gelu_pair(upward)
    act_out[...] = act.astype(BF16)
    slope_out[...] = slope.astype(BF16)
    total[...] += nt(act_out[...], wd[...])

    @pl.when(step == pl.num_programs(0) - 1)
    def _():
        y, normed, inverse = norm_forward(
            hidden[...] + (total[...] + vd[...]), gain[...], shift[...]
        )
        y_out[...] = y
        normed_out[...] = normed
        inverse_out[...] = jnp.broadcast_to(inverse, inverse_out.shape)


def feed_forward(hidden, narrow, weights):
    width = hidden.shape[1]
    units = weights["u"].shape[1]
    vector = whole((1, width))
    full = whole((ROWS, width))
    block = pl.BlockSpec((ROWS, UNITS), lambda i: (0, i))
    shape = jax.ShapeDtypeStruct
    return pl.pallas_call(
        feed_forward_kernel,
        grid=(units // UNITS,),
        in_specs=[
            full, full,
            pl.BlockSpec((width, UNITS), lambda i: (0, i)),
            pl.BlockSpec((width, UNITS), lambda i: (0, i)),
            pl.BlockSpec((1, UNITS), lambda i: (0, i)),
            vector, vector, vector,
        ],
        out_specs=[block, block, full, full, whole((ROWS, 128))],
        out_shape=[
            shape((ROWS, units), BF16), shape((ROWS, units), BF16),
            shape((ROWS, width), F32), shape((ROWS, width), F32), shape((ROWS, 128), F32),
        ],
        scratch_shapes=[pltpu.VMEM((ROWS, width), F32)],
        compiler_params=params(),
        name="feed_forward",
    )(
        hidden, narrow, weights["u"], weights["d"], weights["vu"], weights["vd"],
        weights["og"], weights["os"],
    )


def feed_backward_kernel(
    dy, normed2, inverse2, normed1, inverse1, slope, wd, wu, wo, gain2, gain1,
    gd_out, gu_out, gb_out, dfirst_out, gm_out, vu_out, sums_out,
    dsecond, dhidden,
):
    step = pl.program_id(0)

    @pl.when(step == 0)
    def _():
        grad, normed = dy[...], normed2[...]
        sums_out[0:1, :] = column_sum(grad * normed)
        sums_out[1:2, :] = column_sum(grad)
        second = norm_backward(grad, normed, inverse2[:, 0:1], gain2[...])
        dsecond[...] = second
        narrow = second.astype(BF16)
        gd_out[...] = narrow
        sums_out[2:3, :] = column_sum(narrow.astype(F32))
        dhidden[...] = jnp.zeros_like(dhidden)

    up = (nn(gd_out[...], wd[...]) * slope[...].astype(F32)).astype(BF16)
    gu_out[...] = up
    vu_out[...] = column_sum(up.astype(F32))
    dhidden[...] += nt(up, wu[...])

    @pl.when(step == pl.num_programs(0) - 1)
    def _():
        grad, normed = dhidden[...] + dsecond[...], normed1[...]
        sums_out[3:4, :] = column_sum(grad * normed)
        sums_out[4:5, :] = column_sum(grad)
        first = norm_backward(grad, normed, inverse1[:, 0:1], gain1[...])
        dfirst_out[...] = first
        narrow = first.astype(BF16)
        gb_out[...] = narrow
        sums_out[5:6, :] = column_sum(narrow.astype(F32))
        sums_out[6:8, :] = jnp.zeros((2, narrow.shape[1]), F32)
        gm_out[...] = nn(narrow, wo[...]).astype(BF16)


def feed_backward(dy, saved, weights):
    width = dy.shape[1]
    units = weights["u"].shape[1]
    vector = whole((1, width))
    full = whole((ROWS, width))
    stats = whole((ROWS, 128))
    block = pl.BlockSpec((ROWS, UNITS), lambda i: (0, i))
    shape = jax.ShapeDtypeStruct
    return pl.pallas_call(
        feed_backward_kernel,
        grid=(units // UNITS,),
        in_specs=[
            full, full, stats, full, stats, block,
            pl.BlockSpec((width, UNITS), lambda i: (0, i)),
            pl.BlockSpec((width, UNITS), lambda i: (0, i)),
            whole((width, width)), vector, vector,
        ],
        out_specs=[
            full, block, full, full, full,
            pl.BlockSpec((1, UNITS), lambda i: (0, i)), whole((8, width)),
        ],
        out_shape=[
            shape((ROWS, width), BF16), shape((ROWS, units), BF16), shape((ROWS, width), BF16),
            shape((ROWS, width), F32), shape((ROWS, width), BF16),
            shape((1, units), F32), shape((8, width), F32),
        ],
        scratch_shapes=[pltpu.VMEM((ROWS, width), F32), pltpu.VMEM((ROWS, width), F32)],
        compiler_params=params(),
        name="feed_backward",
    )(
        dy, saved["normed2"], saved["inverse2"], saved["normed1"], saved["inverse1"],
        saved["slope"], weights["d"], weights["u"], weights["o"], weights["og"], weights["ag"],
    )


def attention_backward_kernel(
    q, k, v, e, total, mixed, gm, dfirst, wq, wk, wv,
    gq_out, gk_out, gv_out, dx_out, vq_out, vv_out,
    k_pad, v_pad,
):
    step = pl.program_id(0)

    @pl.when(step == 0)
    def _():
        dx_out[...] = dfirst[...]
        k_pad[...] = jnp.zeros_like(k_pad)
        v_pad[...] = jnp.zeros_like(v_pad)

    k_pad[:ROWS, :] = k[...]
    v_pad[:ROWS, :] = v[...]
    lane = lax.broadcasted_iota(jnp.int32, (ROWS, 128), 1)
    for pair in range(2):
        at = slice(128 * pair, 128 * pair + 128)
        grad = gm[:, at].astype(F32)
        product = grad * mixed[:, at].astype(F32)
        totals = total[...]
        rates, inners = [], []
        for half in range(2):
            mine = (lane < HEAD_DIM) if half == 0 else (lane >= HEAD_DIM)
            head = step * 4 + 2 * pair + half
            rate = 1.0 / jnp.sum(jnp.where(lane == head, totals, 0.0), axis=-1, keepdims=True)
            rates.append(rate)
            inners.append(jnp.sum(jnp.where(mine, product, 0.0), axis=-1, keepdims=True) * rate)
        scaled = (grad * jnp.where(lane < HEAD_DIM, rates[0], rates[1])).astype(BF16)
        scaled_t = scaled.T
        query_t = q[:, at].T
        gq, gk, gv = [], [], []
        for half in range(2):
            mine = (lane < HEAD_DIM) if half == 0 else (lane >= HEAD_DIM)
            rows = slice(HEAD_DIM * half, HEAD_DIM * half + HEAD_DIM)
            gmm = jnp.where(mine, scaled, jnp.zeros((), BF16))
            dp = nt(gmm, v_pad[:, at])
            narrow_e = e[2 * pair + half]
            ds = (narrow_e.astype(F32) * (dp - inners[half])).astype(BF16)
            gq.append(nn(ds, k_pad[:, at]))
            gk.append(nn(query_t[rows, :], ds))
            gv.append(nn(scaled_t[rows, :], narrow_e))
        gq_pair = jnp.where(lane < HEAD_DIM, gq[0], gq[1]) * HEAD_DIM**-0.5
        gq_out[:, at] = gq_pair.astype(BF16)
        gk_out[:, at] = jnp.concatenate(gk, axis=0).T[:ROWS].astype(BF16)
        gv_out[:, at] = jnp.concatenate(gv, axis=0).T[:ROWS].astype(BF16)
    vq_out[...] = column_sum(gq_out[...].astype(F32))
    vv_out[...] = column_sum(gv_out[...].astype(F32))
    dx_out[...] += (
        nn(gq_out[...], wq[...]) + nn(gk_out[...], wk[...]) + nn(gv_out[...], wv[...])
    )


def attention_backward(saved, gm, dfirst, weights):
    width = dfirst.shape[1]
    row_block = pl.BlockSpec((QUAD, width), lambda i: (i, 0))
    rows_block = pl.BlockSpec((ROWS, QUAD), lambda i: (0, i))
    full = whole((ROWS, width))
    sums = pl.BlockSpec((1, QUAD), lambda i: (0, i))
    shape = jax.ShapeDtypeStruct
    return pl.pallas_call(
        attention_backward_kernel,
        grid=(width // QUAD,),
        in_specs=[
            rows_block, rows_block, rows_block,
            pl.BlockSpec((4, ROWS, KEYS), lambda i: (i, 0, 0)),
            whole((ROWS, 128)), rows_block, rows_block, full, row_block, row_block, row_block,
        ],
        out_specs=[rows_block, rows_block, rows_block, full, sums, sums],
        out_shape=[
            shape((ROWS, width), BF16), shape((ROWS, width), BF16), shape((ROWS, width), BF16),
            shape((ROWS, width), F32), shape((1, width), F32), shape((1, width), F32),
        ],
        scratch_shapes=[pltpu.VMEM((KEYS, QUAD), BF16), pltpu.VMEM((KEYS, QUAD), BF16)],
        compiler_params=params(),
        name="attention_backward",
    )(
        saved["q"], saved["k"], saved["v"], saved["e"], saved["total"], saved["mixed"],
        gm, dfirst, weights["q"], weights["k"], weights["v"],
    )


ROWS_MESH = 4
LINES = 16
MESH_IDS = pl.DeviceIdType.MESH
Z_UP, Z_DOWN, ACROSS, ALONG, HALF_ACROSS, HALF_ALONG = range(6)
SHARE = 6


class Place:
    def __init__(self, cols):
        self.row, self.col = lax.axis_index("row"), lax.axis_index("col")
        self.length = cols // 2
        self.core = lax.rem(self.col, 2)
        self.line = lax.div(self.col, 2)
        self.across_row = self.row + 1 - 2 * lax.rem(self.row, 2)
        self.along_row = self.row + 2 - 4 * lax.div(self.row, 2)
        self.corner_row = 3 - self.row
        self.across = (self.across_row, self.col)
        self.along = (self.along_row, self.col)
        self.up = (self.row, self.col + 2)
        self.down = (self.row, self.col - 2)
        self.other_core = 1 - self.core
        self.partner = (self.row, self.col + 1 - 2 * self.core)

    def greet(self):
        barrier = pltpu.get_barrier_semaphore()

        def signal(device):
            pl.semaphore_signal(barrier, inc=1, device_id=device, device_id_type=MESH_IDS)

        signal(self.across)
        signal(self.along)
        signal(self.partner)
        pl.when(self.line > 0)(lambda: signal(self.down))
        pl.when(self.line < self.length - 1)(lambda: signal(self.up))
        has_down = lax.div(self.line + self.length - 1, self.length)
        has_up = lax.div(2 * self.length - 2 - self.line, self.length)
        pl.semaphore_wait(barrier, 3 + has_down + has_up)

    def at_distance(self, distance, visit):
        if distance == 0:
            visit(self.line, None)
        else:
            below, above = self.line - distance, self.line + distance
            pl.when(below >= 0)(lambda: visit(below, True))
            pl.when(above < self.length)(lambda: visit(above, False))


def splits(count):
    first = count // 32 * 16
    return ((0, first), (first, count - first))


def gather_kernel(
    square, upper, lower, wq, wk, wv, wo, lines, whole_upper, whole_lower, gathered, send, recv, own
):
    rows, cols = ROWS_MESH, lines.shape[0]
    place = Place(cols)
    depth, across = upper.shape[0], lower.shape[0]
    sources = (square, upper, lower)

    def target(which, row, col, part=None):
        if which == 0:
            view, count = gathered.at[row * cols + col], square.shape[0]
            begin, size = part if part else (0, count)
            return view.at[pl.ds(begin, size)]
        count, wide = sources[which].shape
        array, high, side = (whole_upper, row, col) if which == 1 else (whole_lower, col, row)
        begin, size = part if part else (0, count)
        return array.at[
            pl.ds(pl.multiple_of(high * count + begin, 16), size),
            pl.ds(pl.multiple_of(side * wide, 128), wide),
        ]

    def copy(which, kind, row, line, device, part=None, mine=None, arrival=None):
        col = 2 * line + (place.core if mine is None else mine)
        there = target(which, row, col, part)
        here = there if arrival is None else sources[which]
        return pltpu.make_async_remote_copy(
            src_ref=here, dst_ref=there,
            send_sem=send.at[which, kind, line], recv_sem=recv.at[which, kind, line],
            device_id=device, device_id_type=MESH_IDS,
        )

    place.greet()
    keeps = []
    for which in range(3):
        keep = pltpu.make_async_copy(
            sources[which], target(which, place.row, place.col), own.at[which]
        )
        keep.start()
        keeps.append(keep)

    def both(which):
        return splits(sources[which].shape[0])

    def by_line(which, distance):
        def visit(line, upward):
            first = True if upward is None else None
            args = (place.row, line)
            if upward is not None:
                kind = Z_UP if upward else Z_DOWN
                copy(which, kind, *args, place.down).wait_recv()
            if upward is None or upward:
                pl.when(place.line < place.length - 1)(
                    lambda: copy(which, Z_UP, *args, place.up, arrival=first).start()
                )
            if upward is None or not upward:
                pl.when(place.line > 0)(
                    lambda: copy(which, Z_DOWN, *args, place.down, arrival=first).start()
                )
            copy(which, ACROSS, *args, place.across, arrival=first).start()
            copy(which, ALONG, *args, place.along, arrival=first).start()
            copy(which, SHARE, *args, place.partner, arrival=first).start()

        place.at_distance(distance, visit)

    def by_side(which, distance):
        halves = both(which)

        def visit(line, upward):
            copy(which, ACROSS, place.across_row, line, place.across).wait_recv()
            copy(which, HALF_ALONG, place.across_row, line, place.along, halves[1]).start()
            copy(which, SHARE + 1, place.across_row, line, place.partner).start()
            copy(which, ALONG, place.along_row, line, place.along).wait_recv()
            copy(which, HALF_ACROSS, place.along_row, line, place.across, halves[0]).start()
            copy(which, SHARE + 2, place.along_row, line, place.partner).start()

        place.at_distance(distance, visit)

    def by_corner(which, distance):
        halves = both(which)

        def visit(line, upward):
            copy(which, HALF_ACROSS, place.corner_row, line, place.across, halves[0]).wait_recv()
            copy(which, SHARE + 3, place.corner_row, line, place.partner, halves[0]).start()
            copy(which, HALF_ALONG, place.corner_row, line, place.along, halves[1]).wait_recv()
            copy(which, SHARE + 4, place.corner_row, line, place.partner, halves[1]).start()

        place.at_distance(distance, visit)

    def from_partner(which):
        halves = both(which)
        for distance in range(place.length):

            def visit(line, upward):
                mine = place.other_core
                for kind, row, part in (
                    (0, place.row, None), (1, place.across_row, None), (2, place.along_row, None),
                    (3, place.corner_row, halves[0]), (4, place.corner_row, halves[1]),
                ):
                    copy(which, SHARE + kind, row, line, place.partner, part, mine=mine).wait_recv()

            place.at_distance(distance, visit)

    def drain(which):
        halves = both(which)
        for distance in range(place.length):

            def visit(line, upward):
                args = (place.row, line)
                first = True if upward is None else None
                if upward is None or upward:
                    pl.when(place.line < place.length - 1)(
                        lambda: copy(which, Z_UP, *args, place.up, arrival=first).wait_send()
                    )
                if upward is None or not upward:
                    pl.when(place.line > 0)(
                        lambda: copy(which, Z_DOWN, *args, place.down, arrival=first).wait_send()
                    )
                copy(which, ACROSS, *args, place.across, arrival=first).wait_send()
                copy(which, ALONG, *args, place.along, arrival=first).wait_send()
                copy(which, SHARE, *args, place.partner, arrival=first).wait_send()
                copy(which, HALF_ALONG, place.across_row, line, place.along, halves[1]).wait_send()
                copy(which, HALF_ACROSS, place.along_row, line, place.across, halves[0]).wait_send()
                copy(which, SHARE + 1, place.across_row, line, place.partner).wait_send()
                copy(which, SHARE + 2, place.along_row, line, place.partner).wait_send()
                copy(which, SHARE + 3, place.corner_row, line, place.partner, halves[0]).wait_send()
                copy(which, SHARE + 4, place.corner_row, line, place.partner, halves[1]).wait_send()

            place.at_distance(distance, visit)

    length = place.length
    finish = length + 2
    for step in range(finish + 4):
        for which in range(3):
            distance = step - 2 * which
            if 0 <= distance < length:
                by_line(which, distance)
            if 1 <= distance < length + 1:
                by_side(which, distance - 1)
            if 2 <= distance < length + 2:
                by_corner(which, distance - 2)
        if step == finish:
            from_partner(0)
            keeps[0].wait()
            outs = (wq, wk, wv, wo)
            for col in range(cols):
                for at, out in enumerate(outs):
                    out[across * col : across * col + across, :] = jnp.concatenate(
                        [
                            gathered[row * cols + col, :across, depth * at : depth * at + depth]
                            for row in range(rows)
                        ],
                        axis=1,
                    )
                lines[col] = gathered[col, across:, :128].astype(F32)
    for which in range(1, 3):
        from_partner(which)
        keeps[which].wait()
    for which in range(3):
        drain(which)


def pack_kernel(wq, wk, wv, wo, wd, vectors, square, lower):
    across, depth = wq.shape[1], wq.shape[0]
    square[:across, :] = jnp.concatenate(
        [item[...].astype(F32).T for item in (wq, wk, wv, wo)], axis=1
    ).astype(BF16)
    square[across:, :] = jnp.zeros((LINES, square.shape[1]), BF16)
    square[across : across + LINES, :128] = vectors[...]
    lower[...] = wd[...].astype(F32).T.astype(BF16)


def fetch_by_kernel(arguments):
    matrices, vectors = arguments[:6], arguments[6:]
    rows, cols = lax.axis_size("row"), lax.axis_size("col")
    depth, across = matrices[0].shape
    width = depth * rows
    units = matrices[4].shape[1] * cols
    table = jnp.stack([*vectors[:5], *vectors[6:]])
    table = jnp.concatenate([table, vectors[5].reshape(-1, across)], axis=0)
    table = jnp.pad(table, ((0, LINES - table.shape[0]), (0, 128 - across)))
    shape = jax.ShapeDtypeStruct
    square, lower = pl.pallas_call(
        pack_kernel,
        out_shape=[shape((across + LINES, 4 * depth), BF16), shape((across, matrices[5].shape[0]), BF16)],
        in_specs=[pl.BlockSpec(memory_space=pltpu.VMEM)] * 6,
        out_specs=[pl.BlockSpec(memory_space=pltpu.VMEM)] * 2,
        name="pack",
    )(*matrices[:4], matrices[5], table)
    anywhere, local = pl.BlockSpec(memory_space=pl.ANY), pl.BlockSpec(memory_space=pltpu.VMEM)
    kinds = (3, SHARE + 5, cols // 2)
    wq, wk, wv, wo, lines, upper, lower = pl.pallas_call(
        gather_kernel,
        out_shape=[shape((width, width), BF16)] * 4
        + [shape((cols, LINES, 128), F32), shape((width, units), BF16), shape((width, units), BF16)],
        in_specs=[anywhere] * 3,
        out_specs=[local] * 5 + [anywhere] * 2,
        scratch_shapes=[
            pltpu.VMEM((rows * cols, across + LINES, 4 * depth), BF16),
            pltpu.SemaphoreType.DMA(kinds), pltpu.SemaphoreType.DMA(kinds), pltpu.SemaphoreType.DMA((3,)),
        ],
        compiler_params=pltpu.CompilerParams(
            collective_id=0, has_side_effects=True, vmem_limit_bytes=40 * 1024 * 1024
        ),
        name="gather",
    )(square, matrices[4], lower)
    names = ("vq", "vv", "vo", "ag", "as", "vd", "og", "os")
    table = lines[:, :, :across]
    weights = dict(q=wq, k=wk, v=wv, o=wo, u=upper, d=lower)
    for at, name in enumerate(names):
        weights[name] = table[:, at].reshape(1, -1)
    weights["vu"] = table[:, len(names) : len(names) + units // cols // across].reshape(1, -1)
    return weights


def scatter_kernel(square, upper, lower, square_out, upper_out, lower_out, *scratch):
    mine, theirs, corner, side, lined = (scratch[3 * at : 3 * at + 3] for at in range(5))
    send, recv, own = scratch[15:]
    rows, cols = ROWS_MESH, square.shape[0] // ROWS_MESH
    place = Place(cols)
    outs = (square_out, upper_out, lower_out)
    length = place.length

    def source(which, row, col):
        count, wide = outs[which].shape
        if which == 0:
            return square.at[row * cols + col]
        array, high, level = (upper, row, col) if which == 1 else (lower, col, row)
        return array.at[
            pl.ds(pl.multiple_of(high * count, 16), count),
            pl.ds(pl.multiple_of(level * wide, 128), wide),
        ]

    def load(which, row, line):
        return pltpu.make_async_copy(
            source(which, row, 2 * line + place.core),
            mine[which].at[row * length + line], own.at[which, row * length + line],
        )

    def share(which, row, line, core):
        at = row * length + line
        return pltpu.make_async_remote_copy(
            src_ref=source(which, row, 2 * line + core), dst_ref=theirs[which].at[at],
            send_sem=send.at[which, SHARE + row, line], recv_sem=recv.at[which, SHARE + row, line],
            device_id=place.partner, device_id_type=MESH_IDS,
        )

    def remote(which, kind, line, here, there, device):
        return pltpu.make_async_remote_copy(
            src_ref=here, dst_ref=there,
            send_sem=send.at[which, kind, line], recv_sem=recv.at[which, kind, line],
            device_id=device, device_id_type=MESH_IDS,
        )

    def corner_copy(which, kind, line):
        begin, size = splits(outs[which].shape[0])[kind - HALF_ACROSS]
        part = pl.ds(begin, size)
        here = mine[which].at[place.corner_row * length + line, part]
        there = corner[which].at[line, part]
        return remote(which, kind, line, here, there, place.across if kind == HALF_ACROSS else place.along)

    def side_copy(which, kind, line):
        row, device = (place.across_row, place.across) if kind == ACROSS else (place.along_row, place.along)
        here = mine[which].at[row * length + line]
        return remote(which, kind, line, here, side[which].at[kind - ACROSS, line], device)

    def line_copy(which, kind, line):
        here = mine[which].at[place.row * length + line]
        return remote(which, kind, line, here, lined[which].at[kind, line], place.up if kind == Z_UP else place.down)

    def add(which, at, arrived, part=None):
        block = mine[which].at[at] if part is None else mine[which].at[at, pl.ds(*part)]
        block[...] = (block[...].astype(F32) + arrived[...].astype(F32)).astype(BF16)

    place.greet()

    def spread(distance, visit):
        place.at_distance(distance, lambda line, upward: visit(line))

    farthest = range(length - 1, -1, -1)
    order = ("corner_row", "across_row", "along_row", "row")
    for which in range(3):
        for distance in farthest:

            def begin(line):
                for name in order:
                    row = getattr(place, name)
                    load(which, row, line).start()
                    share(which, row, line, place.other_core).start()

            spread(distance, begin)

    def merge(which, row, line):
        load(which, row, line).wait()
        share(which, row, line, place.core).wait_recv()
        at = row * length + line
        add(which, at, theirs[which].at[at])

    def cores(which, distance):
        def visit(line):
            merge(which, place.corner_row, line)
            merge(which, place.across_row, line)
            corner_copy(which, HALF_ACROSS, line).start()
            corner_copy(which, HALF_ALONG, line).start()
            merge(which, place.along_row, line)
            merge(which, place.row, line)

        spread(distance, visit)

    def corners(which, distance):
        first, second = splits(outs[which].shape[0])

        def visit(line):
            corner_copy(which, HALF_ACROSS, line).wait_recv()
            add(which, place.along_row * length + line, corner[which].at[line, pl.ds(*first)], first)
            corner_copy(which, HALF_ALONG, line).wait_recv()
            add(which, place.across_row * length + line, corner[which].at[line, pl.ds(*second)], second)
            side_copy(which, ALONG, line).start()
            side_copy(which, ACROSS, line).start()

        spread(distance, visit)

    def sides(which, distance):
        def visit(line):
            at = place.row * length + line
            side_copy(which, ACROSS, line).wait_recv()
            add(which, at, side[which].at[0, line])
            side_copy(which, ALONG, line).wait_recv()
            add(which, at, side[which].at[1, line])

        spread(distance, visit)

    def lines(which, distance):
        def visit(line, downward):
            at = place.row * length + line
            kind = Z_DOWN if downward else Z_UP
            onward = place.line < length - 1 if downward else place.line > 0

            @pl.when(onward)
            def _():
                line_copy(which, kind, line).wait_recv()
                add(which, at, lined[which].at[kind, line])

            line_copy(which, kind, line).start()

        place.at_distance(distance, visit)

    def result(which):
        at = place.row * length + place.line
        for kind, there in ((Z_UP, place.line > 0), (Z_DOWN, place.line < length - 1)):

            @pl.when(there)
            def _():
                line_copy(which, kind, place.line).wait_recv()
                add(which, at, lined[which].at[kind, place.line])

        outs[which][...] = mine[which][at].astype(F32)

    def drain(which):
        for distance in farthest:

            def visit(line, downward):
                for row in range(rows):
                    share(which, row, line, place.other_core).wait_send()
                for kind in (HALF_ACROSS, HALF_ALONG):
                    corner_copy(which, kind, line).wait_send()
                for kind in (ACROSS, ALONG):
                    side_copy(which, kind, line).wait_send()
                if downward is not None:
                    line_copy(which, Z_DOWN if downward else Z_UP, line).wait_send()

            place.at_distance(distance, visit)

    for step in range(length + 3 + 4):
        for which in range(3):
            stage = step - 2 * which
            if 0 <= stage < length:
                cores(which, length - 1 - stage)
            if 1 <= stage < length + 1:
                corners(which, length - stage)
            if 2 <= stage < length + 2:
                sides(which, length + 1 - stage)
            if 3 <= stage < length + 2:
                lines(which, length + 2 - stage)
            if stage == length + 2:
                result(which)
    for which in range(3):
        drain(which)


def scatter_by_kernel(square, upper, lower):
    cols = square.shape[0] // ROWS_MESH
    length = cols // 2
    count, wide = square.shape[1:]
    blocks = (
        (count, wide),
        (upper.shape[0] // ROWS_MESH, upper.shape[1] // cols),
        (lower.shape[0] // cols, lower.shape[1] // ROWS_MESH),
    )
    kinds = (3, SHARE + ROWS_MESH, length)
    anywhere, local = pl.BlockSpec(memory_space=pl.ANY), pl.BlockSpec(memory_space=pltpu.VMEM)
    buffers = [
        pltpu.VMEM((*lead, *block), BF16)
        for lead in ((ROWS_MESH * length,), (ROWS_MESH * length,), (length,), (2, length), (2, length))
        for block in blocks
    ]
    return pl.pallas_call(
        scatter_kernel,
        out_shape=[jax.ShapeDtypeStruct(block, F32) for block in blocks],
        in_specs=[anywhere] * 3,
        out_specs=[local] * 3,
        scratch_shapes=[
            *buffers,
            pltpu.SemaphoreType.DMA(kinds), pltpu.SemaphoreType.DMA(kinds),
            pltpu.SemaphoreType.DMA((3, ROWS_MESH * length)),
        ],
        compiler_params=pltpu.CompilerParams(
            collective_id=1, has_side_effects=True, vmem_limit_bytes=50 * 1024 * 1024
        ),
        name="scatter",
    )(square, upper, lower)


def product_kernel(left1, left2, right1, right2, out, turned):
    @pl.when(pl.program_id(0) == 0)
    def _():
        turned[0] = left1[...].T
        turned[1] = left2[...].T

    out[...] = (nn(turned[0], right1[...]) + nn(turned[1], right2[...])).astype(BF16)


def product_t(left1, left2, right1, right2):
    width, units = left1.shape[1], right1.shape[1]
    block = pl.BlockSpec((ROWS, UNITS), lambda i: (0, i))
    return pl.pallas_call(
        product_kernel,
        grid=(units // UNITS,),
        in_specs=[whole((ROWS, width))] * 2 + [block] * 2,
        out_specs=pl.BlockSpec((width, UNITS), lambda i: (0, i)),
        out_shape=jax.ShapeDtypeStruct((width, units), BF16),
        scratch_shapes=[pltpu.VMEM((2, width, ROWS), BF16)],
        compiler_params=params(),
        name="weight_gradient",
    )(left1, left2, right1, right2)


def square_kernel(
    gq1, gq2, gk1, gk2, gv1, gv2, gb1, gb2, x1, x2, mixed1, mixed2, vectors, wide, out, total
):
    rows = ROWS_MESH
    cols = out.shape[0] // rows
    across, depth = vectors.shape[1] // cols, vectors.shape[1] // rows
    lefts = ((gq1, gq2), (gk1, gk2), (gv1, gv2), (gb1, gb2))
    for at, (left1, left2) in enumerate(lefts):
        right1, right2 = (x1, x2) if at < 3 else (mixed1, mixed2)
        total[at] = (nn(left1[...].T, right1[...]) + nn(left2[...].T, right2[...])).astype(BF16)
    share = wide.shape[1] // cols // across
    for col in range(cols):
        begin = across * col
        narrow = jnp.concatenate(
            [vectors[:, begin : begin + across]]
            + [wide[:, across * (col * share + at) : across * (col * share + at + 1)] for at in range(share)]
            + [jnp.zeros((LINES - 8 - share, across), F32)],
            axis=0,
        )
        narrow = jnp.pad(narrow, ((0, 0), (0, out.shape[2] - across))).astype(BF16)
        for row in range(rows):
            block = row * cols + col
            out[block, :across, :] = jnp.concatenate(
                [total[at, begin : begin + across, depth * row : depth * row + depth] for at in range(4)],
                axis=1,
            )
            out[block, across:, :] = narrow


def square_gradients(grads1, grads2, saved1, saved2, vectors, wide, cols):
    width = vectors.shape[1]
    operands = []
    for name in ("gq", "gk", "gv", "gb"):
        operands += [grads1[name], grads2[name]]
    operands += [saved1["x"], saved2["x"], saved1["mixed"], saved2["mixed"], vectors, wide]
    local = pl.BlockSpec(memory_space=pltpu.VMEM)
    return pl.pallas_call(
        square_kernel,
        in_specs=[local] * len(operands),
        out_specs=local,
        out_shape=jax.ShapeDtypeStruct((ROWS_MESH * cols, width // cols + LINES, width), BF16),
        scratch_shapes=[pltpu.VMEM((4, width, width), BF16)],
        compiler_params=pltpu.CompilerParams(vmem_limit_bytes=58 * 1024 * 1024),
        name="square_gradients",
    )(*operands)


def gather_all(part):
    return lax.all_gather(part, ("row", "col"), axis=0, tiled=False)


def fetch(arguments):
    matrices, vectors = arguments[:6], arguments[6:]
    rows, cols = lax.axis_size("row"), lax.axis_size("col")
    depth, across = matrices[0].shape
    width = depth * rows
    names = ("q", "k", "v", "o")
    square = jnp.concatenate([item.T for item in matrices[:4]], axis=1)
    upper = matrices[4].T.reshape(4, across, depth).transpose(1, 0, 2).reshape(across, 4 * depth)
    lower = matrices[5].T
    line = jnp.concatenate(vectors)
    extra = -(-line.shape[0] // (4 * depth))
    extra += -(across + extra) % 16
    line = jnp.pad(line, (0, extra * 4 * depth - line.shape[0])).reshape(extra, 4 * depth)
    first = gather_all(jnp.concatenate([square, line], axis=0))
    second = gather_all(upper)
    third = gather_all(lower)
    whole_square = (
        first[:, :across].reshape(rows, cols, across, 4, depth)
        .transpose(3, 1, 2, 0, 4).reshape(4, width, width)
    )
    weights = {name: whole_square[at] for at, name in enumerate(names)}
    weights["u"] = (
        second.reshape(rows, cols, across, 4, depth)
        .transpose(0, 4, 1, 3, 2).reshape(width, 4 * width)
    )
    weights["d"] = third.reshape(rows, cols, across, 4 * depth).transpose(1, 2, 0, 3).reshape(width, 4 * width)
    lines = first[:cols, across:].reshape(cols, -1).astype(F32)
    at = 0
    for name, item in zip(("vq", "vv", "vo", "ag", "as", "vu", "vd", "og", "os"), vectors):
        weights[name] = lines[:, at : at + item.shape[0]].reshape(1, -1)
        at += item.shape[0]
    return weights


def scatter_all(terms):
    return lax.psum_scatter(terms, ("row", "col"), scatter_dimension=0, tiled=False)


def scatter(square, upper, lower, lines):
    rows, cols = lax.axis_size("row"), lax.axis_size("col")
    width = square.shape[1]
    depth, across = width // rows, width // cols
    square = square.reshape(4, cols, across, rows, depth).transpose(3, 1, 2, 0, 4)
    square = square.reshape(rows, cols, across, 4 * depth)
    count = lines.shape[1]
    extra = -(-count // (4 * depth))
    extra += -(across + extra) % 16
    lines = jnp.pad(lines, ((0, 0), (0, extra * 4 * depth - count))).astype(BF16)
    lines = jnp.broadcast_to(lines.reshape(1, cols, extra, 4 * depth), (rows, cols, extra, 4 * depth))
    square = jnp.concatenate([square, lines], axis=2)
    square = scatter_all(square.reshape(rows * cols, across + extra, 4 * depth)).astype(F32)
    upper = upper.reshape(rows, depth, cols, 4 * across).transpose(0, 2, 1, 3)
    upper = scatter_all(upper.reshape(rows * cols, depth, 4 * across)).astype(F32)
    lower = lower.reshape(cols, across, rows, 4 * depth).transpose(2, 0, 1, 3)
    lower = scatter_all(lower.reshape(rows * cols, across, 4 * depth)).astype(F32)
    return square[:across], upper, lower, square[across:].reshape(-1)[:count]


def solution_body(
    text, memory, tail_lengths, picture_starts, grad_out, *parameters
):
    rows, cols = lax.axis_size("row"), lax.axis_size("col")
    depth, across = parameters[0].shape
    width = depth * rows
    by_kernel = rows == ROWS_MESH and cols % 2 == 0 and depth % 32 == 0 and across % 32 == 0
    by_kernel = by_kernel and 4 * across % 128 == 0
    weights = fetch_by_kernel(parameters) if by_kernel else fetch(parameters)
    full_length = jnp.full((1,), TEXT, jnp.int32)
    pad = jnp.zeros((ROWS - SEG_ROWS, width), F32)

    def forward(edge, words, length, start):
        info = jnp.concatenate([length, start])
        x = jnp.concatenate([edge, words.astype(F32), edge, pad], axis=0)
        q, k, v, e, total, mixed, hidden, normed1, inverse1, xb, hb = attention_forward(info, x, weights)
        act, slope, y, normed2, inverse2 = feed_forward(hidden, hb, weights)
        saved = dict(
            x=xb, q=q, k=k, v=v, e=e, total=total, mixed=mixed, hidden=hb,
            normed1=normed1, inverse1=inverse1, act=act, slope=slope, normed2=normed2, inverse2=inverse2,
        )
        return y, saved

    y1, saved1 = forward(memory[0].astype(F32), text[0, 0], full_length, picture_starts[:, 0])
    y2, saved2 = forward(y1[MEMORY + TEXT : SEG_ROWS], text[0, 1], tail_lengths, picture_starts[:, 1])
    layer_output = jnp.stack([y1[:SEG_ROWS], y2[:SEG_ROWS]]).astype(BF16)[None]

    def backward(dy, saved):
        gd, gu, gb, dfirst, gm, vu, sums = feed_backward(dy, saved, weights)
        gq, gk, gv, dx, vq, vv = attention_backward(saved, gm, dfirst, weights)
        return dx, dict(gd=gd, gu=gu, gb=gb, gq=gq, gk=gk, gv=gv, vu=vu, sums=sums, vq=vq, vv=vv)

    cotangent = jnp.pad(grad_out[0].astype(F32), ((0, 0), (0, ROWS - SEG_ROWS), (0, 0)))
    dx2, grads2 = backward(cotangent[1], saved2)
    edge = dx2[:MEMORY] + dx2[MEMORY + TEXT : SEG_ROWS]
    dy1 = cotangent[0].at[MEMORY + TEXT : SEG_ROWS].add(edge)
    dx1, grads1 = backward(dy1, saved1)
    memory_grad = (dx1[:MEMORY] + dx1[MEMORY + TEXT : SEG_ROWS]).astype(BF16)[None]
    text_grad = jnp.stack(
        [dx1[MEMORY : MEMORY + TEXT], dx2[MEMORY : MEMORY + TEXT]]
    ).astype(BF16)[None]

    upper = product_t(saved1["hidden"], saved2["hidden"], grads1["gu"], grads2["gu"])
    lower = product_t(grads1["gd"], grads2["gd"], saved1["act"], saved2["act"])
    sums = grads1["sums"] + grads2["sums"]
    wide = grads1["vu"] + grads2["vu"]
    parts = (grads1["vq"] + grads2["vq"], grads1["vv"] + grads2["vv"])
    names = (0, 1, 5, 3, 4, 2, 0, 1)
    vectors = jnp.concatenate([*parts, *(sums[at : at + 1] for at in names[2:])], axis=0)
    if by_kernel:
        square = square_gradients(grads1, grads2, saved1, saved2, vectors, wide, cols)
        square, upper, lower = scatter_by_kernel(square, upper, lower)
        table = square[across : across + LINES, :across]
        square = square[:across]
        lines = [table[at] for at in range(8)]
        lines.insert(5, table[8 : 8 + wide.size // cols // across].reshape(-1))
    else:
        square = jnp.stack(
            [
                product_t(grads1["gq"], grads2["gq"], saved1["x"], saved2["x"]),
                product_t(grads1["gk"], grads2["gk"], saved1["x"], saved2["x"]),
                product_t(grads1["gv"], grads2["gv"], saved1["x"], saved2["x"]),
                product_t(grads1["gb"], grads2["gb"], saved1["mixed"], saved2["mixed"]),
            ]
        )
        table = jnp.concatenate(
            [vectors.reshape(8, cols, across).transpose(1, 0, 2).reshape(cols, -1), wide.reshape(cols, -1)],
            axis=1,
        )
        square, upper, lower, line = scatter(square, upper, lower, table)
        lines = [line[at * across : at * across + across] for at in range(8)]
        lines.insert(5, line[8 * across :])
    own = square.reshape(across, 4, depth)
    result = [own[:, at].T for at in range(4)] + [upper, lower.T]
    return (layer_output, text_grad, memory_grad, *result, *lines)


def solution(mesh):
    batch, matrix, vector = P(("row", "col")), P("row", "col"), P("col")
    return jax.shard_map(
        solution_body,
        mesh=mesh,
        in_specs=(batch,) * 5 + (matrix,) * 6 + (vector,) * 9,
        out_specs=(batch,) * 3 + (matrix,) * 6 + (vector,) * 9,
        check_vma=False,
    )
```

```python
import functools

import jax
import jax.numpy as jnp
from jax import lax
from jax.experimental import pallas as pl
from jax.experimental.pallas import tpu as pltpu
from jax.sharding import PartitionSpec as P

HEADS = 12
HEAD_DIM = 64
MEMORY = 10
TEXT = 502
PICTURE = 256
SEG_ROWS = 522
ROWS = 528
KEYS = 640
QUAD = 256
UNITS = 512
F32 = jnp.float32
BF16 = jnp.bfloat16

EPSILON = 1e-06
MASKED = -1e30
LOG2E = 1.4426950408889634

ERFC_SLOPE = 0.4 * 0.7071067811865476
ERFC_POLY = (0.22562816739082336, 0.2265406847000122, 0.20122945308685303, 0.19582846760749817, 0.07433333992958069, 0.09543049335479736, 0.07776277512311935, -0.1374378800392151, 0.040684547275304794)


def nn(left, right):
    return lax.dot_general(left, right, (((1,), (0,)), ((), ())), preferred_element_type=F32)


def nt(left, right):
    return lax.dot_general(left, right, (((1,), (1,)), ((), ())), preferred_element_type=F32)


def norm_forward(inputs, gain, shift):
    center = jnp.mean(inputs, axis=-1, keepdims=True)
    centred = inputs - center
    spread = jnp.mean(centred * centred, axis=-1, keepdims=True)
    inverse = lax.rsqrt(spread + EPSILON)
    normed = centred * inverse
    return normed * gain + shift, normed, inverse


def norm_backward(grad, normed, inverse, gain):
    scaled = grad * gain
    first = jnp.mean(scaled, axis=-1, keepdims=True)
    second = jnp.mean(scaled * normed, axis=-1, keepdims=True)
    return (scaled - first - normed * second) * inverse


def column_sum(values):
    return jnp.sum(values, axis=0, keepdims=True)


def gelu_pair(upward):
    size = jnp.abs(upward)
    t = 1.0 / (1.0 + ERFC_SLOPE * size)
    poly = jnp.full_like(t, ERFC_POLY[-1])
    for coefficient in ERFC_POLY[-2::-1]:
        poly = poly * t + coefficient
    bell = jnp.exp2(upward * upward * (-0.5 * LOG2E))
    tail = 0.5 * bell * t * poly
    phi = jnp.where(upward < 0.0, tail, 1.0 - tail)
    return upward * phi, phi + upward * (bell * 0.3989422804014327)


def attention_forward_kernel(
    segment, tails, starts, words, edge, wq, wk, wv, wo, vq, vv, vo, gain, shift,
    q_out, k_out, v_out, e_out, total_out, mixed_out, hidden_out, normed_out, inverse_out,
    narrow, narrow_hidden, x, bias, k_pad, v_pad, branch,
):
    step = pl.program_id(0)

    @pl.when(step == 0)
    def _():
        x[...] = words[0]
        x[:MEMORY, :] = edge[:MEMORY, :].astype(F32)
        x[MEMORY + TEXT : SEG_ROWS, :] = edge[:MEMORY, :].astype(F32)
        narrow[...] = x[...].astype(BF16)
        branch[...] = jnp.zeros_like(branch)
        total_out[...] = jnp.ones_like(total_out)
        k_pad[...] = jnp.zeros_like(k_pad)
        v_pad[...] = jnp.zeros_like(v_pad)
        length = TEXT if segment == 0 else tails[0]
        start = starts[0, segment]
        row = lax.broadcasted_iota(jnp.int32, (ROWS, KEYS), 0)
        col = lax.broadcasted_iota(jnp.int32, (ROWS, KEYS), 1)
        low, high = start + MEMORY, start + MEMORY + PICTURE
        text = (col >= MEMORY) & (col < MEMORY + TEXT)
        usable = jnp.logical_not(text & (col >= MEMORY + length)) & (col < SEG_ROWS)
        inside = (row >= low) & (row < high) & (col >= low) & (col < high)
        allowed = usable & ((col <= row) | inside)
        bias[...] = jnp.where(allowed, 0.0, MASKED)

    xb = narrow[...]
    q = ((nt(xb, wq[...]) + vq[...]).astype(BF16).astype(F32) * HEAD_DIM**-0.5).astype(BF16)
    q_out[...] = q
    k_pad[:ROWS, :] = nt(xb, wk[...]).astype(BF16)
    v_pad[:ROWS, :] = (nt(xb, wv[...]) + vv[...]).astype(BF16)
    k_out[...] = k_pad[:ROWS, :]
    v_out[...] = v_pad[:ROWS, :]
    lane = lax.broadcasted_iota(jnp.int32, (ROWS, 128), 1)
    totals = total_out[...]
    for pair in range(2):
        at = slice(128 * pair, 128 * pair + 128)
        halves = []
        for half in range(2):
            mine = (lane < HEAD_DIM) if half == 0 else (lane >= HEAD_DIM)
            qm = jnp.where(mine, q_out[:, at], jnp.zeros((), BF16))
            scores = nt(qm, k_pad[:, at]) + bias[...]
            peak = jnp.max(scores, axis=-1, keepdims=True)
            expos = jnp.exp2((scores - peak) * LOG2E)
            total = jnp.sum(expos, axis=-1, keepdims=True)
            narrow_e = expos.astype(BF16)
            e_out[2 * pair + half] = narrow_e
            totals = jnp.where(lane == step * 4 + 2 * pair + half, total, totals)
            halves.append(nn(narrow_e, v_pad[:, at]) / total)
        mixed_out[:, at] = jnp.where(lane < HEAD_DIM, halves[0], halves[1]).astype(BF16)
    total_out[...] = totals
    branch[...] += nt(mixed_out[...], wo[...])

    @pl.when(step == pl.num_programs(0) - 1)
    def _():
        hidden, normed, inverse = norm_forward(
            x[...] + (branch[...] + vo[...]), gain[...], shift[...]
        )
        hidden_out[...] = hidden
        narrow_hidden[...] = hidden.astype(BF16)
        normed_out[...] = normed
        inverse_out[...] = jnp.broadcast_to(inverse, inverse_out.shape)


def whole(shape):
    return pl.BlockSpec(shape, lambda i: (0,) * len(shape))


def params(limit=58):
    return pltpu.CompilerParams(
        dimension_semantics=("arbitrary",), vmem_limit_bytes=limit * 1024 * 1024
    )


def attention_forward(segment, tails, starts, words, edge, weights):
    width = words.shape[2]
    steps = width // QUAD
    row_block = pl.BlockSpec((QUAD, width), lambda i: (i, 0))
    col_block = pl.BlockSpec((width, QUAD), lambda i: (0, i))
    bias_block = pl.BlockSpec((1, QUAD), lambda i: (0, i))
    rows_block = pl.BlockSpec((ROWS, QUAD), lambda i: (0, i))
    vector = whole((1, width))
    full = whole((ROWS, width))
    stats = whole((ROWS, 128))
    shape = jax.ShapeDtypeStruct
    return pl.pallas_call(
        functools.partial(attention_forward_kernel, segment),
        grid=(steps,),
        in_specs=[
            pl.BlockSpec(memory_space=pltpu.SMEM), pl.BlockSpec(memory_space=pltpu.SMEM),
            pl.BlockSpec((1, ROWS, width), lambda i: (segment, 0, 0)), whole(edge.shape), row_block, row_block, row_block, col_block,
            bias_block, bias_block, vector, vector, vector,
        ],
        out_specs=[
            rows_block, rows_block, rows_block,
            pl.BlockSpec((4, ROWS, KEYS), lambda i: (i, 0, 0)),
            stats, rows_block, full, full, stats, full, full,
        ],
        out_shape=[
            shape((ROWS, width), BF16), shape((ROWS, width), BF16), shape((ROWS, width), BF16),
            shape((HEADS, ROWS, KEYS), BF16),
            shape((ROWS, 128), F32), shape((ROWS, width), BF16),
            shape((ROWS, width), F32), shape((ROWS, width), F32), shape((ROWS, 128), F32),
            shape((ROWS, width), BF16), shape((ROWS, width), BF16),
        ],
        scratch_shapes=[
            pltpu.VMEM((ROWS, width), F32),
            pltpu.VMEM((ROWS, KEYS), F32),
            pltpu.VMEM((KEYS, QUAD), BF16),
            pltpu.VMEM((KEYS, QUAD), BF16),
            pltpu.VMEM((ROWS, width), F32),
        ],
        compiler_params=params(),
        name="attention_forward",
    )(
        tails, starts, words, edge, weights["q"], weights["k"], weights["v"], weights["o"],
        weights["vq"], weights["vv"], weights["vo"], weights["ag"], weights["as"],
    )


def feed_forward_kernel(
    hidden, narrow, wu, wd, vu, vd, gain, shift, act_out, slope_out, y_out, edge_out, normed_out, inverse_out,
    total,
):
    step = pl.program_id(0)

    @pl.when(step == 0)
    def _():
        total[...] = jnp.zeros_like(total)

    upward = nn(narrow[...], wu[...]) + vu[...]
    act, slope = gelu_pair(upward)
    act_out[...] = act.astype(BF16)
    slope_out[...] = slope.astype(BF16)
    total[...] += nt(act_out[...], wd[...])

    @pl.when(step == pl.num_programs(0) - 1)
    def _():
        y, normed, inverse = norm_forward(
            hidden[...] + (total[...] + vd[...]), gain[...], shift[...]
        )
        y_out[...] = y.astype(BF16)
        edge_out[...] = y[MEMORY + TEXT :, :]
        normed_out[...] = normed
        inverse_out[...] = jnp.broadcast_to(inverse, inverse_out.shape)


def feed_forward(hidden, narrow, weights):
    width = hidden.shape[1]
    units = weights["u"].shape[1]
    vector = whole((1, width))
    full = whole((ROWS, width))
    block = pl.BlockSpec((ROWS, UNITS), lambda i: (0, i))
    shape = jax.ShapeDtypeStruct
    return pl.pallas_call(
        feed_forward_kernel,
        grid=(units // UNITS,),
        in_specs=[
            full, full,
            pl.BlockSpec((width, UNITS), lambda i: (0, i)),
            pl.BlockSpec((width, UNITS), lambda i: (0, i)),
            pl.BlockSpec((1, UNITS), lambda i: (0, i)),
            vector, vector, vector,
        ],
        out_specs=[block, block, full, whole((ROWS - MEMORY - TEXT, width)), full, whole((ROWS, 128))],
        out_shape=[
            shape((ROWS, units), BF16), shape((ROWS, units), BF16), shape((ROWS, width), BF16),
            shape((ROWS - MEMORY - TEXT, width), F32), shape((ROWS, width), F32), shape((ROWS, 128), F32),
        ],
        scratch_shapes=[pltpu.VMEM((ROWS, width), F32)],
        compiler_params=params(),
        name="feed_forward",
    )(
        hidden, narrow, weights["u"], weights["d"], weights["vu"], weights["vd"],
        weights["og"], weights["os"],
    )


def feed_backward_kernel(
    segment, dy, top, bottom, normed2, inverse2, normed1, inverse1, slope, wd, wu, wo, gain2, gain1,
    gd_out, gu_out, gb_out, dfirst_out, gm_out, vu_out, sums_out,
    dsecond, dhidden,
):
    step = pl.program_id(0)

    @pl.when(step == 0)
    def _():
        dsecond[...] = dy[0]
        if segment == 0:
            dsecond[MEMORY + TEXT : SEG_ROWS, :] += top[:MEMORY, :] + bottom[:MEMORY, :]
        grad, normed = dsecond[...], normed2[...]
        sums_out[0:1, :] = column_sum(grad * normed)
        sums_out[1:2, :] = column_sum(grad)
        second = norm_backward(grad, normed, inverse2[:, 0:1], gain2[...])
        dsecond[...] = second
        narrow = second.astype(BF16)
        gd_out[...] = narrow
        sums_out[2:3, :] = column_sum(narrow.astype(F32))
        dhidden[...] = jnp.zeros_like(dhidden)

    up = (nn(gd_out[...], wd[...]) * slope[...].astype(F32)).astype(BF16)
    gu_out[...] = up
    vu_out[...] = column_sum(up.astype(F32))
    dhidden[...] += nt(up, wu[...])

    @pl.when(step == pl.num_programs(0) - 1)
    def _():
        grad, normed = dhidden[...] + dsecond[...], normed1[...]
        sums_out[3:4, :] = column_sum(grad * normed)
        sums_out[4:5, :] = column_sum(grad)
        first = norm_backward(grad, normed, inverse1[:, 0:1], gain1[...])
        dfirst_out[...] = first
        narrow = first.astype(BF16)
        gb_out[...] = narrow
        sums_out[5:6, :] = column_sum(narrow.astype(F32))
        sums_out[6:8, :] = jnp.zeros((2, narrow.shape[1]), F32)
        gm_out[...] = nn(narrow, wo[...]).astype(BF16)


def feed_backward(segment, dy, later, saved, weights):
    width = dy.shape[2]
    edges = ROWS - MEMORY - TEXT
    units = weights["u"].shape[1]
    vector = whole((1, width))
    full = whole((ROWS, width))
    stats = whole((ROWS, 128))
    block = pl.BlockSpec((ROWS, UNITS), lambda i: (0, i))
    shape = jax.ShapeDtypeStruct
    return pl.pallas_call(
        functools.partial(feed_backward_kernel, segment),
        grid=(units // UNITS,),
        in_specs=[
            pl.BlockSpec((1, ROWS, width), lambda i: (segment, 0, 0)),
            pl.BlockSpec((edges, width), lambda i: (0, 0)),
            pl.BlockSpec((edges, width), lambda i: ((MEMORY + TEXT) // edges, 0)),
            full, stats, full, stats, block,
            pl.BlockSpec((width, UNITS), lambda i: (0, i)),
            pl.BlockSpec((width, UNITS), lambda i: (0, i)),
            whole((width, width)), vector, vector,
        ],
        out_specs=[
            full, block, full, full, full,
            pl.BlockSpec((1, UNITS), lambda i: (0, i)), whole((8, width)),
        ],
        out_shape=[
            shape((ROWS, width), BF16), shape((ROWS, units), BF16), shape((ROWS, width), BF16),
            shape((ROWS, width), F32), shape((ROWS, width), BF16),
            shape((1, units), F32), shape((8, width), F32),
        ],
        scratch_shapes=[pltpu.VMEM((ROWS, width), F32), pltpu.VMEM((ROWS, width), F32)],
        compiler_params=params(),
        name="feed_backward",
    )(
        dy, later, later, saved["normed2"], saved["inverse2"], saved["normed1"], saved["inverse1"],
        saved["slope"], weights["d"], weights["u"], weights["o"], weights["og"], weights["ag"],
    )


def attention_backward_kernel(
    q, k, v, e, total, mixed, gm, dfirst, wq, wk, wv,
    gq_out, gk_out, gv_out, dx_out, vq_out, vv_out,
    k_pad, v_pad,
):
    step = pl.program_id(0)

    @pl.when(step == 0)
    def _():
        dx_out[...] = dfirst[...]
        k_pad[...] = jnp.zeros_like(k_pad)
        v_pad[...] = jnp.zeros_like(v_pad)

    k_pad[:ROWS, :] = k[...]
    v_pad[:ROWS, :] = v[...]
    lane = lax.broadcasted_iota(jnp.int32, (ROWS, 128), 1)
    for pair in range(2):
        at = slice(128 * pair, 128 * pair + 128)
        grad = gm[:, at].astype(F32)
        product = grad * mixed[:, at].astype(F32)
        totals = total[...]
        rates, inners = [], []
        for half in range(2):
            mine = (lane < HEAD_DIM) if half == 0 else (lane >= HEAD_DIM)
            head = step * 4 + 2 * pair + half
            rate = 1.0 / jnp.sum(jnp.where(lane == head, totals, 0.0), axis=-1, keepdims=True)
            rates.append(rate)
            inners.append(jnp.sum(jnp.where(mine, product, 0.0), axis=-1, keepdims=True) * rate)
        scaled = (grad * jnp.where(lane < HEAD_DIM, rates[0], rates[1])).astype(BF16)
        scaled_t = scaled.T
        query_t = q[:, at].T
        gq, gk, gv = [], [], []
        for half in range(2):
            mine = (lane < HEAD_DIM) if half == 0 else (lane >= HEAD_DIM)
            rows = slice(HEAD_DIM * half, HEAD_DIM * half + HEAD_DIM)
            gmm = jnp.where(mine, scaled, jnp.zeros((), BF16))
            dp = nt(gmm, v_pad[:, at])
            narrow_e = e[2 * pair + half]
            ds = (narrow_e.astype(F32) * (dp - inners[half])).astype(BF16)
            gq.append(nn(ds, k_pad[:, at]))
            gk.append(nn(query_t[rows, :], ds))
            gv.append(nn(scaled_t[rows, :], narrow_e))
        gq_pair = jnp.where(lane < HEAD_DIM, gq[0], gq[1]) * HEAD_DIM**-0.5
        gq_out[:, at] = gq_pair.astype(BF16)
        gk_out[:, at] = jnp.concatenate(gk, axis=0).T[:ROWS].astype(BF16)
        gv_out[:, at] = jnp.concatenate(gv, axis=0).T[:ROWS].astype(BF16)
    vq_out[...] = column_sum(gq_out[...].astype(F32))
    vv_out[...] = column_sum(gv_out[...].astype(F32))
    dx_out[...] += (
        nn(gq_out[...], wq[...]) + nn(gk_out[...], wk[...]) + nn(gv_out[...], wv[...])
    )


def attention_backward(saved, gm, dfirst, weights):
    width = dfirst.shape[1]
    row_block = pl.BlockSpec((QUAD, width), lambda i: (i, 0))
    rows_block = pl.BlockSpec((ROWS, QUAD), lambda i: (0, i))
    full = whole((ROWS, width))
    sums = pl.BlockSpec((1, QUAD), lambda i: (0, i))
    shape = jax.ShapeDtypeStruct
    return pl.pallas_call(
        attention_backward_kernel,
        grid=(width // QUAD,),
        in_specs=[
            rows_block, rows_block, rows_block,
            pl.BlockSpec((4, ROWS, KEYS), lambda i: (i, 0, 0)),
            whole((ROWS, 128)), rows_block, rows_block, full, row_block, row_block, row_block,
        ],
        out_specs=[rows_block, rows_block, rows_block, full, sums, sums],
        out_shape=[
            shape((ROWS, width), BF16), shape((ROWS, width), BF16), shape((ROWS, width), BF16),
            shape((ROWS, width), F32), shape((1, width), F32), shape((1, width), F32),
        ],
        scratch_shapes=[pltpu.VMEM((KEYS, QUAD), BF16), pltpu.VMEM((KEYS, QUAD), BF16)],
        compiler_params=params(),
        name="attention_backward",
    )(
        saved["q"], saved["k"], saved["v"], saved["e"], saved["total"], saved["mixed"],
        gm, dfirst, weights["q"], weights["k"], weights["v"],
    )


ROWS_MESH = 4
LINES = 16
MESH_IDS = pl.DeviceIdType.MESH
Z_UP, Z_DOWN, ACROSS, ALONG, HALF_ACROSS, HALF_ALONG = range(6)
SHARE = 6


class Place:
    def __init__(self, cols):
        self.row, self.col = lax.axis_index("row"), lax.axis_index("col")
        self.length = cols // 2
        self.core = lax.rem(self.col, 2)
        self.line = lax.div(self.col, 2)
        self.across_row = self.row + 1 - 2 * lax.rem(self.row, 2)
        self.along_row = self.row + 2 - 4 * lax.div(self.row, 2)
        self.corner_row = 3 - self.row
        self.across = (self.across_row, self.col)
        self.along = (self.along_row, self.col)
        self.up = (self.row, self.col + 2)
        self.down = (self.row, self.col - 2)
        self.other_core = 1 - self.core
        self.partner = (self.row, self.col + 1 - 2 * self.core)

    def greet(self):
        barrier = pltpu.get_barrier_semaphore()

        def signal(device):
            pl.semaphore_signal(barrier, inc=1, device_id=device, device_id_type=MESH_IDS)

        signal(self.across)
        signal(self.along)
        signal(self.partner)
        pl.when(self.line > 0)(lambda: signal(self.down))
        pl.when(self.line < self.length - 1)(lambda: signal(self.up))
        has_down = lax.div(self.line + self.length - 1, self.length)
        has_up = lax.div(2 * self.length - 2 - self.line, self.length)
        pl.semaphore_wait(barrier, 3 + has_down + has_up)

    def at_distance(self, distance, visit):
        if distance == 0:
            visit(self.line, None)
        else:
            below, above = self.line - distance, self.line + distance
            pl.when(below >= 0)(lambda: visit(below, True))
            pl.when(above < self.length)(lambda: visit(above, False))


def splits(count):
    first = count // 32 * 16
    return ((0, first), (first, count - first))


def gather_kernel(
    square, upper, lower, wq, wk, wv, wo, *rest
):
    vectors, (whole_upper, whole_lower, gathered, send, recv, own) = rest[:9], rest[9:]
    rows, cols = ROWS_MESH, wq.shape[0] // lower.shape[0]
    place = Place(cols)
    depth, across = upper.shape[0], lower.shape[0]
    sources = (square, upper, lower)

    def target(which, row, col, part=None):
        if which == 0:
            view, count = gathered.at[row * cols + col], square.shape[0]
            begin, size = part if part else (0, count)
            return view.at[pl.ds(begin, size)]
        count, wide = sources[which].shape
        array, high, side = (whole_upper, row, col) if which == 1 else (whole_lower, col, row)
        begin, size = part if part else (0, count)
        return array.at[
            pl.ds(pl.multiple_of(high * count + begin, 16), size),
            pl.ds(pl.multiple_of(side * wide, 128), wide),
        ]

    def copy(which, kind, row, line, device, part=None, mine=None, arrival=None):
        col = 2 * line + (place.core if mine is None else mine)
        there = target(which, row, col, part)
        here = there if arrival is None else sources[which]
        return pltpu.make_async_remote_copy(
            src_ref=here, dst_ref=there,
            send_sem=send.at[which, kind, line], recv_sem=recv.at[which, kind, line],
            device_id=device, device_id_type=MESH_IDS,
        )

    place.greet()
    keeps = []
    for which in range(3):
        keep = pltpu.make_async_copy(
            sources[which], target(which, place.row, place.col), own.at[which]
        )
        keep.start()
        keeps.append(keep)

    def both(which):
        return splits(sources[which].shape[0])

    def by_line(which, distance):
        def visit(line, upward):
            first = True if upward is None else None
            args = (place.row, line)
            if upward is not None:
                kind = Z_UP if upward else Z_DOWN
                copy(which, kind, *args, place.down).wait_recv()
            if upward is None or upward:
                pl.when(place.line < place.length - 1)(
                    lambda: copy(which, Z_UP, *args, place.up, arrival=first).start()
                )
            if upward is None or not upward:
                pl.when(place.line > 0)(
                    lambda: copy(which, Z_DOWN, *args, place.down, arrival=first).start()
                )
            copy(which, ACROSS, *args, place.across, arrival=first).start()
            copy(which, ALONG, *args, place.along, arrival=first).start()
            copy(which, SHARE, *args, place.partner, arrival=first).start()

        place.at_distance(distance, visit)

    def by_side(which, distance):
        halves = both(which)

        def visit(line, upward):
            copy(which, ACROSS, place.across_row, line, place.across).wait_recv()
            copy(which, HALF_ALONG, place.across_row, line, place.along, halves[1]).start()
            copy(which, SHARE + 1, place.across_row, line, place.partner).start()
            copy(which, ALONG, place.along_row, line, place.along).wait_recv()
            copy(which, HALF_ACROSS, place.along_row, line, place.across, halves[0]).start()
            copy(which, SHARE + 2, place.along_row, line, place.partner).start()

        place.at_distance(distance, visit)

    def by_corner(which, distance):
        halves = both(which)

        def visit(line, upward):
            copy(which, HALF_ACROSS, place.corner_row, line, place.across, halves[0]).wait_recv()
            copy(which, SHARE + 3, place.corner_row, line, place.partner, halves[0]).start()
            copy(which, HALF_ALONG, place.corner_row, line, place.along, halves[1]).wait_recv()
            copy(which, SHARE + 4, place.corner_row, line, place.partner, halves[1]).start()

        place.at_distance(distance, visit)

    def from_partner(which):
        halves = both(which)
        for distance in range(place.length):

            def visit(line, upward):
                mine = place.other_core
                for kind, row, part in (
                    (0, place.row, None), (1, place.across_row, None), (2, place.along_row, None),
                    (3, place.corner_row, halves[0]), (4, place.corner_row, halves[1]),
                ):
                    copy(which, SHARE + kind, row, line, place.partner, part, mine=mine).wait_recv()

            place.at_distance(distance, visit)

    def drain(which):
        halves = both(which)
        for distance in range(place.length):

            def visit(line, upward):
                args = (place.row, line)
                first = True if upward is None else None
                if upward is None or upward:
                    pl.when(place.line < place.length - 1)(
                        lambda: copy(which, Z_UP, *args, place.up, arrival=first).wait_send()
                    )
                if upward is None or not upward:
                    pl.when(place.line > 0)(
                        lambda: copy(which, Z_DOWN, *args, place.down, arrival=first).wait_send()
                    )
                copy(which, ACROSS, *args, place.across, arrival=first).wait_send()
                copy(which, ALONG, *args, place.along, arrival=first).wait_send()
                copy(which, SHARE, *args, place.partner, arrival=first).wait_send()
                copy(which, HALF_ALONG, place.across_row, line, place.along, halves[1]).wait_send()
                copy(which, HALF_ACROSS, place.along_row, line, place.across, halves[0]).wait_send()
                copy(which, SHARE + 1, place.across_row, line, place.partner).wait_send()
                copy(which, SHARE + 2, place.along_row, line, place.partner).wait_send()
                copy(which, SHARE + 3, place.corner_row, line, place.partner, halves[0]).wait_send()
                copy(which, SHARE + 4, place.corner_row, line, place.partner, halves[1]).wait_send()

            place.at_distance(distance, visit)

    length = place.length
    finish = length + 2
    for step in range(finish + 4):
        for which in range(3):
            distance = step - 2 * which
            if 0 <= distance < length:
                by_line(which, distance)
            if 1 <= distance < length + 1:
                by_side(which, distance - 1)
            if 2 <= distance < length + 2:
                by_corner(which, distance - 2)
        if step == finish:
            from_partner(0)
            keeps[0].wait()
            outs = (wq, wk, wv, wo)
            for col in range(cols):
                for at, out in enumerate(outs):
                    out[across * col : across * col + across, :] = jnp.concatenate(
                        [
                            gathered[row * cols + col, :across, depth * at : depth * at + depth]
                            for row in range(rows)
                        ],
                        axis=1,
                    )
            lines = [gathered[col, across:, :across].astype(F32) for col in range(cols)]
            table = jnp.concatenate(lines, axis=1)
            for at in range(8):
                vectors[at][...] = table[at : at + 1]
            vectors[8][...] = jnp.concatenate(
                [line[8 + at : 9 + at] for line in lines for at in range(upper.shape[1] // across)], axis=1
            )
    for which in range(1, 3):
        from_partner(which)
        keeps[which].wait()
    for which in range(3):
        drain(which)


def pack_kernel(wq, wk, wv, wo, wd, vectors, square, lower):
    across, depth = wq.shape[1], wq.shape[0]
    square[:across, :] = jnp.concatenate(
        [item[...].astype(F32).T for item in (wq, wk, wv, wo)], axis=1
    ).astype(BF16)
    square[across:, :] = jnp.zeros((LINES, square.shape[1]), BF16)
    square[across : across + LINES, :128] = vectors[...]
    lower[...] = wd[...].astype(F32).T.astype(BF16)


def fetch_by_kernel(arguments):
    matrices, vectors = arguments[:6], arguments[6:]
    rows, cols = lax.axis_size("row"), lax.axis_size("col")
    depth, across = matrices[0].shape
    width = depth * rows
    units = matrices[4].shape[1] * cols
    table = jnp.stack([*vectors[:5], *vectors[6:]])
    table = jnp.concatenate([table, vectors[5].reshape(-1, across)], axis=0)
    table = jnp.pad(table, ((0, LINES - table.shape[0]), (0, 128 - across)))
    shape = jax.ShapeDtypeStruct
    square, lower = pl.pallas_call(
        pack_kernel,
        out_shape=[shape((across + LINES, 4 * depth), BF16), shape((across, matrices[5].shape[0]), BF16)],
        in_specs=[pl.BlockSpec(memory_space=pltpu.VMEM)] * 6,
        out_specs=[pl.BlockSpec(memory_space=pltpu.VMEM)] * 2,
        name="pack",
    )(*matrices[:4], matrices[5], table)
    anywhere, local = pl.BlockSpec(memory_space=pl.ANY), pl.BlockSpec(memory_space=pltpu.VMEM)
    kinds = (3, SHARE + 5, cols // 2)
    vector = shape((1, width), F32)
    names = ("q", "k", "v", "o", "vq", "vv", "vo", "ag", "as", "vd", "og", "os", "vu", "u", "d")
    whole_arrays = pl.pallas_call(
        gather_kernel,
        out_shape=[shape((width, width), BF16)] * 4 + [vector] * 8 + [shape((1, units), F32)]
        + [shape((width, units), BF16), shape((width, units), BF16)],
        in_specs=[anywhere] * 3,
        out_specs=[local] * 13 + [anywhere] * 2,
        scratch_shapes=[
            pltpu.VMEM((rows * cols, across + LINES, 4 * depth), BF16),
            pltpu.SemaphoreType.DMA(kinds), pltpu.SemaphoreType.DMA(kinds), pltpu.SemaphoreType.DMA((3,)),
        ],
        compiler_params=pltpu.CompilerParams(
            collective_id=0, has_side_effects=True, vmem_limit_bytes=58 * 1024 * 1024
        ),
        name="gather",
    )(square, matrices[4], lower)
    return dict(zip(names, whole_arrays))


def scatter_kernel(square, upper, lower, square_out, upper_out, lower_out, *scratch):
    mine, theirs, corner, side, lined = (scratch[3 * at : 3 * at + 3] for at in range(5))
    send, recv, own = scratch[15:]
    rows, cols = ROWS_MESH, square.shape[0] // ROWS_MESH
    place = Place(cols)
    outs = (square_out, upper_out, lower_out)
    length = place.length

    def source(which, row, col):
        count, wide = outs[which].shape
        if which == 0:
            return square.at[row * cols + col]
        array, high, level = (upper, row, col) if which == 1 else (lower, col, row)
        return array.at[
            pl.ds(pl.multiple_of(high * count, 16), count),
            pl.ds(pl.multiple_of(level * wide, 128), wide),
        ]

    def load(which, row, line):
        return pltpu.make_async_copy(
            source(which, row, 2 * line + place.core),
            mine[which].at[row * length + line], own.at[which, row * length + line],
        )

    def share(which, row, line, core):
        at = row * length + line
        return pltpu.make_async_remote_copy(
            src_ref=source(which, row, 2 * line + core), dst_ref=theirs[which].at[at],
            send_sem=send.at[which, SHARE + row, line], recv_sem=recv.at[which, SHARE + row, line],
            device_id=place.partner, device_id_type=MESH_IDS,
        )

    def remote(which, kind, line, here, there, device):
        return pltpu.make_async_remote_copy(
            src_ref=here, dst_ref=there,
            send_sem=send.at[which, kind, line], recv_sem=recv.at[which, kind, line],
            device_id=device, device_id_type=MESH_IDS,
        )

    def corner_copy(which, kind, line):
        begin, size = splits(outs[which].shape[0])[kind - HALF_ACROSS]
        part = pl.ds(begin, size)
        here = mine[which].at[place.corner_row * length + line, part]
        there = corner[which].at[line, part]
        return remote(which, kind, line, here, there, place.across if kind == HALF_ACROSS else place.along)

    def side_copy(which, kind, line):
        row, device = (place.across_row, place.across) if kind == ACROSS else (place.along_row, place.along)
        here = mine[which].at[row * length + line]
        return remote(which, kind, line, here, side[which].at[kind - ACROSS, line], device)

    def line_copy(which, kind, line):
        here = mine[which].at[place.row * length + line]
        return remote(which, kind, line, here, lined[which].at[kind, line], place.up if kind == Z_UP else place.down)

    def add(which, at, arrived, part=None):
        block = mine[which].at[at] if part is None else mine[which].at[at, pl.ds(*part)]
        block[...] = (block[...].astype(F32) + arrived[...].astype(F32)).astype(BF16)

    place.greet()

    def spread(distance, visit):
        place.at_distance(distance, lambda line, upward: visit(line))

    farthest = range(length - 1, -1, -1)
    order = ("corner_row", "across_row", "along_row", "row")
    for which in range(3):
        for distance in farthest:

            def begin(line):
                for name in order:
                    row = getattr(place, name)
                    load(which, row, line).start()
                    share(which, row, line, place.other_core).start()

            spread(distance, begin)

    def merge(which, row, line):
        load(which, row, line).wait()
        share(which, row, line, place.core).wait_recv()
        at = row * length + line
        add(which, at, theirs[which].at[at])

    def cores(which, distance):
        def visit(line):
            merge(which, place.corner_row, line)
            merge(which, place.across_row, line)
            corner_copy(which, HALF_ACROSS, line).start()
            corner_copy(which, HALF_ALONG, line).start()
            merge(which, place.along_row, line)
            merge(which, place.row, line)

        spread(distance, visit)

    def corners(which, distance):
        first, second = splits(outs[which].shape[0])

        def visit(line):
            corner_copy(which, HALF_ACROSS, line).wait_recv()
            add(which, place.along_row * length + line, corner[which].at[line, pl.ds(*first)], first)
            corner_copy(which, HALF_ALONG, line).wait_recv()
            add(which, place.across_row * length + line, corner[which].at[line, pl.ds(*second)], second)
            side_copy(which, ALONG, line).start()
            side_copy(which, ACROSS, line).start()

        spread(distance, visit)

    def sides(which, distance):
        def visit(line):
            at = place.row * length + line
            side_copy(which, ACROSS, line).wait_recv()
            add(which, at, side[which].at[0, line])
            side_copy(which, ALONG, line).wait_recv()
            add(which, at, side[which].at[1, line])

        spread(distance, visit)

    def lines(which, distance):
        def visit(line, downward):
            at = place.row * length + line
            kind = Z_DOWN if downward else Z_UP
            onward = place.line < length - 1 if downward else place.line > 0

            @pl.when(onward)
            def _():
                line_copy(which, kind, line).wait_recv()
                add(which, at, lined[which].at[kind, line])

            line_copy(which, kind, line).start()

        place.at_distance(distance, visit)

    def result(which):
        at = place.row * length + place.line
        for kind, there in ((Z_UP, place.line > 0), (Z_DOWN, place.line < length - 1)):

            @pl.when(there)
            def _():
                line_copy(which, kind, place.line).wait_recv()
                add(which, at, lined[which].at[kind, place.line])

        outs[which][...] = mine[which][at].astype(F32)

    def drain(which):
        for distance in farthest:

            def visit(line, downward):
                for row in range(rows):
                    share(which, row, line, place.other_core).wait_send()
                for kind in (HALF_ACROSS, HALF_ALONG):
                    corner_copy(which, kind, line).wait_send()
                for kind in (ACROSS, ALONG):
                    side_copy(which, kind, line).wait_send()
                if downward is not None:
                    line_copy(which, Z_DOWN if downward else Z_UP, line).wait_send()

            place.at_distance(distance, visit)

    for step in range(length + 3 + 4):
        for which in range(3):
            stage = step - 2 * which
            if 0 <= stage < length:
                cores(which, length - 1 - stage)
            if 1 <= stage < length + 1:
                corners(which, length - stage)
            if 2 <= stage < length + 2:
                sides(which, length + 1 - stage)
            if 3 <= stage < length + 2:
                lines(which, length + 2 - stage)
            if stage == length + 2:
                result(which)
    for which in range(3):
        drain(which)


def scatter_by_kernel(square, upper, lower):
    cols = square.shape[0] // ROWS_MESH
    length = cols // 2
    count, wide = square.shape[1:]
    blocks = (
        (count, wide),
        (upper.shape[0] // ROWS_MESH, upper.shape[1] // cols),
        (lower.shape[0] // cols, lower.shape[1] // ROWS_MESH),
    )
    kinds = (3, SHARE + ROWS_MESH, length)
    anywhere, local = pl.BlockSpec(memory_space=pl.ANY), pl.BlockSpec(memory_space=pltpu.VMEM)
    buffers = [
        pltpu.VMEM((*lead, *block), BF16)
        for lead in ((ROWS_MESH * length,), (ROWS_MESH * length,), (length,), (2, length), (2, length))
        for block in blocks
    ]
    return pl.pallas_call(
        scatter_kernel,
        out_shape=[jax.ShapeDtypeStruct(block, F32) for block in blocks],
        in_specs=[anywhere] * 3,
        out_specs=[local] * 3,
        scratch_shapes=[
            *buffers,
            pltpu.SemaphoreType.DMA(kinds), pltpu.SemaphoreType.DMA(kinds),
            pltpu.SemaphoreType.DMA((3, ROWS_MESH * length)),
        ],
        compiler_params=pltpu.CompilerParams(
            collective_id=1, has_side_effects=True, vmem_limit_bytes=50 * 1024 * 1024
        ),
        name="scatter",
    )(square, upper, lower)


def joined(first, second):
    return jnp.concatenate([first, second], axis=0)


def product_kernel(left1, left2, right1, right2, out, turned):
    @pl.when(pl.program_id(0) == 0)
    def _():
        turned[...] = joined(left1[...], left2[...]).T

    out[...] = nn(turned[...], joined(right1[...], right2[...])).astype(BF16)


def product_t(left1, left2, right1, right2):
    width, units = left1.shape[1], right1.shape[1]
    block = pl.BlockSpec((ROWS, UNITS), lambda i: (0, i))
    return pl.pallas_call(
        product_kernel,
        grid=(units // UNITS,),
        in_specs=[whole((ROWS, width))] * 2 + [block] * 2,
        out_specs=pl.BlockSpec((width, UNITS), lambda i: (0, i)),
        out_shape=jax.ShapeDtypeStruct((width, units), BF16),
        scratch_shapes=[pltpu.VMEM((width, 2 * ROWS), BF16)],
        compiler_params=params(),
        name="weight_gradient",
    )(left1, left2, right1, right2)


SUM_ROWS = (5, 3, 4, 2, 0, 1)


def square_kernel(
    gq1, gq2, gk1, gk2, gv1, gv2, gb1, gb2, x1, x2, mixed1, mixed2,
    vq1, vq2, vv1, vv2, sums1, sums2, vu1, vu2, out, total
):
    rows = ROWS_MESH
    cols = out.shape[0] // rows
    width = out.shape[2]
    across, depth = width // cols, width // rows
    sums = sums1[...] + sums2[...]
    wide = vu1[...] + vu2[...]
    vectors = jnp.concatenate(
        [vq1[...] + vq2[...], vv1[...] + vv2[...]] + [sums[at : at + 1] for at in SUM_ROWS], axis=0
    )
    lefts = ((gq1, gq2), (gk1, gk2), (gv1, gv2), (gb1, gb2))
    for at, (left1, left2) in enumerate(lefts):
        right1, right2 = (x1, x2) if at < 3 else (mixed1, mixed2)
        left, right = joined(left1[...], left2[...]), joined(right1[...], right2[...])
        total[at] = nn(left.T, right).astype(BF16)
    share = wide.shape[1] // cols // across
    for col in range(cols):
        begin = across * col
        narrow = jnp.concatenate(
            [vectors[:, begin : begin + across]]
            + [wide[:, across * (col * share + at) : across * (col * share + at + 1)] for at in range(share)]
            + [jnp.zeros((LINES - 8 - share, across), F32)],
            axis=0,
        )
        narrow = jnp.pad(narrow, ((0, 0), (0, out.shape[2] - across))).astype(BF16)
        for row in range(rows):
            block = row * cols + col
            out[block, :across, :] = jnp.concatenate(
                [total[at, begin : begin + across, depth * row : depth * row + depth] for at in range(4)],
                axis=1,
            )
            out[block, across:, :] = narrow


def square_gradients(grads1, grads2, saved1, saved2, cols):
    width = grads1["gq"].shape[1]
    operands = []
    for name in ("gq", "gk", "gv", "gb"):
        operands += [grads1[name], grads2[name]]
    operands += [saved1["x"], saved2["x"], saved1["mixed"], saved2["mixed"]]
    for name in ("vq", "vv", "sums", "vu"):
        operands += [grads1[name], grads2[name]]
    local = pl.BlockSpec(memory_space=pltpu.VMEM)
    return pl.pallas_call(
        square_kernel,
        in_specs=[local] * len(operands),
        out_specs=local,
        out_shape=jax.ShapeDtypeStruct((ROWS_MESH * cols, width // cols + LINES, width), BF16),
        scratch_shapes=[pltpu.VMEM((4, width, width), BF16)],
        compiler_params=pltpu.CompilerParams(vmem_limit_bytes=58 * 1024 * 1024),
        name="square_gradients",
    )(*operands)


def gather_all(part):
    return lax.all_gather(part, ("row", "col"), axis=0, tiled=False)


def fetch(arguments):
    matrices, vectors = arguments[:6], arguments[6:]
    rows, cols = lax.axis_size("row"), lax.axis_size("col")
    depth, across = matrices[0].shape
    width = depth * rows
    names = ("q", "k", "v", "o")
    square = jnp.concatenate([item.T for item in matrices[:4]], axis=1)
    upper = matrices[4].T.reshape(4, across, depth).transpose(1, 0, 2).reshape(across, 4 * depth)
    lower = matrices[5].T
    line = jnp.concatenate(vectors)
    extra = -(-line.shape[0] // (4 * depth))
    extra += -(across + extra) % 16
    line = jnp.pad(line, (0, extra * 4 * depth - line.shape[0])).reshape(extra, 4 * depth)
    first = gather_all(jnp.concatenate([square, line], axis=0))
    second = gather_all(upper)
    third = gather_all(lower)
    whole_square = (
        first[:, :across].reshape(rows, cols, across, 4, depth)
        .transpose(3, 1, 2, 0, 4).reshape(4, width, width)
    )
    weights = {name: whole_square[at] for at, name in enumerate(names)}
    weights["u"] = (
        second.reshape(rows, cols, across, 4, depth)
        .transpose(0, 4, 1, 3, 2).reshape(width, 4 * width)
    )
    weights["d"] = third.reshape(rows, cols, across, 4 * depth).transpose(1, 2, 0, 3).reshape(width, 4 * width)
    lines = first[:cols, across:].reshape(cols, -1).astype(F32)
    at = 0
    for name, item in zip(("vq", "vv", "vo", "ag", "as", "vu", "vd", "og", "os"), vectors):
        weights[name] = lines[:, at : at + item.shape[0]].reshape(1, -1)
        at += item.shape[0]
    return weights


def scatter_all(terms):
    return lax.psum_scatter(terms, ("row", "col"), scatter_dimension=0, tiled=False)


def scatter(square, upper, lower, lines):
    rows, cols = lax.axis_size("row"), lax.axis_size("col")
    width = square.shape[1]
    depth, across = width // rows, width // cols
    square = square.reshape(4, cols, across, rows, depth).transpose(3, 1, 2, 0, 4)
    square = square.reshape(rows, cols, across, 4 * depth)
    count = lines.shape[1]
    extra = -(-count // (4 * depth))
    extra += -(across + extra) % 16
    lines = jnp.pad(lines, ((0, 0), (0, extra * 4 * depth - count))).astype(BF16)
    lines = jnp.broadcast_to(lines.reshape(1, cols, extra, 4 * depth), (rows, cols, extra, 4 * depth))
    square = jnp.concatenate([square, lines], axis=2)
    square = scatter_all(square.reshape(rows * cols, across + extra, 4 * depth)).astype(F32)
    upper = upper.reshape(rows, depth, cols, 4 * across).transpose(0, 2, 1, 3)
    upper = scatter_all(upper.reshape(rows * cols, depth, 4 * across)).astype(F32)
    lower = lower.reshape(cols, across, rows, 4 * depth).transpose(2, 0, 1, 3)
    lower = scatter_all(lower.reshape(rows * cols, across, 4 * depth)).astype(F32)
    return square[:across], upper, lower, square[across:].reshape(-1)[:count]


def solution_body(
    text, memory, tail_lengths, picture_starts, grad_out, *parameters
):
    rows, cols = lax.axis_size("row"), lax.axis_size("col")
    depth, across = parameters[0].shape
    width = depth * rows
    by_kernel = rows == ROWS_MESH and cols % 2 == 0 and depth % 32 == 0 and across % 32 == 0
    by_kernel = by_kernel and 4 * across % 128 == 0
    weights = fetch_by_kernel(parameters) if by_kernel else fetch(parameters)
    words = jnp.pad(text[0].astype(F32), ((0, 0), (MEMORY, ROWS - MEMORY - TEXT), (0, 0)))

    def forward(segment, edge):
        q, k, v, e, total, mixed, hidden, normed1, inverse1, xb, hb = attention_forward(
            segment, tail_lengths, picture_starts, words, edge, weights
        )
        act, slope, y, edge, normed2, inverse2 = feed_forward(hidden, hb, weights)
        saved = dict(
            x=xb, q=q, k=k, v=v, e=e, total=total, mixed=mixed, hidden=hb,
            normed1=normed1, inverse1=inverse1, act=act, slope=slope, normed2=normed2, inverse2=inverse2,
        )
        return y, edge, saved

    def paired(first, second, begin, count):
        which = lax.broadcasted_iota(jnp.int32, (count, 2, width), 1)
        first, second = (item[begin : begin + count, None, :] for item in (first, second))
        return jnp.where(which == 0, first, second).astype(BF16).transpose(1, 0, 2)[None]

    y1, edge1, saved1 = forward(0, memory[0])
    y2, edge2, saved2 = forward(1, edge1)
    layer_output = paired(y1, y2, 0, SEG_ROWS)

    def backward(segment, later, saved):
        gd, gu, gb, dfirst, gm, vu, sums = feed_backward(segment, cotangent, later, saved, weights)
        gq, gk, gv, dx, vq, vv = attention_backward(saved, gm, dfirst, weights)
        return dx, dict(gd=gd, gu=gu, gb=gb, gq=gq, gk=gk, gv=gv, vu=vu, sums=sums, vq=vq, vv=vv)

    cotangent = jnp.pad(grad_out[0].astype(F32), ((0, 0), (0, ROWS - SEG_ROWS), (0, 0)))
    dx2, grads2 = backward(1, saved2["normed2"], saved2)
    dx1, grads1 = backward(0, dx2, saved1)
    memory_grad = (dx1[:MEMORY] + dx1[MEMORY + TEXT : SEG_ROWS]).astype(BF16)[None]
    text_grad = paired(dx1, dx2, MEMORY, TEXT)

    upper = product_t(saved1["hidden"], saved2["hidden"], grads1["gu"], grads2["gu"])
    lower = product_t(grads1["gd"], grads2["gd"], saved1["act"], saved2["act"])
    if by_kernel:
        square = square_gradients(grads1, grads2, saved1, saved2, cols)
        square, upper, lower = scatter_by_kernel(square, upper, lower)
        table = square[across : across + LINES, :across]
        square = square[:across]
        lines = [table[at] for at in range(8)]
        lines.insert(5, table[8 : 8 + upper.shape[1] // across].reshape(-1))
    else:
        square = jnp.stack(
            [
                product_t(grads1["gq"], grads2["gq"], saved1["x"], saved2["x"]),
                product_t(grads1["gk"], grads2["gk"], saved1["x"], saved2["x"]),
                product_t(grads1["gv"], grads2["gv"], saved1["x"], saved2["x"]),
                product_t(grads1["gb"], grads2["gb"], saved1["mixed"], saved2["mixed"]),
            ]
        )
        sums = grads1["sums"] + grads2["sums"]
        wide = grads1["vu"] + grads2["vu"]
        parts = (grads1["vq"] + grads2["vq"], grads1["vv"] + grads2["vv"])
        vectors = jnp.concatenate([*parts, *(sums[at : at + 1] for at in SUM_ROWS)], axis=0)
        table = jnp.concatenate(
            [vectors.reshape(8, cols, across).transpose(1, 0, 2).reshape(cols, -1), wide.reshape(cols, -1)],
            axis=1,
        )
        square, upper, lower, line = scatter(square, upper, lower, table)
        lines = [line[at * across : at * across + across] for at in range(8)]
        lines.insert(5, line[8 * across :])
    own = square.reshape(across, 4, depth)
    result = [own[:, at].T for at in range(4)] + [upper, lower.T]
    return (layer_output, text_grad, memory_grad, *result, *lines)


def solution(mesh):
    batch, matrix, vector = P(("row", "col")), P("row", "col"), P("col")
    return jax.shard_map(
        solution_body,
        mesh=mesh,
        in_specs=(batch,) * 5 + (matrix,) * 6 + (vector,) * 9,
        out_specs=(batch,) * 3 + (matrix,) * 6 + (vector,) * 9,
        check_vma=False,
    )
```

```python
import functools

import jax
import jax.numpy as jnp
from jax import lax
from jax.experimental import pallas as pl
from jax.experimental.pallas import tpu as pltpu
from jax.sharding import PartitionSpec as P

HEADS = 12
HEAD_DIM = 64
MEMORY = 10
TEXT = 502
PICTURE = 256
SEG_ROWS = 522
ROWS = 528
MAIN = 512
LAST = 128
KEYS = MAIN + LAST
QUAD = 256
UNITS = 512
F32 = jnp.float32
BF16 = jnp.bfloat16

EPSILON = 1e-06
MASKED = -1e30
LOG2E = 1.4426950408889634

ERFC_SLOPE = 0.4 * 0.7071067811865476
ERFC_POLY = (0.22562816739082336, 0.2265406847000122, 0.20122945308685303, 0.19582846760749817, 0.07433333992958069, 0.09543049335479736, 0.07776277512311935, -0.1374378800392151, 0.040684547275304794)


def nn(left, right):
    return lax.dot_general(left, right, (((1,), (0,)), ((), ())), preferred_element_type=F32)


def nt(left, right):
    return lax.dot_general(left, right, (((1,), (1,)), ((), ())), preferred_element_type=F32)


def norm_forward(inputs, gain, shift):
    center = jnp.mean(inputs, axis=-1, keepdims=True)
    centred = inputs - center
    spread = jnp.mean(centred * centred, axis=-1, keepdims=True)
    inverse = lax.rsqrt(spread + EPSILON)
    normed = centred * inverse
    return normed * gain + shift, normed, inverse


def norm_backward(grad, normed, inverse, gain):
    scaled = grad * gain
    first = jnp.mean(scaled, axis=-1, keepdims=True)
    second = jnp.mean(scaled * normed, axis=-1, keepdims=True)
    return (scaled - first - normed * second) * inverse


def column_sum(values):
    return jnp.sum(values, axis=0, keepdims=True)


def gelu_pair(upward):
    size = jnp.abs(upward)
    t = 1.0 / (1.0 + ERFC_SLOPE * size)
    poly = jnp.full_like(t, ERFC_POLY[-1])
    for coefficient in ERFC_POLY[-2::-1]:
        poly = poly * t + coefficient
    bell = jnp.exp2(upward * upward * (-0.5 * LOG2E))
    tail = 0.5 * bell * t * poly
    phi = jnp.where(upward < 0.0, tail, 1.0 - tail)
    return upward * phi, phi + upward * (bell * 0.3989422804014327)


def plus_last(values, last):
    return jnp.concatenate([values[:MAIN], values[MAIN:] + last], axis=0)


def attention_forward_kernel(
    segment, tails, starts, words, edge, wq, wk, wv, wo, vq, vv, vo, gain, shift,
    q_out, k_out, v_out, e_out, last_out, total_out, mixed_out, hidden_out, normed_out, inverse_out,
    narrow, narrow_hidden, x, bias, last_bias, k_pad, v_pad, branch,
):
    step = pl.program_id(0)

    @pl.when(step == 0)
    def _():
        x[...] = words[0]
        x[:MEMORY, :] = edge[:MEMORY, :].astype(F32)
        x[MEMORY + TEXT : SEG_ROWS, :] = edge[:MEMORY, :].astype(F32)
        narrow[...] = x[...].astype(BF16)
        branch[...] = jnp.zeros_like(branch)
        total_out[...] = jnp.ones_like(total_out)
        k_pad[...] = jnp.zeros_like(k_pad)
        v_pad[...] = jnp.zeros_like(v_pad)
        length = TEXT if segment == 0 else tails[0]
        start = starts[0, segment]
        low, high = start + MEMORY, start + MEMORY + PICTURE
        row = lax.broadcasted_iota(jnp.int32, (ROWS, MAIN), 0)
        col = lax.broadcasted_iota(jnp.int32, (ROWS, MAIN), 1)
        usable = (col < MEMORY) | (col < MEMORY + length)
        inside = (row >= low) & (row < high) & (col >= low) & (col < high)
        bias[...] = jnp.where(usable & ((col <= row) | inside), 0.0, MASKED)
        row = lax.broadcasted_iota(jnp.int32, (ROWS - MAIN, LAST), 0)
        col = lax.broadcasted_iota(jnp.int32, (ROWS - MAIN, LAST), 1)
        last_bias[...] = jnp.where((col < SEG_ROWS - MAIN) & (col <= row), 0.0, MASKED)

    xb = narrow[...]
    q = ((nt(xb, wq[...]) + vq[...]).astype(BF16).astype(F32) * HEAD_DIM**-0.5).astype(BF16)
    q_out[...] = q
    k_pad[:ROWS, :] = nt(xb, wk[...]).astype(BF16)
    v_pad[:ROWS, :] = (nt(xb, wv[...]) + vv[...]).astype(BF16)
    k_out[...] = k_pad[:ROWS, :]
    v_out[...] = v_pad[:ROWS, :]
    lane = lax.broadcasted_iota(jnp.int32, (ROWS, 128), 1)
    totals = total_out[...]
    for pair in range(2):
        at = slice(128 * pair, 128 * pair + 128)
        halves = []
        for half in range(2):
            mine = (lane < HEAD_DIM) if half == 0 else (lane >= HEAD_DIM)
            qm = jnp.where(mine, q_out[:, at], jnp.zeros((), BF16))
            scores = nt(qm, k_pad[:MAIN, at]) + bias[...]
            last = nt(qm[MAIN:], k_pad[MAIN:, at]) + last_bias[...]
            peak = jnp.max(scores, axis=-1, keepdims=True)
            last_peak = jnp.maximum(peak[MAIN:], jnp.max(last, axis=-1, keepdims=True))
            peak = jnp.concatenate([peak[:MAIN], last_peak], axis=0)
            expos = jnp.exp2((scores - peak) * LOG2E)
            last = jnp.exp2((last - last_peak) * LOG2E)
            total = plus_last(jnp.sum(expos, axis=-1, keepdims=True), jnp.sum(last, axis=-1, keepdims=True))
            narrow_e, last = expos.astype(BF16), last.astype(BF16)
            e_out[2 * pair + half] = narrow_e
            last_out[2 * pair + half] = last
            weighted = plus_last(nn(narrow_e, v_pad[:MAIN, at]), nn(last, v_pad[MAIN:, at]))
            totals = jnp.where(lane == step * 4 + 2 * pair + half, total, totals)
            halves.append(weighted / total)
        mixed_out[:, at] = jnp.where(lane < HEAD_DIM, halves[0], halves[1]).astype(BF16)
    total_out[...] = totals
    branch[...] += nt(mixed_out[...], wo[...])

    @pl.when(step == pl.num_programs(0) - 1)
    def _():
        hidden, normed, inverse = norm_forward(
            x[...] + (branch[...] + vo[...]), gain[...], shift[...]
        )
        hidden_out[...] = hidden
        narrow_hidden[...] = hidden.astype(BF16)
        normed_out[...] = normed
        inverse_out[...] = jnp.broadcast_to(inverse, inverse_out.shape)


def whole(shape):
    return pl.BlockSpec(shape, lambda i: (0,) * len(shape))


def params(limit=58):
    return pltpu.CompilerParams(
        dimension_semantics=("arbitrary",), vmem_limit_bytes=limit * 1024 * 1024
    )


def attention_forward(segment, tails, starts, words, edge, weights):
    width = words.shape[2]
    steps = width // QUAD
    row_block = pl.BlockSpec((QUAD, width), lambda i: (i, 0))
    col_block = pl.BlockSpec((width, QUAD), lambda i: (0, i))
    bias_block = pl.BlockSpec((1, QUAD), lambda i: (0, i))
    rows_block = pl.BlockSpec((ROWS, QUAD), lambda i: (0, i))
    vector = whole((1, width))
    full = whole((ROWS, width))
    stats = whole((ROWS, 128))
    shape = jax.ShapeDtypeStruct
    return pl.pallas_call(
        functools.partial(attention_forward_kernel, segment),
        grid=(steps,),
        in_specs=[
            pl.BlockSpec(memory_space=pltpu.SMEM), pl.BlockSpec(memory_space=pltpu.SMEM),
            pl.BlockSpec((1, ROWS, width), lambda i: (segment, 0, 0)), whole(edge.shape), row_block, row_block, row_block, col_block,
            bias_block, bias_block, vector, vector, vector,
        ],
        out_specs=[
            rows_block, rows_block, rows_block,
            pl.BlockSpec((4, ROWS, MAIN), lambda i: (i, 0, 0)),
            pl.BlockSpec((4, ROWS - MAIN, LAST), lambda i: (i, 0, 0)),
            stats, rows_block, full, full, stats, full, full,
        ],
        out_shape=[
            shape((ROWS, width), BF16), shape((ROWS, width), BF16), shape((ROWS, width), BF16),
            shape((HEADS, ROWS, MAIN), BF16), shape((HEADS, ROWS - MAIN, LAST), BF16),
            shape((ROWS, 128), F32), shape((ROWS, width), BF16),
            shape((ROWS, width), F32), shape((ROWS, width), F32), shape((ROWS, 128), F32),
            shape((ROWS, width), BF16), shape((ROWS, width), BF16),
        ],
        scratch_shapes=[
            pltpu.VMEM((ROWS, width), F32),
            pltpu.VMEM((ROWS, MAIN), F32),
            pltpu.VMEM((ROWS - MAIN, LAST), F32),
            pltpu.VMEM((KEYS, QUAD), BF16),
            pltpu.VMEM((KEYS, QUAD), BF16),
            pltpu.VMEM((ROWS, width), F32),
        ],
        compiler_params=params(),
        name="attention_forward",
    )(
        tails, starts, words, edge, weights["q"], weights["k"], weights["v"], weights["o"],
        weights["vq"], weights["vv"], weights["vo"], weights["ag"], weights["as"],
    )


def feed_forward_kernel(
    hidden, narrow, wu, wd, vu, vd, gain, shift, act_out, slope_out, y_out, edge_out, normed_out, inverse_out,
    total,
):
    step = pl.program_id(0)

    @pl.when(step == 0)
    def _():
        total[...] = jnp.zeros_like(total)

    upward = nn(narrow[...], wu[...]) + vu[...]
    act, slope = gelu_pair(upward)
    act_out[...] = act.astype(BF16)
    slope_out[...] = slope.astype(BF16)
    total[...] += nt(act_out[...], wd[...])

    @pl.when(step == pl.num_programs(0) - 1)
    def _():
        y, normed, inverse = norm_forward(
            hidden[...] + (total[...] + vd[...]), gain[...], shift[...]
        )
        y_out[...] = y.astype(BF16)
        edge_out[...] = y[MEMORY + TEXT :, :]
        normed_out[...] = normed
        inverse_out[...] = jnp.broadcast_to(inverse, inverse_out.shape)


def feed_forward(hidden, narrow, weights):
    width = hidden.shape[1]
    units = weights["u"].shape[1]
    vector = whole((1, width))
    full = whole((ROWS, width))
    block = pl.BlockSpec((ROWS, UNITS), lambda i: (0, i))
    shape = jax.ShapeDtypeStruct
    return pl.pallas_call(
        feed_forward_kernel,
        grid=(units // UNITS,),
        in_specs=[
            full, full,
            pl.BlockSpec((width, UNITS), lambda i: (0, i)),
            pl.BlockSpec((width, UNITS), lambda i: (0, i)),
            pl.BlockSpec((1, UNITS), lambda i: (0, i)),
            vector, vector, vector,
        ],
        out_specs=[block, block, full, whole((ROWS - MEMORY - TEXT, width)), full, whole((ROWS, 128))],
        out_shape=[
            shape((ROWS, units), BF16), shape((ROWS, units), BF16), shape((ROWS, width), BF16),
            shape((ROWS - MEMORY - TEXT, width), F32), shape((ROWS, width), F32), shape((ROWS, 128), F32),
        ],
        scratch_shapes=[pltpu.VMEM((ROWS, width), F32)],
        compiler_params=params(),
        name="feed_forward",
    )(
        hidden, narrow, weights["u"], weights["d"], weights["vu"], weights["vd"],
        weights["og"], weights["os"],
    )


def feed_backward_kernel(
    segment, dy, top, bottom, normed2, inverse2, normed1, inverse1, slope, wd, wu, wo, gain2, gain1,
    gd_out, gu_out, gb_out, dfirst_out, gm_out, vu_out, sums_out,
    dsecond, dhidden,
):
    step = pl.program_id(0)

    @pl.when(step == 0)
    def _():
        dsecond[...] = dy[0]
        if segment == 0:
            dsecond[MEMORY + TEXT : SEG_ROWS, :] += top[:MEMORY, :] + bottom[:MEMORY, :]
        grad, normed = dsecond[...], normed2[...]
        sums_out[0:1, :] = column_sum(grad * normed)
        sums_out[1:2, :] = column_sum(grad)
        second = norm_backward(grad, normed, inverse2[:, 0:1], gain2[...])
        dsecond[...] = second
        narrow = second.astype(BF16)
        gd_out[...] = narrow
        sums_out[2:3, :] = column_sum(narrow.astype(F32))
        dhidden[...] = jnp.zeros_like(dhidden)

    up = (nn(gd_out[...], wd[...]) * slope[...].astype(F32)).astype(BF16)
    gu_out[...] = up
    vu_out[...] = column_sum(up.astype(F32))
    dhidden[...] += nt(up, wu[...])

    @pl.when(step == pl.num_programs(0) - 1)
    def _():
        grad, normed = dhidden[...] + dsecond[...], normed1[...]
        sums_out[3:4, :] = column_sum(grad * normed)
        sums_out[4:5, :] = column_sum(grad)
        first = norm_backward(grad, normed, inverse1[:, 0:1], gain1[...])
        dfirst_out[...] = first
        narrow = first.astype(BF16)
        gb_out[...] = narrow
        sums_out[5:6, :] = column_sum(narrow.astype(F32))
        sums_out[6:8, :] = jnp.zeros((2, narrow.shape[1]), F32)
        gm_out[...] = nn(narrow, wo[...]).astype(BF16)


def feed_backward(segment, dy, later, saved, weights):
    width = dy.shape[2]
    edges = ROWS - MEMORY - TEXT
    units = weights["u"].shape[1]
    vector = whole((1, width))
    full = whole((ROWS, width))
    stats = whole((ROWS, 128))
    block = pl.BlockSpec((ROWS, UNITS), lambda i: (0, i))
    shape = jax.ShapeDtypeStruct
    return pl.pallas_call(
        functools.partial(feed_backward_kernel, segment),
        grid=(units // UNITS,),
        in_specs=[
            pl.BlockSpec((1, ROWS, width), lambda i: (segment, 0, 0)),
            pl.BlockSpec((edges, width), lambda i: (0, 0)),
            pl.BlockSpec((edges, width), lambda i: ((MEMORY + TEXT) // edges, 0)),
            full, stats, full, stats, block,
            pl.BlockSpec((width, UNITS), lambda i: (0, i)),
            pl.BlockSpec((width, UNITS), lambda i: (0, i)),
            whole((width, width)), vector, vector,
        ],
        out_specs=[
            full, block, full, full, full,
            pl.BlockSpec((1, UNITS), lambda i: (0, i)), whole((8, width)),
        ],
        out_shape=[
            shape((ROWS, width), BF16), shape((ROWS, units), BF16), shape((ROWS, width), BF16),
            shape((ROWS, width), F32), shape((ROWS, width), BF16),
            shape((1, units), F32), shape((8, width), F32),
        ],
        scratch_shapes=[pltpu.VMEM((ROWS, width), F32), pltpu.VMEM((ROWS, width), F32)],
        compiler_params=params(),
        name="feed_backward",
    )(
        dy, later, later, saved["normed2"], saved["inverse2"], saved["normed1"], saved["inverse1"],
        saved["slope"], weights["d"], weights["u"], weights["o"], weights["og"], weights["ag"],
    )


def backward_pair(pair, step, q, e, last, total, mixed, gm, k_pad, v_pad, gq_out, gk_out, gv_out):
    lane = lax.broadcasted_iota(jnp.int32, (ROWS, 128), 1)
    at = slice(128 * pair, 128 * pair + 128)
    grad = gm[:, at].astype(F32)
    product = grad * mixed[:, at].astype(F32)
    totals = total[...]
    rates, inners = [], []
    for half in range(2):
        mine = (lane < HEAD_DIM) if half == 0 else (lane >= HEAD_DIM)
        head = step * 4 + 2 * pair + half
        rate = 1.0 / jnp.sum(jnp.where(lane == head, totals, 0.0), axis=-1, keepdims=True)
        rates.append(rate)
        inners.append(jnp.sum(jnp.where(mine, product, 0.0), axis=-1, keepdims=True) * rate)
    scaled = (grad * jnp.where(lane < HEAD_DIM, rates[0], rates[1])).astype(BF16)
    scaled_t = scaled.T
    query_t = q[:, at].T
    gq, gk, gv = [], [], []
    for half in range(2):
        mine = (lane < HEAD_DIM) if half == 0 else (lane >= HEAD_DIM)
        rows = slice(HEAD_DIM * half, HEAD_DIM * half + HEAD_DIM)
        inner = inners[half]
        gmm = jnp.where(mine, scaled, jnp.zeros((), BF16))
        dp = nt(gmm, v_pad[:MAIN, at])
        last_dp = nt(gmm[MAIN:], v_pad[MAIN:, at])
        narrow_e, narrow_last = e[2 * pair + half], last[2 * pair + half]
        ds = (narrow_e.astype(F32) * (dp - inner)).astype(BF16)
        last_ds = (narrow_last.astype(F32) * (last_dp - inner[MAIN:])).astype(BF16)
        gq.append(plus_last(nn(ds, k_pad[:MAIN, at]), nn(last_ds, k_pad[MAIN:, at])))
        gk.append(jnp.concatenate([nn(query_t[rows, :], ds), nn(query_t[rows, MAIN:], last_ds)], axis=1))
        gv.append(
            jnp.concatenate([nn(scaled_t[rows, :], narrow_e), nn(scaled_t[rows, MAIN:], narrow_last)], axis=1)
        )
    gq_pair = jnp.where(lane < HEAD_DIM, gq[0], gq[1]) * HEAD_DIM**-0.5
    gq_out[:, at] = gq_pair.astype(BF16)
    gk_out[:, at] = jnp.concatenate(gk, axis=0).T[:ROWS].astype(BF16)
    gv_out[:, at] = jnp.concatenate(gv, axis=0).T[:ROWS].astype(BF16)


def attention_backward_kernel(
    q, k, v, e, last, total, mixed, gm, dfirst, wq, wk, wv,
    gq_out, gk_out, gv_out, dx_out, vq_out, vv_out,
    k_pad, v_pad,
):
    step = pl.program_id(0)

    @pl.when(step == 0)
    def _():
        dx_out[...] = dfirst[...]
        k_pad[...] = jnp.zeros_like(k_pad)
        v_pad[...] = jnp.zeros_like(v_pad)

    k_pad[:ROWS, :] = k[...]
    v_pad[:ROWS, :] = v[...]
    for pair in range(2):
        backward_pair(pair, step, q, e, last, total, mixed, gm, k_pad, v_pad, gq_out, gk_out, gv_out)
    vq_out[...] = column_sum(gq_out[...].astype(F32))
    vv_out[...] = column_sum(gv_out[...].astype(F32))
    dx_out[...] += (
        nn(gq_out[...], wq[...]) + nn(gk_out[...], wk[...]) + nn(gv_out[...], wv[...])
    )


def attention_backward(saved, gm, dfirst, weights):
    width = dfirst.shape[1]
    row_block = pl.BlockSpec((QUAD, width), lambda i: (i, 0))
    rows_block = pl.BlockSpec((ROWS, QUAD), lambda i: (0, i))
    full = whole((ROWS, width))
    sums = pl.BlockSpec((1, QUAD), lambda i: (0, i))
    shape = jax.ShapeDtypeStruct
    return pl.pallas_call(
        attention_backward_kernel,
        grid=(width // QUAD,),
        in_specs=[
            rows_block, rows_block, rows_block,
            pl.BlockSpec((4, ROWS, MAIN), lambda i: (i, 0, 0)),
            pl.BlockSpec((4, ROWS - MAIN, LAST), lambda i: (i, 0, 0)),
            whole((ROWS, 128)), rows_block, rows_block, full, row_block, row_block, row_block,
        ],
        out_specs=[rows_block, rows_block, rows_block, full, sums, sums],
        out_shape=[
            shape((ROWS, width), BF16), shape((ROWS, width), BF16), shape((ROWS, width), BF16),
            shape((ROWS, width), F32), shape((1, width), F32), shape((1, width), F32),
        ],
        scratch_shapes=[pltpu.VMEM((KEYS, QUAD), BF16), pltpu.VMEM((KEYS, QUAD), BF16)],
        compiler_params=params(),
        name="attention_backward",
    )(
        saved["q"], saved["k"], saved["v"], saved["e"], saved["last"], saved["total"], saved["mixed"],
        gm, dfirst, weights["q"], weights["k"], weights["v"],
    )


ROWS_MESH = 4
LINES = 16
MESH_IDS = pl.DeviceIdType.MESH
Z_UP, Z_DOWN, ACROSS, ALONG, HALF_ACROSS, HALF_ALONG = range(6)
SHARE = 6


class Place:
    def __init__(self, cols):
        self.row, self.col = lax.axis_index("row"), lax.axis_index("col")
        self.length = cols // 2
        self.core = lax.rem(self.col, 2)
        self.line = lax.div(self.col, 2)
        self.across_row = self.row + 1 - 2 * lax.rem(self.row, 2)
        self.along_row = self.row + 2 - 4 * lax.div(self.row, 2)
        self.corner_row = 3 - self.row
        self.across = (self.across_row, self.col)
        self.along = (self.along_row, self.col)
        self.up = (self.row, self.col + 2)
        self.down = (self.row, self.col - 2)
        self.other_core = 1 - self.core
        self.partner = (self.row, self.col + 1 - 2 * self.core)

    def greet(self):
        barrier = pltpu.get_barrier_semaphore()

        def signal(device):
            pl.semaphore_signal(barrier, inc=1, device_id=device, device_id_type=MESH_IDS)

        signal(self.across)
        signal(self.along)
        signal(self.partner)
        pl.when(self.line > 0)(lambda: signal(self.down))
        pl.when(self.line < self.length - 1)(lambda: signal(self.up))
        has_down = lax.div(self.line + self.length - 1, self.length)
        has_up = lax.div(2 * self.length - 2 - self.line, self.length)
        pl.semaphore_wait(barrier, 3 + has_down + has_up)

    def at_distance(self, distance, visit):
        if distance == 0:
            visit(self.line, None)
        else:
            below, above = self.line - distance, self.line + distance
            pl.when(below >= 0)(lambda: visit(below, True))
            pl.when(above < self.length)(lambda: visit(above, False))


def splits(count):
    first = count // 32 * 16
    return ((0, first), (first, count - first))


def gather_kernel(
    square, upper, lower, wq, wk, wv, wo, *rest
):
    vectors, (whole_upper, whole_lower, gathered, send, recv, own) = rest[:9], rest[9:]
    rows, cols = ROWS_MESH, wq.shape[0] // lower.shape[0]
    place = Place(cols)
    depth, across = upper.shape[0], lower.shape[0]
    sources = (square, upper, lower)

    def target(which, row, col, part=None):
        if which == 0:
            view, count = gathered.at[row * cols + col], square.shape[0]
            begin, size = part if part else (0, count)
            return view.at[pl.ds(begin, size)]
        count, wide = sources[which].shape
        array, high, side = (whole_upper, row, col) if which == 1 else (whole_lower, col, row)
        begin, size = part if part else (0, count)
        return array.at[
            pl.ds(pl.multiple_of(high * count + begin, 16), size),
            pl.ds(pl.multiple_of(side * wide, 128), wide),
        ]

    def copy(which, kind, row, line, device, part=None, mine=None, arrival=None):
        col = 2 * line + (place.core if mine is None else mine)
        there = target(which, row, col, part)
        here = there if arrival is None else sources[which]
        return pltpu.make_async_remote_copy(
            src_ref=here, dst_ref=there,
            send_sem=send.at[which, kind, line], recv_sem=recv.at[which, kind, line],
            device_id=device, device_id_type=MESH_IDS,
        )

    place.greet()
    keeps = []
    for which in range(3):
        keep = pltpu.make_async_copy(
            sources[which], target(which, place.row, place.col), own.at[which]
        )
        keep.start()
        keeps.append(keep)

    def both(which):
        return splits(sources[which].shape[0])

    def by_line(which, distance):
        def visit(line, upward):
            first = True if upward is None else None
            args = (place.row, line)
            if upward is not None:
                kind = Z_UP if upward else Z_DOWN
                copy(which, kind, *args, place.down).wait_recv()
            if upward is None or upward:
                pl.when(place.line < place.length - 1)(
                    lambda: copy(which, Z_UP, *args, place.up, arrival=first).start()
                )
            if upward is None or not upward:
                pl.when(place.line > 0)(
                    lambda: copy(which, Z_DOWN, *args, place.down, arrival=first).start()
                )
            copy(which, ACROSS, *args, place.across, arrival=first).start()
            copy(which, ALONG, *args, place.along, arrival=first).start()
            copy(which, SHARE, *args, place.partner, arrival=first).start()

        place.at_distance(distance, visit)

    def by_side(which, distance):
        halves = both(which)

        def visit(line, upward):
            copy(which, ACROSS, place.across_row, line, place.across).wait_recv()
            copy(which, HALF_ALONG, place.across_row, line, place.along, halves[1]).start()
            copy(which, SHARE + 1, place.across_row, line, place.partner).start()
            copy(which, ALONG, place.along_row, line, place.along).wait_recv()
            copy(which, HALF_ACROSS, place.along_row, line, place.across, halves[0]).start()
            copy(which, SHARE + 2, place.along_row, line, place.partner).start()

        place.at_distance(distance, visit)

    def by_corner(which, distance):
        halves = both(which)

        def visit(line, upward):
            copy(which, HALF_ACROSS, place.corner_row, line, place.across, halves[0]).wait_recv()
            copy(which, SHARE + 3, place.corner_row, line, place.partner, halves[0]).start()
            copy(which, HALF_ALONG, place.corner_row, line, place.along, halves[1]).wait_recv()
            copy(which, SHARE + 4, place.corner_row, line, place.partner, halves[1]).start()

        place.at_distance(distance, visit)

    def from_partner(which):
        halves = both(which)
        for distance in range(place.length):

            def visit(line, upward):
                mine = place.other_core
                for kind, row, part in (
                    (0, place.row, None), (1, place.across_row, None), (2, place.along_row, None),
                    (3, place.corner_row, halves[0]), (4, place.corner_row, halves[1]),
                ):
                    copy(which, SHARE + kind, row, line, place.partner, part, mine=mine).wait_recv()

            place.at_distance(distance, visit)

    def drain(which):
        halves = both(which)
        for distance in range(place.length):

            def visit(line, upward):
                args = (place.row, line)
                first = True if upward is None else None
                if upward is None or upward:
                    pl.when(place.line < place.length - 1)(
                        lambda: copy(which, Z_UP, *args, place.up, arrival=first).wait_send()
                    )
                if upward is None or not upward:
                    pl.when(place.line > 0)(
                        lambda: copy(which, Z_DOWN, *args, place.down, arrival=first).wait_send()
                    )
                copy(which, ACROSS, *args, place.across, arrival=first).wait_send()
                copy(which, ALONG, *args, place.along, arrival=first).wait_send()
                copy(which, SHARE, *args, place.partner, arrival=first).wait_send()
                copy(which, HALF_ALONG, place.across_row, line, place.along, halves[1]).wait_send()
                copy(which, HALF_ACROSS, place.along_row, line, place.across, halves[0]).wait_send()
                copy(which, SHARE + 1, place.across_row, line, place.partner).wait_send()
                copy(which, SHARE + 2, place.along_row, line, place.partner).wait_send()
                copy(which, SHARE + 3, place.corner_row, line, place.partner, halves[0]).wait_send()
                copy(which, SHARE + 4, place.corner_row, line, place.partner, halves[1]).wait_send()

            place.at_distance(distance, visit)

    length = place.length
    finish = length + 2
    for step in range(finish + 4):
        for which in range(3):
            distance = step - 2 * which
            if 0 <= distance < length:
                by_line(which, distance)
            if 1 <= distance < length + 1:
                by_side(which, distance - 1)
            if 2 <= distance < length + 2:
                by_corner(which, distance - 2)
        if step == finish:
            from_partner(0)
            keeps[0].wait()
            outs = (wq, wk, wv, wo)
            for col in range(cols):
                for at, out in enumerate(outs):
                    out[across * col : across * col + across, :] = jnp.concatenate(
                        [
                            gathered[row * cols + col, :across, depth * at : depth * at + depth]
                            for row in range(rows)
                        ],
                        axis=1,
                    )
            lines = [gathered[col, across:, :across].astype(F32) for col in range(cols)]
            table = jnp.concatenate(lines, axis=1)
            for at in range(8):
                vectors[at][...] = table[at : at + 1]
            vectors[8][...] = jnp.concatenate(
                [line[8 + at : 9 + at] for line in lines for at in range(upper.shape[1] // across)], axis=1
            )
    for which in range(1, 3):
        from_partner(which)
        keeps[which].wait()
    for which in range(3):
        drain(which)


def pack_kernel(wq, wk, wv, wo, wd, vectors, square, lower):
    across, depth = wq.shape[1], wq.shape[0]
    square[:across, :] = jnp.concatenate(
        [item[...].astype(F32).T for item in (wq, wk, wv, wo)], axis=1
    ).astype(BF16)
    square[across:, :] = jnp.zeros((LINES, square.shape[1]), BF16)
    square[across : across + LINES, :128] = vectors[...]
    lower[...] = wd[...].astype(F32).T.astype(BF16)


def fetch_by_kernel(arguments):
    matrices, vectors = arguments[:6], arguments[6:]
    rows, cols = lax.axis_size("row"), lax.axis_size("col")
    depth, across = matrices[0].shape
    width = depth * rows
    units = matrices[4].shape[1] * cols
    table = jnp.stack([*vectors[:5], *vectors[6:]])
    table = jnp.concatenate([table, vectors[5].reshape(-1, across)], axis=0)
    table = jnp.pad(table, ((0, LINES - table.shape[0]), (0, 128 - across)))
    shape = jax.ShapeDtypeStruct
    square, lower = pl.pallas_call(
        pack_kernel,
        out_shape=[shape((across + LINES, 4 * depth), BF16), shape((across, matrices[5].shape[0]), BF16)],
        in_specs=[pl.BlockSpec(memory_space=pltpu.VMEM)] * 6,
        out_specs=[pl.BlockSpec(memory_space=pltpu.VMEM)] * 2,
        name="pack",
    )(*matrices[:4], matrices[5], table)
    anywhere, local = pl.BlockSpec(memory_space=pl.ANY), pl.BlockSpec(memory_space=pltpu.VMEM)
    kinds = (3, SHARE + 5, cols // 2)
    vector = shape((1, width), F32)
    names = ("q", "k", "v", "o", "vq", "vv", "vo", "ag", "as", "vd", "og", "os", "vu", "u", "d")
    whole_arrays = pl.pallas_call(
        gather_kernel,
        out_shape=[shape((width, width), BF16)] * 4 + [vector] * 8 + [shape((1, units), F32)]
        + [shape((width, units), BF16), shape((width, units), BF16)],
        in_specs=[anywhere] * 3,
        out_specs=[local] * 13 + [anywhere] * 2,
        scratch_shapes=[
            pltpu.VMEM((rows * cols, across + LINES, 4 * depth), BF16),
            pltpu.SemaphoreType.DMA(kinds), pltpu.SemaphoreType.DMA(kinds), pltpu.SemaphoreType.DMA((3,)),
        ],
        compiler_params=pltpu.CompilerParams(
            collective_id=0, has_side_effects=True, vmem_limit_bytes=58 * 1024 * 1024
        ),
        name="gather",
    )(square, matrices[4], lower)
    return dict(zip(names, whole_arrays))


def scatter_kernel(square, upper, lower, square_out, upper_out, lower_out, *scratch):
    mine, theirs, corner, side, lined = (scratch[3 * at : 3 * at + 3] for at in range(5))
    send, recv, own = scratch[15:]
    rows, cols = ROWS_MESH, square.shape[0] // ROWS_MESH
    place = Place(cols)
    outs = (square_out, upper_out, lower_out)
    length = place.length

    def source(which, row, col):
        count, wide = outs[which].shape
        if which == 0:
            return square.at[row * cols + col]
        array, high, level = (upper, row, col) if which == 1 else (lower, col, row)
        return array.at[
            pl.ds(pl.multiple_of(high * count, 16), count),
            pl.ds(pl.multiple_of(level * wide, 128), wide),
        ]

    def load(which, row, line):
        return pltpu.make_async_copy(
            source(which, row, 2 * line + place.core),
            mine[which].at[row * length + line], own.at[which, row * length + line],
        )

    def share(which, row, line, core):
        at = row * length + line
        return pltpu.make_async_remote_copy(
            src_ref=source(which, row, 2 * line + core), dst_ref=theirs[which].at[at],
            send_sem=send.at[which, SHARE + row, line], recv_sem=recv.at[which, SHARE + row, line],
            device_id=place.partner, device_id_type=MESH_IDS,
        )

    def remote(which, kind, line, here, there, device):
        return pltpu.make_async_remote_copy(
            src_ref=here, dst_ref=there,
            send_sem=send.at[which, kind, line], recv_sem=recv.at[which, kind, line],
            device_id=device, device_id_type=MESH_IDS,
        )

    def corner_copy(which, kind, line):
        begin, size = splits(outs[which].shape[0])[kind - HALF_ACROSS]
        part = pl.ds(begin, size)
        here = mine[which].at[place.corner_row * length + line, part]
        there = corner[which].at[line, part]
        return remote(which, kind, line, here, there, place.across if kind == HALF_ACROSS else place.along)

    def side_copy(which, kind, line):
        row, device = (place.across_row, place.across) if kind == ACROSS else (place.along_row, place.along)
        here = mine[which].at[row * length + line]
        return remote(which, kind, line, here, side[which].at[kind - ACROSS, line], device)

    def line_copy(which, kind, line):
        here = mine[which].at[place.row * length + line]
        return remote(which, kind, line, here, lined[which].at[kind, line], place.up if kind == Z_UP else place.down)

    def add(which, at, arrived, part=None):
        block = mine[which].at[at] if part is None else mine[which].at[at, pl.ds(*part)]
        block[...] = (block[...].astype(F32) + arrived[...].astype(F32)).astype(BF16)

    place.greet()

    def spread(distance, visit):
        place.at_distance(distance, lambda line, upward: visit(line))

    farthest = range(length - 1, -1, -1)
    order = ("corner_row", "across_row", "along_row", "row")
    for which in range(3):
        for distance in farthest:

            def begin(line):
                for name in order:
                    row = getattr(place, name)
                    load(which, row, line).start()
                    share(which, row, line, place.other_core).start()

            spread(distance, begin)

    def merge(which, row, line):
        load(which, row, line).wait()
        share(which, row, line, place.core).wait_recv()
        at = row * length + line
        add(which, at, theirs[which].at[at])

    def cores(which, distance):
        def visit(line):
            merge(which, place.corner_row, line)
            merge(which, place.across_row, line)
            corner_copy(which, HALF_ACROSS, line).start()
            corner_copy(which, HALF_ALONG, line).start()
            merge(which, place.along_row, line)
            merge(which, place.row, line)

        spread(distance, visit)

    def corners(which, distance):
        first, second = splits(outs[which].shape[0])

        def visit(line):
            corner_copy(which, HALF_ACROSS, line).wait_recv()
            add(which, place.along_row * length + line, corner[which].at[line, pl.ds(*first)], first)
            corner_copy(which, HALF_ALONG, line).wait_recv()
            add(which, place.across_row * length + line, corner[which].at[line, pl.ds(*second)], second)
            side_copy(which, ALONG, line).start()
            side_copy(which, ACROSS, line).start()

        spread(distance, visit)

    def sides(which, distance):
        def visit(line):
            at = place.row * length + line
            side_copy(which, ACROSS, line).wait_recv()
            add(which, at, side[which].at[0, line])
            side_copy(which, ALONG, line).wait_recv()
            add(which, at, side[which].at[1, line])

        spread(distance, visit)

    def lines(which, distance):
        def visit(line, downward):
            at = place.row * length + line
            kind = Z_DOWN if downward else Z_UP
            onward = place.line < length - 1 if downward else place.line > 0

            @pl.when(onward)
            def _():
                line_copy(which, kind, line).wait_recv()
                add(which, at, lined[which].at[kind, line])

            line_copy(which, kind, line).start()

        place.at_distance(distance, visit)

    def result(which):
        at = place.row * length + place.line
        for kind, there in ((Z_UP, place.line > 0), (Z_DOWN, place.line < length - 1)):

            @pl.when(there)
            def _():
                line_copy(which, kind, place.line).wait_recv()
                add(which, at, lined[which].at[kind, place.line])

        outs[which][...] = mine[which][at].astype(F32)

    def drain(which):
        for distance in farthest:

            def visit(line, downward):
                for row in range(rows):
                    share(which, row, line, place.other_core).wait_send()
                for kind in (HALF_ACROSS, HALF_ALONG):
                    corner_copy(which, kind, line).wait_send()
                for kind in (ACROSS, ALONG):
                    side_copy(which, kind, line).wait_send()
                if downward is not None:
                    line_copy(which, Z_DOWN if downward else Z_UP, line).wait_send()

            place.at_distance(distance, visit)

    for step in range(length + 3 + 4):
        for which in range(3):
            stage = step - 2 * which
            if 0 <= stage < length:
                cores(which, length - 1 - stage)
            if 1 <= stage < length + 1:
                corners(which, length - stage)
            if 2 <= stage < length + 2:
                sides(which, length + 1 - stage)
            if 3 <= stage < length + 2:
                lines(which, length + 2 - stage)
            if stage == length + 2:
                result(which)
    for which in range(3):
        drain(which)


def scatter_by_kernel(square, upper, lower):
    cols = square.shape[0] // ROWS_MESH
    length = cols // 2
    count, wide = square.shape[1:]
    blocks = (
        (count, wide),
        (upper.shape[0] // ROWS_MESH, upper.shape[1] // cols),
        (lower.shape[0] // cols, lower.shape[1] // ROWS_MESH),
    )
    kinds = (3, SHARE + ROWS_MESH, length)
    anywhere, local = pl.BlockSpec(memory_space=pl.ANY), pl.BlockSpec(memory_space=pltpu.VMEM)
    buffers = [
        pltpu.VMEM((*lead, *block), BF16)
        for lead in ((ROWS_MESH * length,), (ROWS_MESH * length,), (length,), (2, length), (2, length))
        for block in blocks
    ]
    return pl.pallas_call(
        scatter_kernel,
        out_shape=[jax.ShapeDtypeStruct(block, F32) for block in blocks],
        in_specs=[anywhere] * 3,
        out_specs=[local] * 3,
        scratch_shapes=[
            *buffers,
            pltpu.SemaphoreType.DMA(kinds), pltpu.SemaphoreType.DMA(kinds),
            pltpu.SemaphoreType.DMA((3, ROWS_MESH * length)),
        ],
        compiler_params=pltpu.CompilerParams(
            collective_id=1, has_side_effects=True, vmem_limit_bytes=50 * 1024 * 1024
        ),
        name="scatter",
    )(square, upper, lower)


def joined(first, second):
    return jnp.concatenate([first, second], axis=0)


def product_kernel(left1, left2, right1, right2, out, turned):
    @pl.when(pl.program_id(0) == 0)
    def _():
        turned[...] = joined(left1[...], left2[...]).T

    out[...] = nn(turned[...], joined(right1[...], right2[...])).astype(BF16)


def product_t(left1, left2, right1, right2):
    width, units = left1.shape[1], right1.shape[1]
    block = pl.BlockSpec((ROWS, UNITS), lambda i: (0, i))
    return pl.pallas_call(
        product_kernel,
        grid=(units // UNITS,),
        in_specs=[whole((ROWS, width))] * 2 + [block] * 2,
        out_specs=pl.BlockSpec((width, UNITS), lambda i: (0, i)),
        out_shape=jax.ShapeDtypeStruct((width, units), BF16),
        scratch_shapes=[pltpu.VMEM((width, 2 * ROWS), BF16)],
        compiler_params=params(),
        name="weight_gradient",
    )(left1, left2, right1, right2)


SUM_ROWS = (5, 3, 4, 2, 0, 1)


def square_kernel(
    gq1, gq2, gk1, gk2, gv1, gv2, gb1, gb2, x1, x2, mixed1, mixed2,
    vq1, vq2, vv1, vv2, sums1, sums2, vu1, vu2, out, total
):
    rows = ROWS_MESH
    cols = out.shape[0] // rows
    width = out.shape[2]
    across, depth = width // cols, width // rows
    sums = sums1[...] + sums2[...]
    wide = vu1[...] + vu2[...]
    vectors = jnp.concatenate(
        [vq1[...] + vq2[...], vv1[...] + vv2[...]] + [sums[at : at + 1] for at in SUM_ROWS], axis=0
    )
    lefts = ((gq1, gq2), (gk1, gk2), (gv1, gv2), (gb1, gb2))
    for at, (left1, left2) in enumerate(lefts):
        right1, right2 = (x1, x2) if at < 3 else (mixed1, mixed2)
        left, right = joined(left1[...], left2[...]), joined(right1[...], right2[...])
        total[at] = nn(left.T, right).astype(BF16)
    share = wide.shape[1] // cols // across
    for col in range(cols):
        begin = across * col
        narrow = jnp.concatenate(
            [vectors[:, begin : begin + across]]
            + [wide[:, across * (col * share + at) : across * (col * share + at + 1)] for at in range(share)]
            + [jnp.zeros((LINES - 8 - share, across), F32)],
            axis=0,
        )
        narrow = jnp.pad(narrow, ((0, 0), (0, out.shape[2] - across))).astype(BF16)
        for row in range(rows):
            block = row * cols + col
            out[block, :across, :] = jnp.concatenate(
                [total[at, begin : begin + across, depth * row : depth * row + depth] for at in range(4)],
                axis=1,
            )
            out[block, across:, :] = narrow


def square_gradients(grads1, grads2, saved1, saved2, cols):
    width = grads1["gq"].shape[1]
    operands = []
    for name in ("gq", "gk", "gv", "gb"):
        operands += [grads1[name], grads2[name]]
    operands += [saved1["x"], saved2["x"], saved1["mixed"], saved2["mixed"]]
    for name in ("vq", "vv", "sums", "vu"):
        operands += [grads1[name], grads2[name]]
    local = pl.BlockSpec(memory_space=pltpu.VMEM)
    return pl.pallas_call(
        square_kernel,
        in_specs=[local] * len(operands),
        out_specs=local,
        out_shape=jax.ShapeDtypeStruct((ROWS_MESH * cols, width // cols + LINES, width), BF16),
        scratch_shapes=[pltpu.VMEM((4, width, width), BF16)],
        compiler_params=pltpu.CompilerParams(vmem_limit_bytes=58 * 1024 * 1024),
        name="square_gradients",
    )(*operands)


def gather_all(part):
    return lax.all_gather(part, ("row", "col"), axis=0, tiled=False)


def fetch(arguments):
    matrices, vectors = arguments[:6], arguments[6:]
    rows, cols = lax.axis_size("row"), lax.axis_size("col")
    depth, across = matrices[0].shape
    width = depth * rows
    names = ("q", "k", "v", "o")
    square = jnp.concatenate([item.T for item in matrices[:4]], axis=1)
    upper = matrices[4].T.reshape(4, across, depth).transpose(1, 0, 2).reshape(across, 4 * depth)
    lower = matrices[5].T
    line = jnp.concatenate(vectors)
    extra = -(-line.shape[0] // (4 * depth))
    extra += -(across + extra) % 16
    line = jnp.pad(line, (0, extra * 4 * depth - line.shape[0])).reshape(extra, 4 * depth)
    first = gather_all(jnp.concatenate([square, line], axis=0))
    second = gather_all(upper)
    third = gather_all(lower)
    whole_square = (
        first[:, :across].reshape(rows, cols, across, 4, depth)
        .transpose(3, 1, 2, 0, 4).reshape(4, width, width)
    )
    weights = {name: whole_square[at] for at, name in enumerate(names)}
    weights["u"] = (
        second.reshape(rows, cols, across, 4, depth)
        .transpose(0, 4, 1, 3, 2).reshape(width, 4 * width)
    )
    weights["d"] = third.reshape(rows, cols, across, 4 * depth).transpose(1, 2, 0, 3).reshape(width, 4 * width)
    lines = first[:cols, across:].reshape(cols, -1).astype(F32)
    at = 0
    for name, item in zip(("vq", "vv", "vo", "ag", "as", "vu", "vd", "og", "os"), vectors):
        weights[name] = lines[:, at : at + item.shape[0]].reshape(1, -1)
        at += item.shape[0]
    return weights


def scatter_all(terms):
    return lax.psum_scatter(terms, ("row", "col"), scatter_dimension=0, tiled=False)


def scatter(square, upper, lower, lines):
    rows, cols = lax.axis_size("row"), lax.axis_size("col")
    width = square.shape[1]
    depth, across = width // rows, width // cols
    square = square.reshape(4, cols, across, rows, depth).transpose(3, 1, 2, 0, 4)
    square = square.reshape(rows, cols, across, 4 * depth)
    count = lines.shape[1]
    extra = -(-count // (4 * depth))
    extra += -(across + extra) % 16
    lines = jnp.pad(lines, ((0, 0), (0, extra * 4 * depth - count))).astype(BF16)
    lines = jnp.broadcast_to(lines.reshape(1, cols, extra, 4 * depth), (rows, cols, extra, 4 * depth))
    square = jnp.concatenate([square, lines], axis=2)
    square = scatter_all(square.reshape(rows * cols, across + extra, 4 * depth)).astype(F32)
    upper = upper.reshape(rows, depth, cols, 4 * across).transpose(0, 2, 1, 3)
    upper = scatter_all(upper.reshape(rows * cols, depth, 4 * across)).astype(F32)
    lower = lower.reshape(cols, across, rows, 4 * depth).transpose(2, 0, 1, 3)
    lower = scatter_all(lower.reshape(rows * cols, across, 4 * depth)).astype(F32)
    return square[:across], upper, lower, square[across:].reshape(-1)[:count]


def solution_body(
    text, memory, tail_lengths, picture_starts, grad_out, *parameters
):
    rows, cols = lax.axis_size("row"), lax.axis_size("col")
    depth, across = parameters[0].shape
    width = depth * rows
    by_kernel = rows == ROWS_MESH and cols % 2 == 0 and depth % 32 == 0 and across % 32 == 0
    by_kernel = by_kernel and 4 * across % 128 == 0
    weights = fetch_by_kernel(parameters) if by_kernel else fetch(parameters)
    words = jnp.pad(text[0].astype(F32), ((0, 0), (MEMORY, ROWS - MEMORY - TEXT), (0, 0)))

    def forward(segment, edge):
        q, k, v, e, last, total, mixed, hidden, normed1, inverse1, xb, hb = attention_forward(
            segment, tail_lengths, picture_starts, words, edge, weights
        )
        act, slope, y, edge, normed2, inverse2 = feed_forward(hidden, hb, weights)
        saved = dict(
            x=xb, q=q, k=k, v=v, e=e, last=last, total=total, mixed=mixed, hidden=hb,
            normed1=normed1, inverse1=inverse1, act=act, slope=slope, normed2=normed2, inverse2=inverse2,
        )
        return y, edge, saved

    def paired(first, second, begin, count):
        which = lax.broadcasted_iota(jnp.int32, (count, 2, width), 1)
        first, second = (item[begin : begin + count, None, :] for item in (first, second))
        return jnp.where(which == 0, first, second).astype(BF16).transpose(1, 0, 2)[None]

    y1, edge1, saved1 = forward(0, memory[0])
    y2, edge2, saved2 = forward(1, edge1)
    layer_output = paired(y1, y2, 0, SEG_ROWS)

    def backward(segment, later, saved):
        gd, gu, gb, dfirst, gm, vu, sums = feed_backward(segment, cotangent, later, saved, weights)
        gq, gk, gv, dx, vq, vv = attention_backward(saved, gm, dfirst, weights)
        return dx, dict(gd=gd, gu=gu, gb=gb, gq=gq, gk=gk, gv=gv, vu=vu, sums=sums, vq=vq, vv=vv)

    cotangent = jnp.pad(grad_out[0].astype(F32), ((0, 0), (0, ROWS - SEG_ROWS), (0, 0)))
    dx2, grads2 = backward(1, saved2["normed2"], saved2)
    dx1, grads1 = backward(0, dx2, saved1)
    memory_grad = (dx1[:MEMORY] + dx1[MEMORY + TEXT : SEG_ROWS]).astype(BF16)[None]
    text_grad = paired(dx1, dx2, MEMORY, TEXT)

    upper = product_t(saved1["hidden"], saved2["hidden"], grads1["gu"], grads2["gu"])
    lower = product_t(grads1["gd"], grads2["gd"], saved1["act"], saved2["act"])
    if by_kernel:
        square = square_gradients(grads1, grads2, saved1, saved2, cols)
        square, upper, lower = scatter_by_kernel(square, upper, lower)
        table = square[across : across + LINES, :across]
        square = square[:across]
        lines = [table[at] for at in range(8)]
        lines.insert(5, table[8 : 8 + upper.shape[1] // across].reshape(-1))
    else:
        square = jnp.stack(
            [
                product_t(grads1["gq"], grads2["gq"], saved1["x"], saved2["x"]),
                product_t(grads1["gk"], grads2["gk"], saved1["x"], saved2["x"]),
                product_t(grads1["gv"], grads2["gv"], saved1["x"], saved2["x"]),
                product_t(grads1["gb"], grads2["gb"], saved1["mixed"], saved2["mixed"]),
            ]
        )
        sums = grads1["sums"] + grads2["sums"]
        wide = grads1["vu"] + grads2["vu"]
        parts = (grads1["vq"] + grads2["vq"], grads1["vv"] + grads2["vv"])
        vectors = jnp.concatenate([*parts, *(sums[at : at + 1] for at in SUM_ROWS)], axis=0)
        table = jnp.concatenate(
            [vectors.reshape(8, cols, across).transpose(1, 0, 2).reshape(cols, -1), wide.reshape(cols, -1)],
            axis=1,
        )
        square, upper, lower, line = scatter(square, upper, lower, table)
        lines = [line[at * across : at * across + across] for at in range(8)]
        lines.insert(5, line[8 * across :])
    own = square.reshape(across, 4, depth)
    result = [own[:, at].T for at in range(4)] + [upper, lower.T]
    return (layer_output, text_grad, memory_grad, *result, *lines)


def solution(mesh):
    batch, matrix, vector = P(("row", "col")), P("row", "col"), P("col")
    return jax.shard_map(
        solution_body,
        mesh=mesh,
        in_specs=(batch,) * 5 + (matrix,) * 6 + (vector,) * 9,
        out_specs=(batch,) * 3 + (matrix,) * 6 + (vector,) * 9,
        check_vma=False,
    )
```

```python
import functools

import jax
import jax.numpy as jnp
from jax import lax
from jax.experimental import pallas as pl
from jax.experimental.pallas import tpu as pltpu
from jax.sharding import PartitionSpec as P

HEADS = 12
HEAD_DIM = 64
MEMORY = 10
TEXT = 502
PICTURE = 256
SEG_ROWS = 522
ROWS = 528
MAIN = 512
LAST = 128
KEYS = MAIN + LAST
QUAD = 256
UNITS = 512
F32 = jnp.float32
BF16 = jnp.bfloat16

EPSILON = 1e-06
MASKED = -1e30
LOG2E = 1.4426950408889634

ERFC_SLOPE = 0.4 * 0.7071067811865476
ERFC_POLY = (0.22562816739082336, 0.2265406847000122, 0.20122945308685303, 0.19582846760749817, 0.07433333992958069, 0.09543049335479736, 0.07776277512311935, -0.1374378800392151, 0.040684547275304794)


def nn(left, right):
    return lax.dot_general(left, right, (((1,), (0,)), ((), ())), preferred_element_type=F32)


def nt(left, right):
    return lax.dot_general(left, right, (((1,), (1,)), ((), ())), preferred_element_type=F32)


def norm_forward(inputs, gain, shift):
    center = jnp.mean(inputs, axis=-1, keepdims=True)
    centred = inputs - center
    spread = jnp.mean(centred * centred, axis=-1, keepdims=True)
    inverse = lax.rsqrt(spread + EPSILON)
    normed = centred * inverse
    return normed * gain + shift, normed, inverse


def norm_backward(grad, normed, inverse, gain):
    scaled = grad * gain
    first = jnp.mean(scaled, axis=-1, keepdims=True)
    second = jnp.mean(scaled * normed, axis=-1, keepdims=True)
    return (scaled - first - normed * second) * inverse


def column_sum(values):
    return jnp.sum(values, axis=0, keepdims=True)


def gelu_pair(upward):
    size = jnp.abs(upward)
    t = 1.0 / (1.0 + ERFC_SLOPE * size)
    poly = jnp.full_like(t, ERFC_POLY[-1])
    for coefficient in ERFC_POLY[-2::-1]:
        poly = poly * t + coefficient
    bell = jnp.exp2(upward * upward * (-0.5 * LOG2E))
    tail = 0.5 * bell * t * poly
    phi = jnp.where(upward < 0.0, tail, 1.0 - tail)
    return upward * phi, phi + upward * (bell * 0.3989422804014327)


def plus_last(values, last):
    return jnp.concatenate([values[:MAIN], values[MAIN:] + last], axis=0)


def attention_forward_kernel(
    segment, tails, starts, words, edge, wq, wk, wv, wo, vq, vv, vo, gain, shift,
    q_out, k_out, v_out, e_out, last_out, total_out, mixed_out, hidden_out, normed_out, inverse_out,
    narrow, narrow_hidden, x, bias, last_bias, k_pad, v_pad, branch,
):
    step = pl.program_id(0)

    @pl.when(step == 0)
    def _():
        x[...] = words[0]
        x[:MEMORY, :] = edge[:MEMORY, :].astype(F32)
        x[MEMORY + TEXT : SEG_ROWS, :] = edge[:MEMORY, :].astype(F32)
        narrow[...] = x[...].astype(BF16)
        branch[...] = jnp.zeros_like(branch)
        total_out[...] = jnp.ones_like(total_out)
        k_pad[...] = jnp.zeros_like(k_pad)
        v_pad[...] = jnp.zeros_like(v_pad)
        length = TEXT if segment == 0 else tails[0]
        start = starts[0, segment]
        low, high = start + MEMORY, start + MEMORY + PICTURE
        row = lax.broadcasted_iota(jnp.int32, (ROWS, MAIN), 0)
        col = lax.broadcasted_iota(jnp.int32, (ROWS, MAIN), 1)
        usable = (col < MEMORY) | (col < MEMORY + length)
        inside = (row >= low) & (row < high) & (col >= low) & (col < high)
        bias[...] = jnp.where(usable & ((col <= row) | inside), 0.0, MASKED)
        row = lax.broadcasted_iota(jnp.int32, (ROWS - MAIN, LAST), 0)
        col = lax.broadcasted_iota(jnp.int32, (ROWS - MAIN, LAST), 1)
        last_bias[...] = jnp.where((col < SEG_ROWS - MAIN) & (col <= row), 0.0, MASKED)

    xb = narrow[...]
    q = ((nt(xb, wq[...]) + vq[...]).astype(BF16).astype(F32) * HEAD_DIM**-0.5).astype(BF16)
    q_out[...] = q
    k_pad[:ROWS, :] = nt(xb, wk[...]).astype(BF16)
    v_pad[:ROWS, :] = (nt(xb, wv[...]) + vv[...]).astype(BF16)
    k_out[...] = k_pad[:ROWS, :]
    v_out[...] = v_pad[:ROWS, :]
    lane = lax.broadcasted_iota(jnp.int32, (ROWS, 128), 1)
    totals = total_out[...]
    for pair in range(2):
        at = slice(128 * pair, 128 * pair + 128)
        halves = []
        for half in range(2):
            mine = (lane < HEAD_DIM) if half == 0 else (lane >= HEAD_DIM)
            qm = jnp.where(mine, q_out[:, at], jnp.zeros((), BF16))
            scores = nt(qm, k_pad[:MAIN, at]) + bias[...]
            last = nt(qm[MAIN:], k_pad[MAIN:, at]) + last_bias[...]
            peak = jnp.max(scores, axis=-1, keepdims=True)
            last_peak = jnp.maximum(peak[MAIN:], jnp.max(last, axis=-1, keepdims=True))
            peak = jnp.concatenate([peak[:MAIN], last_peak], axis=0)
            expos = jnp.exp2((scores - peak) * LOG2E)
            last = jnp.exp2((last - last_peak) * LOG2E)
            total = plus_last(jnp.sum(expos, axis=-1, keepdims=True), jnp.sum(last, axis=-1, keepdims=True))
            narrow_e, last = expos.astype(BF16), last.astype(BF16)
            e_out[2 * pair + half] = narrow_e
            last_out[2 * pair + half] = last
            weighted = plus_last(nn(narrow_e, v_pad[:MAIN, at]), nn(last, v_pad[MAIN:, at]))
            totals = jnp.where(lane == step * 4 + 2 * pair + half, total, totals)
            halves.append(weighted / total)
        mixed_out[:, at] = jnp.where(lane < HEAD_DIM, halves[0], halves[1]).astype(BF16)
    total_out[...] = totals
    branch[...] += nt(mixed_out[...], wo[...])

    @pl.when(step == pl.num_programs(0) - 1)
    def _():
        hidden, normed, inverse = norm_forward(
            x[...] + (branch[...] + vo[...]), gain[...], shift[...]
        )
        hidden_out[...] = hidden
        narrow_hidden[...] = hidden.astype(BF16)
        normed_out[...] = normed
        inverse_out[...] = jnp.broadcast_to(inverse, inverse_out.shape)


def whole(shape):
    return pl.BlockSpec(shape, lambda i: (0,) * len(shape))


def params(limit=58):
    return pltpu.CompilerParams(
        dimension_semantics=("arbitrary",), vmem_limit_bytes=limit * 1024 * 1024
    )


def attention_forward(segment, tails, starts, words, edge, weights):
    width = words.shape[2]
    steps = width // QUAD
    row_block = pl.BlockSpec((QUAD, width), lambda i: (i, 0))
    col_block = pl.BlockSpec((width, QUAD), lambda i: (0, i))
    bias_block = pl.BlockSpec((1, QUAD), lambda i: (0, i))
    rows_block = pl.BlockSpec((ROWS, QUAD), lambda i: (0, i))
    vector = whole((1, width))
    full = whole((ROWS, width))
    stats = whole((ROWS, 128))
    shape = jax.ShapeDtypeStruct
    return pl.pallas_call(
        functools.partial(attention_forward_kernel, segment),
        grid=(steps,),
        in_specs=[
            pl.BlockSpec(memory_space=pltpu.SMEM), pl.BlockSpec(memory_space=pltpu.SMEM),
            pl.BlockSpec((1, ROWS, width), lambda i: (segment, 0, 0)), whole(edge.shape), row_block, row_block, row_block, col_block,
            bias_block, bias_block, vector, vector, vector,
        ],
        out_specs=[
            rows_block, rows_block, rows_block,
            pl.BlockSpec((4, ROWS, MAIN), lambda i: (i, 0, 0)),
            pl.BlockSpec((4, ROWS - MAIN, LAST), lambda i: (i, 0, 0)),
            stats, rows_block, full, full, stats, full, full,
        ],
        out_shape=[
            shape((ROWS, width), BF16), shape((ROWS, width), BF16), shape((ROWS, width), BF16),
            shape((HEADS, ROWS, MAIN), BF16), shape((HEADS, ROWS - MAIN, LAST), BF16),
            shape((ROWS, 128), F32), shape((ROWS, width), BF16),
            shape((ROWS, width), F32), shape((ROWS, width), F32), shape((ROWS, 128), F32),
            shape((ROWS, width), BF16), shape((ROWS, width), BF16),
        ],
        scratch_shapes=[
            pltpu.VMEM((ROWS, width), F32),
            pltpu.VMEM((ROWS, MAIN), F32),
            pltpu.VMEM((ROWS - MAIN, LAST), F32),
            pltpu.VMEM((KEYS, QUAD), BF16),
            pltpu.VMEM((KEYS, QUAD), BF16),
            pltpu.VMEM((ROWS, width), F32),
        ],
        compiler_params=params(),
        name="attention_forward",
    )(
        tails, starts, words, edge, weights["q"], weights["k"], weights["v"], weights["o"],
        weights["vq"], weights["vv"], weights["vo"], weights["ag"], weights["as"],
    )


def feed_forward_kernel(
    hidden, narrow, wu, wd, vu, vd, gain, shift, act_out, slope_out, y_out, edge_out, normed_out, inverse_out,
    total,
):
    step = pl.program_id(0)

    @pl.when(step == 0)
    def _():
        total[...] = jnp.zeros_like(total)

    upward = nn(narrow[...], wu[...]) + vu[...]
    act, slope = gelu_pair(upward)
    act_out[...] = act.astype(BF16)
    slope_out[...] = slope.astype(BF16)
    total[...] += nt(act_out[...], wd[...])

    @pl.when(step == pl.num_programs(0) - 1)
    def _():
        y, normed, inverse = norm_forward(
            hidden[...] + (total[...] + vd[...]), gain[...], shift[...]
        )
        y_out[...] = y.astype(BF16)
        edge_out[...] = y[MEMORY + TEXT :, :]
        normed_out[...] = normed
        inverse_out[...] = jnp.broadcast_to(inverse, inverse_out.shape)


def feed_forward(hidden, narrow, weights):
    width = hidden.shape[1]
    units = weights["u"].shape[1]
    vector = whole((1, width))
    full = whole((ROWS, width))
    block = pl.BlockSpec((ROWS, UNITS), lambda i: (0, i))
    shape = jax.ShapeDtypeStruct
    return pl.pallas_call(
        feed_forward_kernel,
        grid=(units // UNITS,),
        in_specs=[
            full, full,
            pl.BlockSpec((width, UNITS), lambda i: (0, i)),
            pl.BlockSpec((width, UNITS), lambda i: (0, i)),
            pl.BlockSpec((1, UNITS), lambda i: (0, i)),
            vector, vector, vector,
        ],
        out_specs=[block, block, full, whole((ROWS - MEMORY - TEXT, width)), full, whole((ROWS, 128))],
        out_shape=[
            shape((ROWS, units), BF16), shape((ROWS, units), BF16), shape((ROWS, width), BF16),
            shape((ROWS - MEMORY - TEXT, width), F32), shape((ROWS, width), F32), shape((ROWS, 128), F32),
        ],
        scratch_shapes=[pltpu.VMEM((ROWS, width), F32)],
        compiler_params=params(),
        name="feed_forward",
    )(
        hidden, narrow, weights["u"], weights["d"], weights["vu"], weights["vd"],
        weights["og"], weights["os"],
    )


def feed_backward_kernel(
    segment, dy, top, bottom, normed2, inverse2, normed1, inverse1, slope, wd, wu, wo, gain2, gain1,
    gd_out, gu_out, gb_out, dfirst_out, gm_out, vu_out, sums_out,
    dsecond, dhidden,
):
    step = pl.program_id(0)

    @pl.when(step == 0)
    def _():
        dsecond[...] = dy[0]
        if segment == 0:
            dsecond[MEMORY + TEXT : SEG_ROWS, :] += top[:MEMORY, :] + bottom[:MEMORY, :]
        grad, normed = dsecond[...], normed2[...]
        sums_out[0:1, :] = column_sum(grad * normed)
        sums_out[1:2, :] = column_sum(grad)
        second = norm_backward(grad, normed, inverse2[:, 0:1], gain2[...])
        dsecond[...] = second
        narrow = second.astype(BF16)
        gd_out[...] = narrow
        sums_out[2:3, :] = column_sum(narrow.astype(F32))
        dhidden[...] = jnp.zeros_like(dhidden)

    up = (nn(gd_out[...], wd[...]) * slope[...].astype(F32)).astype(BF16)
    gu_out[...] = up
    vu_out[...] = column_sum(up.astype(F32))
    dhidden[...] += nt(up, wu[...])

    @pl.when(step == pl.num_programs(0) - 1)
    def _():
        grad, normed = dhidden[...] + dsecond[...], normed1[...]
        sums_out[3:4, :] = column_sum(grad * normed)
        sums_out[4:5, :] = column_sum(grad)
        first = norm_backward(grad, normed, inverse1[:, 0:1], gain1[...])
        dfirst_out[...] = first
        narrow = first.astype(BF16)
        gb_out[...] = narrow
        sums_out[5:6, :] = column_sum(narrow.astype(F32))
        sums_out[6:8, :] = jnp.zeros((2, narrow.shape[1]), F32)
        gm_out[...] = nn(narrow, wo[...]).astype(BF16)


def feed_backward(segment, dy, later, saved, weights):
    width = dy.shape[2]
    edges = ROWS - MEMORY - TEXT
    units = weights["u"].shape[1]
    vector = whole((1, width))
    full = whole((ROWS, width))
    stats = whole((ROWS, 128))
    block = pl.BlockSpec((ROWS, UNITS), lambda i: (0, i))
    shape = jax.ShapeDtypeStruct
    return pl.pallas_call(
        functools.partial(feed_backward_kernel, segment),
        grid=(units // UNITS,),
        in_specs=[
            pl.BlockSpec((1, ROWS, width), lambda i: (segment, 0, 0)),
            pl.BlockSpec((edges, width), lambda i: (0, 0)),
            pl.BlockSpec((edges, width), lambda i: ((MEMORY + TEXT) // edges, 0)),
            full, stats, full, stats, block,
            pl.BlockSpec((width, UNITS), lambda i: (0, i)),
            pl.BlockSpec((width, UNITS), lambda i: (0, i)),
            whole((width, width)), vector, vector,
        ],
        out_specs=[
            full, block, full, full, full,
            pl.BlockSpec((1, UNITS), lambda i: (0, i)), whole((8, width)),
        ],
        out_shape=[
            shape((ROWS, width), BF16), shape((ROWS, units), BF16), shape((ROWS, width), BF16),
            shape((ROWS, width), F32), shape((ROWS, width), BF16),
            shape((1, units), F32), shape((8, width), F32),
        ],
        scratch_shapes=[pltpu.VMEM((ROWS, width), F32), pltpu.VMEM((ROWS, width), F32)],
        compiler_params=params(),
        name="feed_backward",
    )(
        dy, later, later, saved["normed2"], saved["inverse2"], saved["normed1"], saved["inverse1"],
        saved["slope"], weights["d"], weights["u"], weights["o"], weights["og"], weights["ag"],
    )


def backward_pair(pair, step, q, e, last, total, mixed, gm, k_pad, v_pad, gq_out, gk_out, gv_out):
    lane = lax.broadcasted_iota(jnp.int32, (ROWS, 128), 1)
    at = slice(128 * pair, 128 * pair + 128)
    grad = gm[:, at].astype(F32)
    product = grad * mixed[:, at].astype(F32)
    totals = total[...]
    rates, inners = [], []
    for half in range(2):
        mine = (lane < HEAD_DIM) if half == 0 else (lane >= HEAD_DIM)
        head = step * 4 + 2 * pair + half
        rate = 1.0 / jnp.sum(jnp.where(lane == head, totals, 0.0), axis=-1, keepdims=True)
        rates.append(rate)
        inners.append(jnp.sum(jnp.where(mine, product, 0.0), axis=-1, keepdims=True) * rate)
    scaled = (grad * jnp.where(lane < HEAD_DIM, rates[0], rates[1])).astype(BF16)
    scaled_t = scaled.T
    query_t = q[:, at].T
    gq, gk, gv = [], [], []
    for half in range(2):
        mine = (lane < HEAD_DIM) if half == 0 else (lane >= HEAD_DIM)
        rows = slice(HEAD_DIM * half, HEAD_DIM * half + HEAD_DIM)
        inner = inners[half]
        gmm = jnp.where(mine, scaled, jnp.zeros((), BF16))
        dp = nt(gmm, v_pad[:MAIN, at])
        last_dp = nt(gmm[MAIN:], v_pad[MAIN:, at])
        narrow_e, narrow_last = e[2 * pair + half], last[2 * pair + half]
        ds = (narrow_e.astype(F32) * (dp - inner)).astype(BF16)
        last_ds = (narrow_last.astype(F32) * (last_dp - inner[MAIN:])).astype(BF16)
        gq.append(plus_last(nn(ds, k_pad[:MAIN, at]), nn(last_ds, k_pad[MAIN:, at])))
        gk.append(jnp.concatenate([nn(query_t[rows, :], ds), nn(query_t[rows, MAIN:], last_ds)], axis=1))
        gv.append(
            jnp.concatenate([nn(scaled_t[rows, :], narrow_e), nn(scaled_t[rows, MAIN:], narrow_last)], axis=1)
        )
    gq_pair = jnp.where(lane < HEAD_DIM, gq[0], gq[1]) * HEAD_DIM**-0.5
    gq_out[:, at] = gq_pair.astype(BF16)
    gk_out[:, at] = jnp.concatenate(gk, axis=0).T[:ROWS].astype(BF16)
    gv_out[:, at] = jnp.concatenate(gv, axis=0).T[:ROWS].astype(BF16)


def attention_backward_kernel(
    q, k, v, e, last, total, mixed, gm, dfirst, wq, wk, wv,
    gq_out, gk_out, gv_out, dx_out, vq_out, vv_out,
    k_pad, v_pad,
):
    step = pl.program_id(0)

    @pl.when(step == 0)
    def _():
        dx_out[...] = dfirst[...]
        k_pad[...] = jnp.zeros_like(k_pad)
        v_pad[...] = jnp.zeros_like(v_pad)

    k_pad[:ROWS, :] = k[...]
    v_pad[:ROWS, :] = v[...]
    for pair in range(2):
        backward_pair(pair, step, q, e, last, total, mixed, gm, k_pad, v_pad, gq_out, gk_out, gv_out)
    vq_out[...] = column_sum(gq_out[...].astype(F32))
    vv_out[...] = column_sum(gv_out[...].astype(F32))
    dx_out[...] += (
        nn(gq_out[...], wq[...]) + nn(gk_out[...], wk[...]) + nn(gv_out[...], wv[...])
    )


def attention_backward(saved, gm, dfirst, weights):
    width = dfirst.shape[1]
    row_block = pl.BlockSpec((QUAD, width), lambda i: (i, 0))
    rows_block = pl.BlockSpec((ROWS, QUAD), lambda i: (0, i))
    full = whole((ROWS, width))
    sums = pl.BlockSpec((1, QUAD), lambda i: (0, i))
    shape = jax.ShapeDtypeStruct
    return pl.pallas_call(
        attention_backward_kernel,
        grid=(width // QUAD,),
        in_specs=[
            rows_block, rows_block, rows_block,
            pl.BlockSpec((4, ROWS, MAIN), lambda i: (i, 0, 0)),
            pl.BlockSpec((4, ROWS - MAIN, LAST), lambda i: (i, 0, 0)),
            whole((ROWS, 128)), rows_block, rows_block, full, row_block, row_block, row_block,
        ],
        out_specs=[rows_block, rows_block, rows_block, full, sums, sums],
        out_shape=[
            shape((ROWS, width), BF16), shape((ROWS, width), BF16), shape((ROWS, width), BF16),
            shape((ROWS, width), F32), shape((1, width), F32), shape((1, width), F32),
        ],
        scratch_shapes=[pltpu.VMEM((KEYS, QUAD), BF16), pltpu.VMEM((KEYS, QUAD), BF16)],
        compiler_params=params(),
        name="attention_backward",
    )(
        saved["q"], saved["k"], saved["v"], saved["e"], saved["last"], saved["total"], saved["mixed"],
        gm, dfirst, weights["q"], weights["k"], weights["v"],
    )


ROWS_MESH = 4
LINES = 16
MESH_IDS = pl.DeviceIdType.MESH
Z_UP, Z_DOWN, ACROSS, ALONG, HALF_ACROSS, HALF_ALONG = range(6)
SHARE = 6


class Place:
    def __init__(self, cols):
        self.row, self.col = lax.axis_index("row"), lax.axis_index("col")
        self.length = cols // 2
        self.core = lax.rem(self.col, 2)
        self.line = lax.div(self.col, 2)
        self.across_row = self.row + 1 - 2 * lax.rem(self.row, 2)
        self.along_row = self.row + 2 - 4 * lax.div(self.row, 2)
        self.corner_row = 3 - self.row
        self.across = (self.across_row, self.col)
        self.along = (self.along_row, self.col)
        self.up = (self.row, self.col + 2)
        self.down = (self.row, self.col - 2)
        self.other_core = 1 - self.core
        self.partner = (self.row, self.col + 1 - 2 * self.core)

    def greet(self):
        barrier = pltpu.get_barrier_semaphore()

        def signal(device):
            pl.semaphore_signal(barrier, inc=1, device_id=device, device_id_type=MESH_IDS)

        signal(self.across)
        signal(self.along)
        signal(self.partner)
        pl.when(self.line > 0)(lambda: signal(self.down))
        pl.when(self.line < self.length - 1)(lambda: signal(self.up))
        has_down = lax.div(self.line + self.length - 1, self.length)
        has_up = lax.div(2 * self.length - 2 - self.line, self.length)
        pl.semaphore_wait(barrier, 3 + has_down + has_up)

    def at_distance(self, distance, visit):
        if distance == 0:
            visit(self.line, None)
        else:
            below, above = self.line - distance, self.line + distance
            pl.when(below >= 0)(lambda: visit(below, True))
            pl.when(above < self.length)(lambda: visit(above, False))


def splits(count):
    first = count // 32 * 16
    return ((0, first), (first, count - first))


def gather_kernel(
    square, upper, lower, wq, wk, wv, wo, *rest
):
    vectors, (whole_upper, whole_lower, gathered, send, recv, own) = rest[:9], rest[9:]
    rows, cols = ROWS_MESH, wq.shape[0] // lower.shape[0]
    place = Place(cols)
    depth, across = upper.shape[0], lower.shape[0]
    sources = (square, upper, lower)

    def target(which, row, col, part=None):
        if which == 0:
            view, count = gathered.at[row * cols + col], square.shape[0]
            begin, size = part if part else (0, count)
            return view.at[pl.ds(begin, size)]
        count, wide = sources[which].shape
        array, high, side = (whole_upper, row, col) if which == 1 else (whole_lower, col, row)
        begin, size = part if part else (0, count)
        return array.at[
            pl.ds(pl.multiple_of(high * count + begin, 16), size),
            pl.ds(pl.multiple_of(side * wide, 128), wide),
        ]

    def copy(which, kind, row, line, device, part=None, mine=None, arrival=None):
        col = 2 * line + (place.core if mine is None else mine)
        there = target(which, row, col, part)
        here = there if arrival is None else sources[which]
        return pltpu.make_async_remote_copy(
            src_ref=here, dst_ref=there,
            send_sem=send.at[which, kind, line], recv_sem=recv.at[which, kind, line],
            device_id=device, device_id_type=MESH_IDS,
        )

    place.greet()
    keeps = []
    for which in range(3):
        keep = pltpu.make_async_copy(
            sources[which], target(which, place.row, place.col), own.at[which]
        )
        keep.start()
        keeps.append(keep)

    def both(which):
        return splits(sources[which].shape[0])

    def by_line(which, distance):
        def visit(line, upward):
            first = True if upward is None else None
            args = (place.row, line)
            if upward is not None:
                kind = Z_UP if upward else Z_DOWN
                copy(which, kind, *args, place.down).wait_recv()
            if upward is None or upward:
                pl.when(place.line < place.length - 1)(
                    lambda: copy(which, Z_UP, *args, place.up, arrival=first).start()
                )
            if upward is None or not upward:
                pl.when(place.line > 0)(
                    lambda: copy(which, Z_DOWN, *args, place.down, arrival=first).start()
                )
            copy(which, ACROSS, *args, place.across, arrival=first).start()
            copy(which, ALONG, *args, place.along, arrival=first).start()
            copy(which, SHARE, *args, place.partner, arrival=first).start()

        place.at_distance(distance, visit)

    def by_side(which, distance):
        halves = both(which)

        def visit(line, upward):
            copy(which, ACROSS, place.across_row, line, place.across).wait_recv()
            copy(which, HALF_ALONG, place.across_row, line, place.along, halves[1]).start()
            copy(which, SHARE + 1, place.across_row, line, place.partner).start()
            copy(which, ALONG, place.along_row, line, place.along).wait_recv()
            copy(which, HALF_ACROSS, place.along_row, line, place.across, halves[0]).start()
            copy(which, SHARE + 2, place.along_row, line, place.partner).start()

        place.at_distance(distance, visit)

    def by_corner(which, distance):
        halves = both(which)

        def visit(line, upward):
            copy(which, HALF_ACROSS, place.corner_row, line, place.across, halves[0]).wait_recv()
            copy(which, SHARE + 3, place.corner_row, line, place.partner, halves[0]).start()
            copy(which, HALF_ALONG, place.corner_row, line, place.along, halves[1]).wait_recv()
            copy(which, SHARE + 4, place.corner_row, line, place.partner, halves[1]).start()

        place.at_distance(distance, visit)

    def from_partner(which):
        halves = both(which)
        for distance in range(place.length):

            def visit(line, upward):
                mine = place.other_core
                for kind, row, part in (
                    (0, place.row, None), (1, place.across_row, None), (2, place.along_row, None),
                    (3, place.corner_row, halves[0]), (4, place.corner_row, halves[1]),
                ):
                    copy(which, SHARE + kind, row, line, place.partner, part, mine=mine).wait_recv()

            place.at_distance(distance, visit)

    def drain(which):
        halves = both(which)
        for distance in range(place.length):

            def visit(line, upward):
                args = (place.row, line)
                first = True if upward is None else None
                if upward is None or upward:
                    pl.when(place.line < place.length - 1)(
                        lambda: copy(which, Z_UP, *args, place.up, arrival=first).wait_send()
                    )
                if upward is None or not upward:
                    pl.when(place.line > 0)(
                        lambda: copy(which, Z_DOWN, *args, place.down, arrival=first).wait_send()
                    )
                copy(which, ACROSS, *args, place.across, arrival=first).wait_send()
                copy(which, ALONG, *args, place.along, arrival=first).wait_send()
                copy(which, SHARE, *args, place.partner, arrival=first).wait_send()
                copy(which, HALF_ALONG, place.across_row, line, place.along, halves[1]).wait_send()
                copy(which, HALF_ACROSS, place.along_row, line, place.across, halves[0]).wait_send()
                copy(which, SHARE + 1, place.across_row, line, place.partner).wait_send()
                copy(which, SHARE + 2, place.along_row, line, place.partner).wait_send()
                copy(which, SHARE + 3, place.corner_row, line, place.partner, halves[0]).wait_send()
                copy(which, SHARE + 4, place.corner_row, line, place.partner, halves[1]).wait_send()

            place.at_distance(distance, visit)

    length = place.length
    finish = length + 2
    for step in range(finish + 4):
        for which in range(3):
            distance = step - 2 * which
            if 0 <= distance < length:
                by_line(which, distance)
            if 1 <= distance < length + 1:
                by_side(which, distance - 1)
            if 2 <= distance < length + 2:
                by_corner(which, distance - 2)
        if step == finish:
            from_partner(0)
            keeps[0].wait()
            outs = (wq, wk, wv, wo)
            for col in range(cols):
                for at, out in enumerate(outs):
                    out[across * col : across * col + across, :] = jnp.concatenate(
                        [
                            gathered[row * cols + col, :across, depth * at : depth * at + depth]
                            for row in range(rows)
                        ],
                        axis=1,
                    )
            lines = [gathered[col, across:, :across].astype(F32) for col in range(cols)]
            table = jnp.concatenate(lines, axis=1)
            for at in range(8):
                vectors[at][...] = table[at : at + 1]
            vectors[8][...] = jnp.concatenate(
                [line[8 + at : 9 + at] for line in lines for at in range(upper.shape[1] // across)], axis=1
            )
    for which in range(1, 3):
        from_partner(which)
        keeps[which].wait()
    for which in range(3):
        drain(which)


def pack_kernel(wq, wk, wv, wo, wd, vectors, square, lower):
    across, depth = wq.shape[1], wq.shape[0]
    square[:across, :] = jnp.concatenate(
        [item[...].astype(F32).T for item in (wq, wk, wv, wo)], axis=1
    ).astype(BF16)
    square[across:, :] = jnp.zeros((LINES, square.shape[1]), BF16)
    square[across : across + LINES, :128] = vectors[...]
    lower[...] = wd[...].astype(F32).T.astype(BF16)


def fetch_by_kernel(arguments):
    matrices, vectors = arguments[:6], arguments[6:]
    rows, cols = lax.axis_size("row"), lax.axis_size("col")
    depth, across = matrices[0].shape
    width = depth * rows
    units = matrices[4].shape[1] * cols
    table = jnp.stack([*vectors[:5], *vectors[6:]])
    table = jnp.concatenate([table, vectors[5].reshape(-1, across)], axis=0)
    table = jnp.pad(table, ((0, LINES - table.shape[0]), (0, 128 - across)))
    shape = jax.ShapeDtypeStruct
    square, lower = pl.pallas_call(
        pack_kernel,
        out_shape=[shape((across + LINES, 4 * depth), BF16), shape((across, matrices[5].shape[0]), BF16)],
        in_specs=[pl.BlockSpec(memory_space=pltpu.VMEM)] * 6,
        out_specs=[pl.BlockSpec(memory_space=pltpu.VMEM)] * 2,
        name="pack",
    )(*matrices[:4], matrices[5], table)
    anywhere, local = pl.BlockSpec(memory_space=pl.ANY), pl.BlockSpec(memory_space=pltpu.VMEM)
    kinds = (3, SHARE + 5, cols // 2)
    vector = shape((1, width), F32)
    names = ("q", "k", "v", "o", "vq", "vv", "vo", "ag", "as", "vd", "og", "os", "vu", "u", "d")
    whole_arrays = pl.pallas_call(
        gather_kernel,
        out_shape=[shape((width, width), BF16)] * 4 + [vector] * 8 + [shape((1, units), F32)]
        + [shape((width, units), BF16), shape((width, units), BF16)],
        in_specs=[anywhere] * 3,
        out_specs=[local] * 13 + [anywhere] * 2,
        scratch_shapes=[
            pltpu.VMEM((rows * cols, across + LINES, 4 * depth), BF16),
            pltpu.SemaphoreType.DMA(kinds), pltpu.SemaphoreType.DMA(kinds), pltpu.SemaphoreType.DMA((3,)),
        ],
        compiler_params=pltpu.CompilerParams(
            collective_id=0, has_side_effects=True, vmem_limit_bytes=58 * 1024 * 1024
        ),
        name="gather",
    )(square, matrices[4], lower)
    return dict(zip(names, whole_arrays))


def joined(first, second):
    return jnp.concatenate([first, second], axis=0)


def product_kernel(left1, left2, right1, right2, out, turned):
    @pl.when(pl.program_id(0) == 0)
    def _():
        turned[...] = joined(left1[...], left2[...]).T

    out[...] = nn(turned[...], joined(right1[...], right2[...])).astype(BF16)


def product_t(left1, left2, right1, right2):
    width, units = left1.shape[1], right1.shape[1]
    block = pl.BlockSpec((ROWS, UNITS), lambda i: (0, i))
    return pl.pallas_call(
        product_kernel,
        grid=(units // UNITS,),
        in_specs=[whole((ROWS, width))] * 2 + [block] * 2,
        out_specs=pl.BlockSpec((width, UNITS), lambda i: (0, i)),
        out_shape=jax.ShapeDtypeStruct((width, units), BF16),
        scratch_shapes=[pltpu.VMEM((width, 2 * ROWS), BF16)],
        compiler_params=params(),
        name="weight_gradient",
    )(left1, left2, right1, right2)


SUM_ROWS = (5, 3, 4, 2, 0, 1)


class Scatter:
    def __init__(self, square, upper, lower, outs, scratch):
        self.square, self.upper, self.lower, self.outs = square, upper, lower, outs
        held, self.theirs, self.corner, self.side, self.lined = (
            scratch[:2], scratch[2:5], scratch[5:8], scratch[8:11], scratch[11:14]
        )
        self.held = (None, *held)
        self.send, self.recv, self.own = scratch[14:]
        self.cols = square.shape[0] // ROWS_MESH
        self.place = Place(self.cols)
        self.length = self.place.length
        self.stages = self.length + 3

    def source(self, which, row, col):
        count, wide = self.outs[which].shape
        if which == 0:
            return self.square.at[row * self.cols + col]
        array, high, level = (self.upper, row, col) if which == 1 else (self.lower, col, row)
        return array.at[
            pl.ds(pl.multiple_of(high * count, 16), count),
            pl.ds(pl.multiple_of(level * wide, 128), wide),
        ]

    def mine(self, which, row, line, part=None):
        if which == 0:
            array, at = self.square, row * self.cols + 2 * line + self.place.core
        else:
            array, at = self.held[which], row * self.length + line
        return array.at[at] if part is None else array.at[at, pl.ds(*part)]

    def load(self, which, row, line):
        at = row * self.length + line
        return pltpu.make_async_copy(
            self.source(which, row, 2 * line + self.place.core),
            self.held[which].at[at], self.own.at[which - 1, at],
        )

    def remote(self, which, kind, line, here, there, device):
        return pltpu.make_async_remote_copy(
            src_ref=here, dst_ref=there,
            send_sem=self.send.at[which, kind, line], recv_sem=self.recv.at[which, kind, line],
            device_id=device, device_id_type=MESH_IDS,
        )

    def share(self, which, row, line, core):
        here = self.source(which, row, 2 * line + core)
        there = self.theirs[which].at[row * self.length + line]
        return self.remote(which, SHARE + row, line, here, there, self.place.partner)

    def corner_copy(self, which, kind, line):
        part = splits(self.outs[which].shape[0])[kind - HALF_ACROSS]
        here = self.mine(which, self.place.corner_row, line, part)
        there = self.corner[which].at[line, pl.ds(*part)]
        device = self.place.across if kind == HALF_ACROSS else self.place.along
        return self.remote(which, kind, line, here, there, device)

    def side_copy(self, which, kind, line):
        place = self.place
        row, device = (place.across_row, place.across) if kind == ACROSS else (place.along_row, place.along)
        there = self.side[which].at[kind - ACROSS, line]
        return self.remote(which, kind, line, self.mine(which, row, line), there, device)

    def line_copy(self, which, kind, line):
        device = self.place.up if kind == Z_UP else self.place.down
        here = self.mine(which, self.place.row, line)
        return self.remote(which, kind, line, here, self.lined[which].at[kind, line], device)

    def add(self, block, arrived):
        block[...] = (block[...].astype(F32) + arrived[...].astype(F32)).astype(BF16)

    def begin(self, which):
        place = self.place
        for distance in range(self.length - 1, -1, -1):

            def visit(line, downward):
                for row in (place.corner_row, place.across_row, place.along_row, place.row):
                    if which:
                        self.load(which, row, line).start()
                    self.share(which, row, line, place.other_core).start()

            place.at_distance(distance, visit)

    def merge(self, which, row, line):
        if which:
            self.load(which, row, line).wait()
        self.share(which, row, line, self.place.core).wait_recv()
        self.add(self.mine(which, row, line), self.theirs[which].at[row * self.length + line])

    def cores(self, which, distance):
        place = self.place

        def visit(line, downward):
            self.merge(which, place.corner_row, line)
            self.merge(which, place.across_row, line)
            self.corner_copy(which, HALF_ACROSS, line).start()
            self.corner_copy(which, HALF_ALONG, line).start()
            self.merge(which, place.along_row, line)
            self.merge(which, place.row, line)

        place.at_distance(distance, visit)

    def corners(self, which, distance):
        place = self.place
        first, second = splits(self.outs[which].shape[0])

        def visit(line, downward):
            for kind, row, part in (
                (HALF_ACROSS, place.along_row, first), (HALF_ALONG, place.across_row, second)
            ):
                self.corner_copy(which, kind, line).wait_recv()
                self.add(self.mine(which, row, line, part), self.corner[which].at[line, pl.ds(*part)])
            self.side_copy(which, ALONG, line).start()
            self.side_copy(which, ACROSS, line).start()

        place.at_distance(distance, visit)

    def sides(self, which, distance):
        def visit(line, downward):
            for kind in (ACROSS, ALONG):
                self.side_copy(which, kind, line).wait_recv()
                self.add(self.mine(which, self.place.row, line), self.side[which].at[kind - ACROSS, line])

        self.place.at_distance(distance, visit)

    def lines(self, which, distance):
        place = self.place

        def visit(line, downward):
            kind = Z_DOWN if downward else Z_UP
            onward = place.line < self.length - 1 if downward else place.line > 0

            @pl.when(onward)
            def _():
                self.line_copy(which, kind, line).wait_recv()
                self.add(self.mine(which, place.row, line), self.lined[which].at[kind, line])

            self.line_copy(which, kind, line).start()

        place.at_distance(distance, visit)

    def result(self, which):
        place = self.place
        block = self.mine(which, place.row, place.line)
        for kind, there in ((Z_UP, place.line > 0), (Z_DOWN, place.line < self.length - 1)):

            @pl.when(there)
            def _():
                self.line_copy(which, kind, place.line).wait_recv()
                self.add(block, self.lined[which].at[kind, place.line])

        self.outs[which][...] = block[...].astype(F32)

    def stage(self, which, stage):
        length = self.length
        if 0 <= stage < length:
            self.cores(which, length - 1 - stage)
        if 1 <= stage < length + 1:
            self.corners(which, length - stage)
        if 2 <= stage < length + 2:
            self.sides(which, length + 1 - stage)
        if 3 <= stage < length + 2:
            self.lines(which, length + 2 - stage)
        if stage == length + 2:
            self.result(which)

    def drain(self, which):
        for distance in range(self.length):

            def visit(line, downward):
                for row in range(ROWS_MESH):
                    self.share(which, row, line, self.place.other_core).wait_send()
                for kind in (HALF_ACROSS, HALF_ALONG):
                    self.corner_copy(which, kind, line).wait_send()
                for kind in (ACROSS, ALONG):
                    self.side_copy(which, kind, line).wait_send()
                if downward is not None:
                    self.line_copy(which, Z_DOWN if downward else Z_UP, line).wait_send()

            self.place.at_distance(distance, visit)


PAIRS = QUAD // 128


def last_backward_kernel(
    q, k, v, e, last, total, mixed, gm, dfirst, wq, wk, wv,
    gq2, gk2, gv2, gb1, gb2, x1, x2, mixed1, mixed2, vq2, vv2, sums1, sums2, vu1, vu2, upper, lower,
    dx_out, square_out, upper_out, lower_out,
    k_pad, v_pad, gq, gk, gv, vq, vv, totals, blocks, *scratch,
):
    step = pl.program_id(0)
    quads = gq.shape[0]
    travel = Scatter(blocks, upper, lower, (square_out, upper_out, lower_out), scratch)
    moves = [(which, at - 2 * which + 2) for at in range(travel.stages + 2) for which in (1, 2)]
    moves = [(which, stage) for which, stage in moves if 0 <= stage < travel.stages]
    slots = quads * PAIRS + 4

    def advance(slot):
        for which, stage in moves[len(moves) * slot // slots : len(moves) * (slot + 1) // slots]:
            travel.stage(which, stage)

    @pl.when(step == 0)
    def _():
        travel.place.greet()
        travel.begin(1)
        travel.begin(2)
        dx_out[...] = dfirst[...]
        k_pad[...] = jnp.zeros_like(k_pad)
        v_pad[...] = jnp.zeros_like(v_pad)

    @pl.when(step < quads)
    def _():
        outs = gq.at[step], gk.at[step], gv.at[step]
        k_pad[:ROWS, :] = k[...]
        v_pad[:ROWS, :] = v[...]
        for pair in range(PAIRS):
            backward_pair(pair, step, q, e, last, total, mixed, gm, k_pad, v_pad, *outs)
            for at in range(quads):
                pl.when(step == at)(functools.partial(advance, at * PAIRS + pair))
        vq[step] = column_sum(outs[0][...].astype(F32))
        vv[step] = column_sum(outs[2][...].astype(F32))
        dx_out[...] += nn(outs[0][...], wq[...]) + nn(outs[1][...], wk[...]) + nn(outs[2][...], wv[...])

    @pl.when(step == quads)
    def _():
        rows, cols = ROWS_MESH, travel.cols
        width = blocks.shape[2]
        across, depth = width // cols, width // rows
        inputs = joined(x1[...], x2[...])
        for at, (first, second) in enumerate(((gq, gq2), (gk, gk2), (gv, gv2))):
            for quad in range(quads):
                part = slice(QUAD * quad, QUAD * quad + QUAD)
                totals[at, part, :] = nn(joined(first[quad], second[:, part]).T, inputs).astype(BF16)
            advance(quads * PAIRS + at)
        totals[3] = nn(joined(gb1[...], gb2[...]).T, joined(mixed1[...], mixed2[...])).astype(BF16)
        sums = sums1[...] + sums2[...]
        wide = vu1[...] + vu2[...]
        vectors = jnp.concatenate(
            [
                jnp.concatenate([vq[quad] for quad in range(quads)], axis=1) + vq2[...],
                jnp.concatenate([vv[quad] for quad in range(quads)], axis=1) + vv2[...],
            ]
            + [sums[at : at + 1] for at in SUM_ROWS],
            axis=0,
        )
        share = wide.shape[1] // cols // across
        for col in range(cols):
            begin = across * col
            narrow = jnp.concatenate(
                [vectors[:, begin : begin + across]]
                + [wide[:, across * (col * share + at) : across * (col * share + at + 1)] for at in range(share)]
                + [jnp.zeros((LINES - 8 - share, across), F32)],
                axis=0,
            )
            narrow = jnp.pad(narrow, ((0, 0), (0, width - across))).astype(BF16)
            for row in range(rows):
                block = row * cols + col
                blocks[block, :across, :] = jnp.concatenate(
                    [totals[at, begin : begin + across, depth * row : depth * row + depth] for at in range(4)],
                    axis=1,
                )
                blocks[block, across:, :] = narrow
        travel.begin(0)
        advance(slots - 1)
        for stage in range(travel.stages):
            travel.stage(0, stage)
        for which in range(3):
            travel.drain(which)


def last_backward(saved1, saved2, gm, dfirst, weights, grads1, grads2, upper, lower, cols):
    width = dfirst.shape[1]
    quads = width // QUAD
    length = cols // 2
    across, depth = width // cols, width // ROWS_MESH
    units = upper.shape[1]
    sizes = ((across + LINES, width), (depth, units // cols), (across, units // ROWS_MESH))
    kinds = (3, SHARE + ROWS_MESH, length)

    def once(array):
        return pl.BlockSpec(array.shape, lambda i: (0,) * array.ndim, pipeline_mode=pl.Buffered(1))

    def turn(i):
        return jnp.minimum(i, quads - 1)

    rows_block = pl.BlockSpec((ROWS, QUAD), lambda i: (0, turn(i)))
    row_block = pl.BlockSpec((QUAD, width), lambda i: (turn(i), 0))
    anywhere = pl.BlockSpec(memory_space=pl.ANY)
    singles = (
        grads2["gq"], grads2["gk"], grads2["gv"], grads1["gb"], grads2["gb"], saved1["x"], saved2["x"],
        saved1["mixed"], saved2["mixed"], grads2["vq"], grads2["vv"],
        grads1["sums"], grads2["sums"], grads1["vu"], grads2["vu"],
    )
    buffers = [
        pltpu.VMEM((*lead, *size), BF16)
        for lead in ((ROWS_MESH * length,), (ROWS_MESH * length,), (length,), (2, length), (2, length))
        for size in sizes
    ][1:]
    shape = jax.ShapeDtypeStruct
    return pl.pallas_call(
        last_backward_kernel,
        grid=(quads + 1,),
        in_specs=[
            rows_block, rows_block, rows_block,
            pl.BlockSpec((4, ROWS, MAIN), lambda i: (turn(i), 0, 0)),
            pl.BlockSpec((4, ROWS - MAIN, LAST), lambda i: (turn(i), 0, 0)),
            once(saved1["total"]), rows_block, rows_block, once(dfirst), row_block, row_block, row_block,
            *(once(item) for item in singles), anywhere, anywhere,
        ],
        out_specs=[whole((ROWS, width)), *(whole(size) for size in sizes)],
        out_shape=[shape((ROWS, width), F32), *(shape(size, F32) for size in sizes)],
        scratch_shapes=[
            pltpu.VMEM((KEYS, QUAD), BF16), pltpu.VMEM((KEYS, QUAD), BF16),
            *[pltpu.VMEM((quads, ROWS, QUAD), BF16)] * 3, *[pltpu.VMEM((quads, 1, QUAD), F32)] * 2,
            pltpu.VMEM((4, width, width), BF16),
            pltpu.VMEM((ROWS_MESH * cols, *sizes[0]), BF16),
            *buffers,
            pltpu.SemaphoreType.DMA(kinds), pltpu.SemaphoreType.DMA(kinds),
            pltpu.SemaphoreType.DMA((2, ROWS_MESH * length)),
        ],
        compiler_params=pltpu.CompilerParams(
            dimension_semantics=("arbitrary",), collective_id=1, has_side_effects=True,
            vmem_limit_bytes=63 * 1024 * 1024,
        ),
        name="last_backward",
    )(
        saved1["q"], saved1["k"], saved1["v"], saved1["e"], saved1["last"], saved1["total"], saved1["mixed"],
        gm, dfirst, weights["q"], weights["k"], weights["v"], *singles, upper, lower,
    )


def gather_all(part):
    return lax.all_gather(part, ("row", "col"), axis=0, tiled=False)


def fetch(arguments):
    matrices, vectors = arguments[:6], arguments[6:]
    rows, cols = lax.axis_size("row"), lax.axis_size("col")
    depth, across = matrices[0].shape
    width = depth * rows
    names = ("q", "k", "v", "o")
    square = jnp.concatenate([item.T for item in matrices[:4]], axis=1)
    upper = matrices[4].T.reshape(4, across, depth).transpose(1, 0, 2).reshape(across, 4 * depth)
    lower = matrices[5].T
    line = jnp.concatenate(vectors)
    extra = -(-line.shape[0] // (4 * depth))
    extra += -(across + extra) % 16
    line = jnp.pad(line, (0, extra * 4 * depth - line.shape[0])).reshape(extra, 4 * depth)
    first = gather_all(jnp.concatenate([square, line], axis=0))
    second = gather_all(upper)
    third = gather_all(lower)
    whole_square = (
        first[:, :across].reshape(rows, cols, across, 4, depth)
        .transpose(3, 1, 2, 0, 4).reshape(4, width, width)
    )
    weights = {name: whole_square[at] for at, name in enumerate(names)}
    weights["u"] = (
        second.reshape(rows, cols, across, 4, depth)
        .transpose(0, 4, 1, 3, 2).reshape(width, 4 * width)
    )
    weights["d"] = third.reshape(rows, cols, across, 4 * depth).transpose(1, 2, 0, 3).reshape(width, 4 * width)
    lines = first[:cols, across:].reshape(cols, -1).astype(F32)
    at = 0
    for name, item in zip(("vq", "vv", "vo", "ag", "as", "vu", "vd", "og", "os"), vectors):
        weights[name] = lines[:, at : at + item.shape[0]].reshape(1, -1)
        at += item.shape[0]
    return weights


def scatter_all(terms):
    return lax.psum_scatter(terms, ("row", "col"), scatter_dimension=0, tiled=False)


def scatter(square, upper, lower, lines):
    rows, cols = lax.axis_size("row"), lax.axis_size("col")
    width = square.shape[1]
    depth, across = width // rows, width // cols
    square = square.reshape(4, cols, across, rows, depth).transpose(3, 1, 2, 0, 4)
    square = square.reshape(rows, cols, across, 4 * depth)
    count = lines.shape[1]
    extra = -(-count // (4 * depth))
    extra += -(across + extra) % 16
    lines = jnp.pad(lines, ((0, 0), (0, extra * 4 * depth - count))).astype(BF16)
    lines = jnp.broadcast_to(lines.reshape(1, cols, extra, 4 * depth), (rows, cols, extra, 4 * depth))
    square = jnp.concatenate([square, lines], axis=2)
    square = scatter_all(square.reshape(rows * cols, across + extra, 4 * depth)).astype(F32)
    upper = upper.reshape(rows, depth, cols, 4 * across).transpose(0, 2, 1, 3)
    upper = scatter_all(upper.reshape(rows * cols, depth, 4 * across)).astype(F32)
    lower = lower.reshape(cols, across, rows, 4 * depth).transpose(2, 0, 1, 3)
    lower = scatter_all(lower.reshape(rows * cols, across, 4 * depth)).astype(F32)
    return square[:across], upper, lower, square[across:].reshape(-1)[:count]


def solution_body(
    text, memory, tail_lengths, picture_starts, grad_out, *parameters
):
    rows, cols = lax.axis_size("row"), lax.axis_size("col")
    depth, across = parameters[0].shape
    width = depth * rows
    by_kernel = rows == ROWS_MESH and cols % 2 == 0 and depth % 32 == 0 and across % 32 == 0
    by_kernel = by_kernel and 4 * across % 128 == 0
    weights = fetch_by_kernel(parameters) if by_kernel else fetch(parameters)
    words = jnp.pad(text[0].astype(F32), ((0, 0), (MEMORY, ROWS - MEMORY - TEXT), (0, 0)))

    def forward(segment, edge):
        q, k, v, e, last, total, mixed, hidden, normed1, inverse1, xb, hb = attention_forward(
            segment, tail_lengths, picture_starts, words, edge, weights
        )
        act, slope, y, edge, normed2, inverse2 = feed_forward(hidden, hb, weights)
        saved = dict(
            x=xb, q=q, k=k, v=v, e=e, last=last, total=total, mixed=mixed, hidden=hb,
            normed1=normed1, inverse1=inverse1, act=act, slope=slope, normed2=normed2, inverse2=inverse2,
        )
        return y, edge, saved

    def paired(first, second, begin, count):
        which = lax.broadcasted_iota(jnp.int32, (count, 2, width), 1)
        first, second = (item[begin : begin + count, None, :] for item in (first, second))
        return jnp.where(which == 0, first, second).astype(BF16).transpose(1, 0, 2)[None]

    y1, edge1, saved1 = forward(0, memory[0])
    y2, edge2, saved2 = forward(1, edge1)
    layer_output = paired(y1, y2, 0, SEG_ROWS)

    def feed(segment, later, saved):
        gd, gu, gb, dfirst, gm, vu, sums = feed_backward(segment, cotangent, later, saved, weights)
        return gm, dfirst, dict(gd=gd, gu=gu, gb=gb, vu=vu, sums=sums)

    def attend(saved, gm, dfirst):
        gq, gk, gv, dx, vq, vv = attention_backward(saved, gm, dfirst, weights)
        return dx, dict(gq=gq, gk=gk, gv=gv, vq=vq, vv=vv)

    cotangent = jnp.pad(grad_out[0].astype(F32), ((0, 0), (0, ROWS - SEG_ROWS), (0, 0)))
    gm2, dfirst2, grads2 = feed(1, saved2["normed2"], saved2)
    dx2, more = attend(saved2, gm2, dfirst2)
    grads2.update(more)
    gm1, dfirst1, grads1 = feed(0, dx2, saved1)
    upper = product_t(saved1["hidden"], saved2["hidden"], grads1["gu"], grads2["gu"])
    lower = product_t(grads1["gd"], grads2["gd"], saved1["act"], saved2["act"])
    if by_kernel:
        dx1, square, upper, lower = last_backward(
            saved1, saved2, gm1, dfirst1, weights, grads1, grads2, upper, lower, cols
        )
        table = square[across : across + LINES, :across]
        square = square[:across]
        lines = [table[at] for at in range(8)]
        lines.insert(5, table[8 : 8 + upper.shape[1] // across].reshape(-1))
    else:
        dx1, more = attend(saved1, gm1, dfirst1)
        grads1.update(more)
        square = jnp.stack(
            [
                product_t(grads1["gq"], grads2["gq"], saved1["x"], saved2["x"]),
                product_t(grads1["gk"], grads2["gk"], saved1["x"], saved2["x"]),
                product_t(grads1["gv"], grads2["gv"], saved1["x"], saved2["x"]),
                product_t(grads1["gb"], grads2["gb"], saved1["mixed"], saved2["mixed"]),
            ]
        )
        sums = grads1["sums"] + grads2["sums"]
        wide = grads1["vu"] + grads2["vu"]
        parts = (grads1["vq"] + grads2["vq"], grads1["vv"] + grads2["vv"])
        vectors = jnp.concatenate([*parts, *(sums[at : at + 1] for at in SUM_ROWS)], axis=0)
        table = jnp.concatenate(
            [vectors.reshape(8, cols, across).transpose(1, 0, 2).reshape(cols, -1), wide.reshape(cols, -1)],
            axis=1,
        )
        square, upper, lower, line = scatter(square, upper, lower, table)
        lines = [line[at * across : at * across + across] for at in range(8)]
        lines.insert(5, line[8 * across :])
    memory_grad = (dx1[:MEMORY] + dx1[MEMORY + TEXT : SEG_ROWS]).astype(BF16)[None]
    text_grad = paired(dx1, dx2, MEMORY, TEXT)
    own = square.reshape(across, 4, depth)
    result = [own[:, at].T for at in range(4)] + [upper, lower.T]
    return (layer_output, text_grad, memory_grad, *result, *lines)


def solution(mesh):
    batch, matrix, vector = P(("row", "col")), P("row", "col"), P("col")
    return jax.shard_map(
        solution_body,
        mesh=mesh,
        in_specs=(batch,) * 5 + (matrix,) * 6 + (vector,) * 9,
        out_specs=(batch,) * 3 + (matrix,) * 6 + (vector,) * 9,
        check_vma=False,
    )
```

```python
import functools

import jax
import jax.numpy as jnp
from jax import lax
from jax.experimental import pallas as pl
from jax.experimental.pallas import tpu as pltpu
from jax.sharding import PartitionSpec as P

HEADS = 12
HEAD_DIM = 64
MEMORY = 10
TEXT = 502
PICTURE = 256
SEG_ROWS = 522
ROWS = 528
MAIN = 512
LAST = 128
KEYS = MAIN + LAST
QUAD = 256
UNITS = 512
F32 = jnp.float32
BF16 = jnp.bfloat16

EPSILON = 1e-06
MASKED = -1e30
LOG2E = 1.4426950408889634

ERFC_SLOPE = 0.4 * 0.7071067811865476
ERFC_POLY = (0.22562816739082336, 0.2265406847000122, 0.20122945308685303, 0.19582846760749817, 0.07433333992958069, 0.09543049335479736, 0.07776277512311935, -0.1374378800392151, 0.040684547275304794)


def nn(left, right):
    return lax.dot_general(left, right, (((1,), (0,)), ((), ())), preferred_element_type=F32)


def nt(left, right):
    return lax.dot_general(left, right, (((1,), (1,)), ((), ())), preferred_element_type=F32)


def norm_forward(inputs, gain, shift):
    center = jnp.mean(inputs, axis=-1, keepdims=True)
    centred = inputs - center
    spread = jnp.mean(centred * centred, axis=-1, keepdims=True)
    inverse = lax.rsqrt(spread + EPSILON)
    normed = centred * inverse
    return normed * gain + shift, normed, inverse


def norm_backward(grad, normed, inverse, gain):
    scaled = grad * gain
    first = jnp.mean(scaled, axis=-1, keepdims=True)
    second = jnp.mean(scaled * normed, axis=-1, keepdims=True)
    return (scaled - first - normed * second) * inverse


def column_sum(values):
    return jnp.sum(values, axis=0, keepdims=True)


def gelu_pair(upward):
    size = jnp.abs(upward)
    t = 1.0 / (1.0 + ERFC_SLOPE * size)
    poly = jnp.full_like(t, ERFC_POLY[-1])
    for coefficient in ERFC_POLY[-2::-1]:
        poly = poly * t + coefficient
    bell = jnp.exp2(upward * upward * (-0.5 * LOG2E))
    tail = 0.5 * bell * t * poly
    phi = jnp.where(upward < 0.0, tail, 1.0 - tail)
    return upward * phi, phi + upward * (bell * 0.3989422804014327)


def plus_last(values, last):
    return jnp.concatenate([values[:MAIN], values[MAIN:] + last], axis=0)


def attention_forward_kernel(
    segment, tails, starts, words, edge, wq, wk, wv, wo, vq, vv, vo, gain, shift,
    q_out, k_out, v_out, e_out, last_out, total_out, mixed_out, hidden_out, normed_out, inverse_out,
    narrow, narrow_hidden, x, bias, last_bias, k_pad, v_pad, branch,
):
    step = pl.program_id(0)

    @pl.when(step == 0)
    def _():
        x[...] = words[0]
        x[:MEMORY, :] = edge[:MEMORY, :].astype(F32)
        x[MEMORY + TEXT : SEG_ROWS, :] = edge[:MEMORY, :].astype(F32)
        narrow[...] = x[...].astype(BF16)
        branch[...] = jnp.zeros_like(branch)
        total_out[...] = jnp.ones_like(total_out)
        k_pad[...] = jnp.zeros_like(k_pad)
        v_pad[...] = jnp.zeros_like(v_pad)
        length = TEXT if segment == 0 else tails[0]
        start = starts[0, segment]
        low, high = start + MEMORY, start + MEMORY + PICTURE
        row = lax.broadcasted_iota(jnp.int32, (ROWS, MAIN), 0)
        col = lax.broadcasted_iota(jnp.int32, (ROWS, MAIN), 1)
        usable = (col < MEMORY) | (col < MEMORY + length)
        inside = (row >= low) & (row < high) & (col >= low) & (col < high)
        bias[...] = jnp.where(usable & ((col <= row) | inside), 0.0, MASKED)
        row = lax.broadcasted_iota(jnp.int32, (ROWS - MAIN, LAST), 0)
        col = lax.broadcasted_iota(jnp.int32, (ROWS - MAIN, LAST), 1)
        last_bias[...] = jnp.where((col < SEG_ROWS - MAIN) & (col <= row), 0.0, MASKED)

    xb = narrow[...]
    q = ((nt(xb, wq[...]) + vq[...]).astype(BF16).astype(F32) * HEAD_DIM**-0.5).astype(BF16)
    q_out[...] = q
    k_pad[:ROWS, :] = nt(xb, wk[...]).astype(BF16)
    v_pad[:ROWS, :] = (nt(xb, wv[...]) + vv[...]).astype(BF16)
    k_out[...] = k_pad[:ROWS, :]
    v_out[...] = v_pad[:ROWS, :]
    lane = lax.broadcasted_iota(jnp.int32, (ROWS, 128), 1)
    totals = total_out[...]
    for pair in range(2):
        at = slice(128 * pair, 128 * pair + 128)
        halves = []
        for half in range(2):
            mine = (lane < HEAD_DIM) if half == 0 else (lane >= HEAD_DIM)
            qm = jnp.where(mine, q_out[:, at], jnp.zeros((), BF16))
            scores = nt(qm, k_pad[:MAIN, at]) + bias[...]
            last = nt(qm[MAIN:], k_pad[MAIN:, at]) + last_bias[...]
            peak = jnp.max(scores, axis=-1, keepdims=True)
            last_peak = jnp.maximum(peak[MAIN:], jnp.max(last, axis=-1, keepdims=True))
            peak = jnp.concatenate([peak[:MAIN], last_peak], axis=0)
            expos = jnp.exp2((scores - peak) * LOG2E)
            last = jnp.exp2((last - last_peak) * LOG2E)
            total = plus_last(jnp.sum(expos, axis=-1, keepdims=True), jnp.sum(last, axis=-1, keepdims=True))
            narrow_e, last = expos.astype(BF16), last.astype(BF16)
            e_out[2 * pair + half] = narrow_e
            last_out[2 * pair + half] = last
            weighted = plus_last(nn(narrow_e, v_pad[:MAIN, at]), nn(last, v_pad[MAIN:, at]))
            totals = jnp.where(lane == step * 4 + 2 * pair + half, total, totals)
            halves.append(weighted / total)
        mixed_out[:, at] = jnp.where(lane < HEAD_DIM, halves[0], halves[1]).astype(BF16)
    total_out[...] = totals
    branch[...] += nt(mixed_out[...], wo[...])

    @pl.when(step == pl.num_programs(0) - 1)
    def _():
        hidden, normed, inverse = norm_forward(
            x[...] + (branch[...] + vo[...]), gain[...], shift[...]
        )
        hidden_out[...] = hidden
        narrow_hidden[...] = hidden.astype(BF16)
        normed_out[...] = normed
        inverse_out[...] = jnp.broadcast_to(inverse, inverse_out.shape)


def whole(shape):
    return pl.BlockSpec(shape, lambda i: (0,) * len(shape))


def params(limit=58):
    return pltpu.CompilerParams(
        dimension_semantics=("arbitrary",), vmem_limit_bytes=limit * 1024 * 1024
    )


def attention_forward(segment, tails, starts, words, edge, weights):
    width = words.shape[2]
    steps = width // QUAD
    row_block = pl.BlockSpec((QUAD, width), lambda i: (i, 0))
    col_block = pl.BlockSpec((width, QUAD), lambda i: (0, i))
    bias_block = pl.BlockSpec((1, QUAD), lambda i: (0, i))
    rows_block = pl.BlockSpec((ROWS, QUAD), lambda i: (0, i))
    vector = whole((1, width))
    full = whole((ROWS, width))
    stats = whole((ROWS, 128))
    shape = jax.ShapeDtypeStruct
    return pl.pallas_call(
        functools.partial(attention_forward_kernel, segment),
        grid=(steps,),
        in_specs=[
            pl.BlockSpec(memory_space=pltpu.SMEM), pl.BlockSpec(memory_space=pltpu.SMEM),
            pl.BlockSpec((1, ROWS, width), lambda i: (segment, 0, 0)), whole(edge.shape), row_block, row_block, row_block, col_block,
            bias_block, bias_block, vector, vector, vector,
        ],
        out_specs=[
            rows_block, rows_block, rows_block,
            pl.BlockSpec((4, ROWS, MAIN), lambda i: (i, 0, 0)),
            pl.BlockSpec((4, ROWS - MAIN, LAST), lambda i: (i, 0, 0)),
            stats, rows_block, full, full, stats, full, full,
        ],
        out_shape=[
            shape((ROWS, width), BF16), shape((ROWS, width), BF16), shape((ROWS, width), BF16),
            shape((HEADS, ROWS, MAIN), BF16), shape((HEADS, ROWS - MAIN, LAST), BF16),
            shape((ROWS, 128), F32), shape((ROWS, width), BF16),
            shape((ROWS, width), F32), shape((ROWS, width), F32), shape((ROWS, 128), F32),
            shape((ROWS, width), BF16), shape((ROWS, width), BF16),
        ],
        scratch_shapes=[
            pltpu.VMEM((ROWS, width), F32),
            pltpu.VMEM((ROWS, MAIN), F32),
            pltpu.VMEM((ROWS - MAIN, LAST), F32),
            pltpu.VMEM((KEYS, QUAD), BF16),
            pltpu.VMEM((KEYS, QUAD), BF16),
            pltpu.VMEM((ROWS, width), F32),
        ],
        compiler_params=params(),
        name="attention_forward",
    )(
        tails, starts, words, edge, weights["q"], weights["k"], weights["v"], weights["o"],
        weights["vq"], weights["vv"], weights["vo"], weights["ag"], weights["as"],
    )


def feed_forward_kernel(
    hidden, narrow, wu, wd, vu, vd, gain, shift, act_out, slope_out, y_out, edge_out, normed_out, inverse_out,
    total,
):
    step = pl.program_id(0)

    @pl.when(step == 0)
    def _():
        total[...] = jnp.zeros_like(total)

    upward = nn(narrow[...], wu[...]) + vu[...]
    act, slope = gelu_pair(upward)
    act_out[...] = act.astype(BF16)
    slope_out[...] = slope.astype(BF16)
    total[...] += nt(act_out[...], wd[...])

    @pl.when(step == pl.num_programs(0) - 1)
    def _():
        y, normed, inverse = norm_forward(
            hidden[...] + (total[...] + vd[...]), gain[...], shift[...]
        )
        y_out[...] = y.astype(BF16)
        edge_out[...] = y[MEMORY + TEXT :, :]
        normed_out[...] = normed
        inverse_out[...] = jnp.broadcast_to(inverse, inverse_out.shape)


def feed_forward(hidden, narrow, weights):
    width = hidden.shape[1]
    units = weights["u"].shape[1]
    vector = whole((1, width))
    full = whole((ROWS, width))
    block = pl.BlockSpec((ROWS, UNITS), lambda i: (0, i))
    shape = jax.ShapeDtypeStruct
    return pl.pallas_call(
        feed_forward_kernel,
        grid=(units // UNITS,),
        in_specs=[
            full, full,
            pl.BlockSpec((width, UNITS), lambda i: (0, i)),
            pl.BlockSpec((width, UNITS), lambda i: (0, i)),
            pl.BlockSpec((1, UNITS), lambda i: (0, i)),
            vector, vector, vector,
        ],
        out_specs=[block, block, full, whole((ROWS - MEMORY - TEXT, width)), full, whole((ROWS, 128))],
        out_shape=[
            shape((ROWS, units), BF16), shape((ROWS, units), BF16), shape((ROWS, width), BF16),
            shape((ROWS - MEMORY - TEXT, width), F32), shape((ROWS, width), F32), shape((ROWS, 128), F32),
        ],
        scratch_shapes=[pltpu.VMEM((ROWS, width), F32)],
        compiler_params=params(),
        name="feed_forward",
    )(
        hidden, narrow, weights["u"], weights["d"], weights["vu"], weights["vd"],
        weights["og"], weights["os"],
    )


def feed_backward_kernel(
    segment, dy, top, bottom, normed2, inverse2, normed1, inverse1, slope, wd, wu, wo, gain2, gain1,
    gd_out, gu_out, gb_out, dfirst_out, gm_out, vu_out, sums_out,
    dsecond, dhidden,
):
    step = pl.program_id(0)

    @pl.when(step == 0)
    def _():
        dsecond[...] = dy[0]
        if segment == 0:
            dsecond[MEMORY + TEXT : SEG_ROWS, :] += top[:MEMORY, :] + bottom[:MEMORY, :]
        grad, normed = dsecond[...], normed2[...]
        sums_out[0:1, :] = column_sum(grad * normed)
        sums_out[1:2, :] = column_sum(grad)
        second = norm_backward(grad, normed, inverse2[:, 0:1], gain2[...])
        dsecond[...] = second
        narrow = second.astype(BF16)
        gd_out[...] = narrow
        sums_out[2:3, :] = column_sum(narrow.astype(F32))
        dhidden[...] = jnp.zeros_like(dhidden)

    up = (nn(gd_out[...], wd[...]) * slope[...].astype(F32)).astype(BF16)
    gu_out[...] = up
    vu_out[...] = column_sum(up.astype(F32))
    dhidden[...] += nt(up, wu[...])

    @pl.when(step == pl.num_programs(0) - 1)
    def _():
        grad, normed = dhidden[...] + dsecond[...], normed1[...]
        sums_out[3:4, :] = column_sum(grad * normed)
        sums_out[4:5, :] = column_sum(grad)
        first = norm_backward(grad, normed, inverse1[:, 0:1], gain1[...])
        dfirst_out[...] = first
        narrow = first.astype(BF16)
        gb_out[...] = narrow
        sums_out[5:6, :] = column_sum(narrow.astype(F32))
        sums_out[6:8, :] = jnp.zeros((2, narrow.shape[1]), F32)
        gm_out[...] = nn(narrow, wo[...]).astype(BF16)


def feed_backward(segment, dy, later, saved, weights):
    width = dy.shape[2]
    edges = ROWS - MEMORY - TEXT
    units = weights["u"].shape[1]
    vector = whole((1, width))
    full = whole((ROWS, width))
    stats = whole((ROWS, 128))
    block = pl.BlockSpec((ROWS, UNITS), lambda i: (0, i))
    shape = jax.ShapeDtypeStruct
    return pl.pallas_call(
        functools.partial(feed_backward_kernel, segment),
        grid=(units // UNITS,),
        in_specs=[
            pl.BlockSpec((1, ROWS, width), lambda i: (segment, 0, 0)),
            pl.BlockSpec((edges, width), lambda i: (0, 0)),
            pl.BlockSpec((edges, width), lambda i: ((MEMORY + TEXT) // edges, 0)),
            full, stats, full, stats, block,
            pl.BlockSpec((width, UNITS), lambda i: (0, i)),
            pl.BlockSpec((width, UNITS), lambda i: (0, i)),
            whole((width, width)), vector, vector,
        ],
        out_specs=[
            full, block, full, full, full,
            pl.BlockSpec((1, UNITS), lambda i: (0, i)), whole((8, width)),
        ],
        out_shape=[
            shape((ROWS, width), BF16), shape((ROWS, units), BF16), shape((ROWS, width), BF16),
            shape((ROWS, width), F32), shape((ROWS, width), BF16),
            shape((1, units), F32), shape((8, width), F32),
        ],
        scratch_shapes=[pltpu.VMEM((ROWS, width), F32), pltpu.VMEM((ROWS, width), F32)],
        compiler_params=params(),
        name="feed_backward",
    )(
        dy, later, later, saved["normed2"], saved["inverse2"], saved["normed1"], saved["inverse1"],
        saved["slope"], weights["d"], weights["u"], weights["o"], weights["og"], weights["ag"],
    )


def backward_pair(pair, step, q, e, last, total, mixed, gm, k_pad, v_pad, gq_out, gk_out, gv_out):
    lane = lax.broadcasted_iota(jnp.int32, (ROWS, 128), 1)
    at = slice(128 * pair, 128 * pair + 128)
    grad = gm[:, at].astype(F32)
    product = grad * mixed[:, at].astype(F32)
    totals = total[...]
    rates, inners = [], []
    for half in range(2):
        mine = (lane < HEAD_DIM) if half == 0 else (lane >= HEAD_DIM)
        head = step * 4 + 2 * pair + half
        rate = 1.0 / jnp.sum(jnp.where(lane == head, totals, 0.0), axis=-1, keepdims=True)
        rates.append(rate)
        inners.append(jnp.sum(jnp.where(mine, product, 0.0), axis=-1, keepdims=True) * rate)
    scaled = (grad * jnp.where(lane < HEAD_DIM, rates[0], rates[1])).astype(BF16)
    scaled_t = scaled.T
    query_t = q[:, at].T
    gq, gk, gv = [], [], []
    for half in range(2):
        mine = (lane < HEAD_DIM) if half == 0 else (lane >= HEAD_DIM)
        rows = slice(HEAD_DIM * half, HEAD_DIM * half + HEAD_DIM)
        inner = inners[half]
        gmm = jnp.where(mine, scaled, jnp.zeros((), BF16))
        dp = nt(gmm, v_pad[:MAIN, at])
        last_dp = nt(gmm[MAIN:], v_pad[MAIN:, at])
        narrow_e, narrow_last = e[2 * pair + half], last[2 * pair + half]
        ds = (narrow_e.astype(F32) * (dp - inner)).astype(BF16)
        last_ds = (narrow_last.astype(F32) * (last_dp - inner[MAIN:])).astype(BF16)
        gq.append(plus_last(nn(ds, k_pad[:MAIN, at]), nn(last_ds, k_pad[MAIN:, at])))
        gk.append(jnp.concatenate([nn(query_t[rows, :], ds), nn(query_t[rows, MAIN:], last_ds)], axis=1))
        gv.append(
            jnp.concatenate([nn(scaled_t[rows, :], narrow_e), nn(scaled_t[rows, MAIN:], narrow_last)], axis=1)
        )
    gq_pair = jnp.where(lane < HEAD_DIM, gq[0], gq[1]) * HEAD_DIM**-0.5
    gq_out[:, at] = gq_pair.astype(BF16)
    gk_out[:, at] = jnp.concatenate(gk, axis=0).T[:ROWS].astype(BF16)
    gv_out[:, at] = jnp.concatenate(gv, axis=0).T[:ROWS].astype(BF16)


def attention_backward_kernel(
    q, k, v, e, last, total, mixed, gm, dfirst, wq, wk, wv,
    gq_out, gk_out, gv_out, dx_out, vq_out, vv_out,
    k_pad, v_pad,
):
    step = pl.program_id(0)

    @pl.when(step == 0)
    def _():
        dx_out[...] = dfirst[...]
        k_pad[...] = jnp.zeros_like(k_pad)
        v_pad[...] = jnp.zeros_like(v_pad)

    k_pad[:ROWS, :] = k[...]
    v_pad[:ROWS, :] = v[...]
    for pair in range(2):
        backward_pair(pair, step, q, e, last, total, mixed, gm, k_pad, v_pad, gq_out, gk_out, gv_out)
    vq_out[...] = column_sum(gq_out[...].astype(F32))
    vv_out[...] = column_sum(gv_out[...].astype(F32))
    dx_out[...] += (
        nn(gq_out[...], wq[...]) + nn(gk_out[...], wk[...]) + nn(gv_out[...], wv[...])
    )


def attention_backward(saved, gm, dfirst, weights):
    width = dfirst.shape[1]
    row_block = pl.BlockSpec((QUAD, width), lambda i: (i, 0))
    rows_block = pl.BlockSpec((ROWS, QUAD), lambda i: (0, i))
    full = whole((ROWS, width))
    sums = pl.BlockSpec((1, QUAD), lambda i: (0, i))
    shape = jax.ShapeDtypeStruct
    return pl.pallas_call(
        attention_backward_kernel,
        grid=(width // QUAD,),
        in_specs=[
            rows_block, rows_block, rows_block,
            pl.BlockSpec((4, ROWS, MAIN), lambda i: (i, 0, 0)),
            pl.BlockSpec((4, ROWS - MAIN, LAST), lambda i: (i, 0, 0)),
            whole((ROWS, 128)), rows_block, rows_block, full, row_block, row_block, row_block,
        ],
        out_specs=[rows_block, rows_block, rows_block, full, sums, sums],
        out_shape=[
            shape((ROWS, width), BF16), shape((ROWS, width), BF16), shape((ROWS, width), BF16),
            shape((ROWS, width), F32), shape((1, width), F32), shape((1, width), F32),
        ],
        scratch_shapes=[pltpu.VMEM((KEYS, QUAD), BF16), pltpu.VMEM((KEYS, QUAD), BF16)],
        compiler_params=params(),
        name="attention_backward",
    )(
        saved["q"], saved["k"], saved["v"], saved["e"], saved["last"], saved["total"], saved["mixed"],
        gm, dfirst, weights["q"], weights["k"], weights["v"],
    )


ROWS_MESH = 4
LINES = 16
MESH_IDS = pl.DeviceIdType.MESH
Z_UP, Z_DOWN, ACROSS, ALONG, HALF_ACROSS, HALF_ALONG = range(6)
SHARE = 6


class Place:
    def __init__(self, cols):
        self.row, self.col = lax.axis_index("row"), lax.axis_index("col")
        self.length = cols // 2
        self.core = lax.rem(self.col, 2)
        self.line = lax.div(self.col, 2)
        self.across_row = self.row + 1 - 2 * lax.rem(self.row, 2)
        self.along_row = self.row + 2 - 4 * lax.div(self.row, 2)
        self.corner_row = 3 - self.row
        self.across = (self.across_row, self.col)
        self.along = (self.along_row, self.col)
        self.up = (self.row, self.col + 2)
        self.down = (self.row, self.col - 2)
        self.other_core = 1 - self.core
        self.partner = (self.row, self.col + 1 - 2 * self.core)

    def greet(self):
        barrier = pltpu.get_barrier_semaphore()

        def signal(device):
            pl.semaphore_signal(barrier, inc=1, device_id=device, device_id_type=MESH_IDS)

        signal(self.across)
        signal(self.along)
        signal(self.partner)
        pl.when(self.line > 0)(lambda: signal(self.down))
        pl.when(self.line < self.length - 1)(lambda: signal(self.up))
        has_down = lax.div(self.line + self.length - 1, self.length)
        has_up = lax.div(2 * self.length - 2 - self.line, self.length)
        pl.semaphore_wait(barrier, 3 + has_down + has_up)

    def at_distance(self, distance, visit):
        if distance == 0:
            visit(self.line, None)
        else:
            below, above = self.line - distance, self.line + distance
            pl.when(below >= 0)(lambda: visit(below, True))
            pl.when(above < self.length)(lambda: visit(above, False))


def splits(count):
    first = count // 32 * 16
    return ((0, first), (first, count - first))


def gather_kernel(
    square, upper, lower, wq, wk, wv, wo, *rest
):
    vectors, (whole_upper, whole_lower, gathered, send, recv, own) = rest[:9], rest[9:]
    rows, cols = ROWS_MESH, wq.shape[0] // lower.shape[0]
    place = Place(cols)
    depth, across = upper.shape[0], lower.shape[0]
    sources = (square, upper, lower)

    def target(which, row, col, part=None):
        if which == 0:
            view, count = gathered.at[row * cols + col], square.shape[0]
            begin, size = part if part else (0, count)
            return view.at[pl.ds(begin, size)]
        count, wide = sources[which].shape
        array, high, side = (whole_upper, row, col) if which == 1 else (whole_lower, col, row)
        begin, size = part if part else (0, count)
        return array.at[
            pl.ds(pl.multiple_of(high * count + begin, 16), size),
            pl.ds(pl.multiple_of(side * wide, 128), wide),
        ]

    def copy(which, kind, row, line, device, part=None, mine=None, arrival=None):
        col = 2 * line + (place.core if mine is None else mine)
        there = target(which, row, col, part)
        here = there if arrival is None else sources[which]
        return pltpu.make_async_remote_copy(
            src_ref=here, dst_ref=there,
            send_sem=send.at[which, kind, line], recv_sem=recv.at[which, kind, line],
            device_id=device, device_id_type=MESH_IDS,
        )

    place.greet()
    keeps = []
    for which in range(3):
        keep = pltpu.make_async_copy(
            sources[which], target(which, place.row, place.col), own.at[which]
        )
        keep.start()
        keeps.append(keep)

    def both(which):
        return splits(sources[which].shape[0])

    def by_line(which, distance):
        def visit(line, upward):
            first = True if upward is None else None
            args = (place.row, line)
            if upward is not None:
                kind = Z_UP if upward else Z_DOWN
                copy(which, kind, *args, place.down).wait_recv()
            if upward is None or upward:
                pl.when(place.line < place.length - 1)(
                    lambda: copy(which, Z_UP, *args, place.up, arrival=first).start()
                )
            if upward is None or not upward:
                pl.when(place.line > 0)(
                    lambda: copy(which, Z_DOWN, *args, place.down, arrival=first).start()
                )
            copy(which, ACROSS, *args, place.across, arrival=first).start()
            copy(which, ALONG, *args, place.along, arrival=first).start()
            copy(which, SHARE, *args, place.partner, arrival=first).start()

        place.at_distance(distance, visit)

    def by_side(which, distance):
        halves = both(which)

        def visit(line, upward):
            copy(which, ACROSS, place.across_row, line, place.across).wait_recv()
            copy(which, HALF_ALONG, place.across_row, line, place.along, halves[1]).start()
            copy(which, SHARE + 1, place.across_row, line, place.partner).start()
            copy(which, ALONG, place.along_row, line, place.along).wait_recv()
            copy(which, HALF_ACROSS, place.along_row, line, place.across, halves[0]).start()
            copy(which, SHARE + 2, place.along_row, line, place.partner).start()

        place.at_distance(distance, visit)

    def by_corner(which, distance):
        halves = both(which)

        def visit(line, upward):
            copy(which, HALF_ACROSS, place.corner_row, line, place.across, halves[0]).wait_recv()
            copy(which, SHARE + 3, place.corner_row, line, place.partner, halves[0]).start()
            copy(which, HALF_ALONG, place.corner_row, line, place.along, halves[1]).wait_recv()
            copy(which, SHARE + 4, place.corner_row, line, place.partner, halves[1]).start()

        place.at_distance(distance, visit)

    def from_partner(which):
        halves = both(which)
        for distance in range(place.length):

            def visit(line, upward):
                mine = place.other_core
                for kind, row, part in (
                    (0, place.row, None), (1, place.across_row, None), (2, place.along_row, None),
                    (3, place.corner_row, halves[0]), (4, place.corner_row, halves[1]),
                ):
                    copy(which, SHARE + kind, row, line, place.partner, part, mine=mine).wait_recv()

            place.at_distance(distance, visit)

    def drain(which):
        halves = both(which)
        for distance in range(place.length):

            def visit(line, upward):
                args = (place.row, line)
                first = True if upward is None else None
                if upward is None or upward:
                    pl.when(place.line < place.length - 1)(
                        lambda: copy(which, Z_UP, *args, place.up, arrival=first).wait_send()
                    )
                if upward is None or not upward:
                    pl.when(place.line > 0)(
                        lambda: copy(which, Z_DOWN, *args, place.down, arrival=first).wait_send()
                    )
                copy(which, ACROSS, *args, place.across, arrival=first).wait_send()
                copy(which, ALONG, *args, place.along, arrival=first).wait_send()
                copy(which, SHARE, *args, place.partner, arrival=first).wait_send()
                copy(which, HALF_ALONG, place.across_row, line, place.along, halves[1]).wait_send()
                copy(which, HALF_ACROSS, place.along_row, line, place.across, halves[0]).wait_send()
                copy(which, SHARE + 1, place.across_row, line, place.partner).wait_send()
                copy(which, SHARE + 2, place.along_row, line, place.partner).wait_send()
                copy(which, SHARE + 3, place.corner_row, line, place.partner, halves[0]).wait_send()
                copy(which, SHARE + 4, place.corner_row, line, place.partner, halves[1]).wait_send()

            place.at_distance(distance, visit)

    length = place.length
    finish = length + 2
    for step in range(finish + 4):
        for which in range(3):
            distance = step - 2 * which
            if 0 <= distance < length:
                by_line(which, distance)
            if 1 <= distance < length + 1:
                by_side(which, distance - 1)
            if 2 <= distance < length + 2:
                by_corner(which, distance - 2)
        if step == finish:
            from_partner(0)
            keeps[0].wait()
            outs = (wq, wk, wv, wo)
            for col in range(cols):
                for at, out in enumerate(outs):
                    out[across * col : across * col + across, :] = jnp.concatenate(
                        [
                            gathered[row * cols + col, :across, depth * at : depth * at + depth]
                            for row in range(rows)
                        ],
                        axis=1,
                    )
            lines = [gathered[col, across:, :across].astype(F32) for col in range(cols)]
            table = jnp.concatenate(lines, axis=1)
            for at in range(8):
                vectors[at][...] = table[at : at + 1]
            vectors[8][...] = jnp.concatenate(
                [line[8 + at : 9 + at] for line in lines for at in range(upper.shape[1] // across)], axis=1
            )
    for which in range(1, 3):
        from_partner(which)
        keeps[which].wait()
    for which in range(3):
        drain(which)


def pack_kernel(wq, wk, wv, wo, wd, vectors, square, lower):
    across, depth = wq.shape[1], wq.shape[0]
    square[:across, :] = jnp.concatenate(
        [item[...].astype(F32).T for item in (wq, wk, wv, wo)], axis=1
    ).astype(BF16)
    square[across:, :] = jnp.zeros((LINES, square.shape[1]), BF16)
    square[across : across + LINES, :128] = vectors[...]
    lower[...] = wd[...].astype(F32).T.astype(BF16)


def fetch_by_kernel(arguments):
    matrices, vectors = arguments[:6], arguments[6:]
    rows, cols = lax.axis_size("row"), lax.axis_size("col")
    depth, across = matrices[0].shape
    width = depth * rows
    units = matrices[4].shape[1] * cols
    table = jnp.stack([*vectors[:5], *vectors[6:]])
    table = jnp.concatenate([table, vectors[5].reshape(-1, across)], axis=0)
    table = jnp.pad(table, ((0, LINES - table.shape[0]), (0, 128 - across)))
    shape = jax.ShapeDtypeStruct
    square, lower = pl.pallas_call(
        pack_kernel,
        out_shape=[shape((across + LINES, 4 * depth), BF16), shape((across, matrices[5].shape[0]), BF16)],
        in_specs=[pl.BlockSpec(memory_space=pltpu.VMEM)] * 6,
        out_specs=[pl.BlockSpec(memory_space=pltpu.VMEM)] * 2,
        name="pack",
    )(*matrices[:4], matrices[5], table)
    anywhere, local = pl.BlockSpec(memory_space=pl.ANY), pl.BlockSpec(memory_space=pltpu.VMEM)
    kinds = (3, SHARE + 5, cols // 2)
    vector = shape((1, width), F32)
    names = ("q", "k", "v", "o", "vq", "vv", "vo", "ag", "as", "vd", "og", "os", "vu", "u", "d")
    whole_arrays = pl.pallas_call(
        gather_kernel,
        out_shape=[shape((width, width), BF16)] * 4 + [vector] * 8 + [shape((1, units), F32)]
        + [shape((width, units), BF16), shape((width, units), BF16)],
        in_specs=[anywhere] * 3,
        out_specs=[local] * 13 + [anywhere] * 2,
        scratch_shapes=[
            pltpu.VMEM((rows * cols, across + LINES, 4 * depth), BF16),
            pltpu.SemaphoreType.DMA(kinds), pltpu.SemaphoreType.DMA(kinds), pltpu.SemaphoreType.DMA((3,)),
        ],
        compiler_params=pltpu.CompilerParams(
            collective_id=0, has_side_effects=True, vmem_limit_bytes=58 * 1024 * 1024
        ),
        name="gather",
    )(square, matrices[4], lower)
    return dict(zip(names, whole_arrays))


def joined(first, second):
    return jnp.concatenate([first, second], axis=0)


def product_kernel(left1, left2, right1, right2, out, turned):
    @pl.when(pl.program_id(0) == 0)
    def _():
        turned[...] = joined(left1[...], left2[...]).T

    out[...] = nn(turned[...], joined(right1[...], right2[...])).astype(BF16)


def product_t(left1, left2, right1, right2):
    width, units = left1.shape[1], right1.shape[1]
    block = pl.BlockSpec((ROWS, UNITS), lambda i: (0, i))
    return pl.pallas_call(
        product_kernel,
        grid=(units // UNITS,),
        in_specs=[whole((ROWS, width))] * 2 + [block] * 2,
        out_specs=pl.BlockSpec((width, UNITS), lambda i: (0, i)),
        out_shape=jax.ShapeDtypeStruct((width, units), BF16),
        scratch_shapes=[pltpu.VMEM((width, 2 * ROWS), BF16)],
        compiler_params=params(),
        name="weight_gradient",
    )(left1, left2, right1, right2)


SUM_ROWS = (5, 3, 4, 2, 0, 1)


class Scatter:
    def __init__(self, square, upper, lower, outs, scratch):
        self.square, self.upper, self.lower, self.outs = square, upper, lower, outs
        held, self.theirs, self.corner, self.side, self.lined = (
            scratch[:2], scratch[2:5], scratch[5:8], scratch[8:11], scratch[11:14]
        )
        self.held = (None, *held)
        self.send, self.recv, self.own = scratch[14:]
        self.cols = square.shape[0] // ROWS_MESH
        self.place = Place(self.cols)
        self.length = self.place.length

    def source(self, which, row, col):
        count, wide = self.outs[which].shape
        if which == 0:
            return self.square.at[row * self.cols + col]
        array, high, level = (self.upper, row, col) if which == 1 else (self.lower, col, row)
        return array.at[
            pl.ds(pl.multiple_of(high * count, 16), count),
            pl.ds(pl.multiple_of(level * wide, 128), wide),
        ]

    def mine(self, which, row, line, part=None):
        if which == 0:
            array, at = self.square, row * self.cols + 2 * line + self.place.core
        else:
            array, at = self.held[which], row * self.length + line
        return array.at[at] if part is None else array.at[at, pl.ds(*part)]

    def load(self, which, row, line):
        at = row * self.length + line
        return pltpu.make_async_copy(
            self.source(which, row, 2 * line + self.place.core),
            self.held[which].at[at], self.own.at[which - 1, at],
        )

    def remote(self, which, kind, line, here, there, device):
        return pltpu.make_async_remote_copy(
            src_ref=here, dst_ref=there,
            send_sem=self.send.at[which, kind, line], recv_sem=self.recv.at[which, kind, line],
            device_id=device, device_id_type=MESH_IDS,
        )

    def share(self, which, row, line, core):
        here = self.source(which, row, 2 * line + core)
        there = self.theirs[which].at[row * self.length + line]
        return self.remote(which, SHARE + row, line, here, there, self.place.partner)

    def corner_copy(self, which, kind, line):
        part = splits(self.outs[which].shape[0])[kind - HALF_ACROSS]
        here = self.mine(which, self.place.corner_row, line, part)
        there = self.corner[which].at[line, pl.ds(*part)]
        device = self.place.across if kind == HALF_ACROSS else self.place.along
        return self.remote(which, kind, line, here, there, device)

    def side_copy(self, which, kind, line):
        place = self.place
        row, device = (place.across_row, place.across) if kind == ACROSS else (place.along_row, place.along)
        there = self.side[which].at[kind - ACROSS, line]
        return self.remote(which, kind, line, self.mine(which, row, line), there, device)

    def line_copy(self, which, kind, line):
        device = self.place.up if kind == Z_UP else self.place.down
        here = self.mine(which, self.place.row, line)
        return self.remote(which, kind, line, here, self.lined[which].at[kind, line], device)

    def add(self, block, arrived):
        block[...] = (block[...].astype(F32) + arrived[...].astype(F32)).astype(BF16)

    def begin(self, which):
        place = self.place
        for distance in range(self.length - 1, -1, -1):

            def visit(line, downward):
                for row in (place.corner_row, place.across_row, place.along_row, place.row):
                    if which:
                        self.load(which, row, line).start()
                    self.share(which, row, line, place.other_core).start()

            place.at_distance(distance, visit)

    def merge(self, which, row, line):
        if which:
            self.load(which, row, line).wait()
        self.share(which, row, line, self.place.core).wait_recv()
        self.add(self.mine(which, row, line), self.theirs[which].at[row * self.length + line])

    def cores(self, which, distance):
        place = self.place

        def visit(line, downward):
            self.merge(which, place.corner_row, line)
            self.merge(which, place.across_row, line)
            self.corner_copy(which, HALF_ACROSS, line).start()
            self.corner_copy(which, HALF_ALONG, line).start()
            self.merge(which, place.along_row, line)
            self.merge(which, place.row, line)

        place.at_distance(distance, visit)

    def corners(self, which, distance):
        place = self.place
        first, second = splits(self.outs[which].shape[0])

        def visit(line, downward):
            for kind, row, part in (
                (HALF_ACROSS, place.along_row, first), (HALF_ALONG, place.across_row, second)
            ):
                self.corner_copy(which, kind, line).wait_recv()
                self.add(self.mine(which, row, line, part), self.corner[which].at[line, pl.ds(*part)])
            self.side_copy(which, ALONG, line).start()
            self.side_copy(which, ACROSS, line).start()

        place.at_distance(distance, visit)

    def sides(self, which, distance):
        def visit(line, downward):
            for kind in (ACROSS, ALONG):
                self.side_copy(which, kind, line).wait_recv()
                self.add(self.mine(which, self.place.row, line), self.side[which].at[kind - ACROSS, line])

        self.place.at_distance(distance, visit)

    def lines(self, which, distance):
        place = self.place

        def visit(line, downward):
            kind = Z_DOWN if downward else Z_UP
            onward = place.line < self.length - 1 if downward else place.line > 0

            @pl.when(onward)
            def _():
                self.line_copy(which, kind, line).wait_recv()
                self.add(self.mine(which, place.row, line), self.lined[which].at[kind, line])

            self.line_copy(which, kind, line).start()

        place.at_distance(distance, visit)

    def result(self, which):
        place = self.place
        block = self.mine(which, place.row, place.line)
        for kind, there in ((Z_UP, place.line > 0), (Z_DOWN, place.line < self.length - 1)):

            @pl.when(there)
            def _():
                self.line_copy(which, kind, place.line).wait_recv()
                self.add(block, self.lined[which].at[kind, place.line])

        self.outs[which][...] = block[...].astype(F32)

    def all_cores(self, which):
        for distance in range(self.length - 1, -1, -1):
            self.cores(which, distance)

    def all_corners(self, which):
        for distance in range(self.length - 1, -1, -1):
            self.corners(which, distance)

    def step(self, which, at):
        if at < self.length:
            self.sides(which, self.length - 1 - at)
        if 1 <= at < self.length:
            self.lines(which, self.length - at)
        if at == self.length:
            self.result(which)

    def drain(self, which):
        for distance in range(self.length):

            def visit(line, downward):
                for row in range(ROWS_MESH):
                    self.share(which, row, line, self.place.other_core).wait_send()
                for kind in (HALF_ACROSS, HALF_ALONG):
                    self.corner_copy(which, kind, line).wait_send()
                for kind in (ACROSS, ALONG):
                    self.side_copy(which, kind, line).wait_send()
                if downward is not None:
                    self.line_copy(which, Z_DOWN if downward else Z_UP, line).wait_send()

            self.place.at_distance(distance, visit)


PAIRS = QUAD // 128


def last_backward_kernel(
    q, k, v, e, last, total, mixed, gm, dfirst, wq, wk, wv,
    gq2, gk2, gv2, gb1, gb2, x1, x2, mixed1, mixed2, vq2, vv2, sums1, sums2, vu1, vu2, upper, lower,
    dx_out, square_out, upper_out, lower_out,
    k_pad, v_pad, gq, gk, gv, vq, vv, totals, blocks, *scratch,
):
    step = pl.program_id(0)
    quads = gq.shape[0]
    travel = Scatter(blocks, upper, lower, (square_out, upper_out, lower_out), scratch)
    length = travel.length
    steps = [functools.partial(travel.step, which, at) for which in (1, 2) for at in range(length + 1)]
    early = {
        0: (functools.partial(travel.all_cores, 1),), 1: (functools.partial(travel.all_cores, 2),),
        2: (functools.partial(travel.all_corners, 1),), 4: (functools.partial(travel.all_corners, 2),),
    }
    taken = 0
    for slot in range(quads * PAIRS, quads * PAIRS + 3):
        early[slot], taken = (steps[taken],), taken + 1
    squares = [functools.partial(travel.all_cores, 0), functools.partial(travel.all_corners, 0)]
    squares += [functools.partial(travel.step, 0, at) for at in range(length + 1)]
    late = []
    while steps[taken:] or squares:
        late += steps[taken : taken + 2] if len(squares) > length else steps[taken : taken + 1]
        taken += 2 if len(squares) > length else 1
        late += squares[:1]
        squares = squares[1:]

    def advance(slot):
        for move in early.get(slot, ()):
            move()

    @pl.when(step == 0)
    def _():
        travel.place.greet()
        travel.begin(1)
        travel.begin(2)
        dx_out[...] = dfirst[...]
        k_pad[...] = jnp.zeros_like(k_pad)
        v_pad[...] = jnp.zeros_like(v_pad)

    @pl.when(step < quads)
    def _():
        outs = gq.at[step], gk.at[step], gv.at[step]
        k_pad[:ROWS, :] = k[...]
        v_pad[:ROWS, :] = v[...]
        for pair in range(PAIRS):
            backward_pair(pair, step, q, e, last, total, mixed, gm, k_pad, v_pad, *outs)
            for at in range(quads):
                pl.when(step == at)(functools.partial(advance, at * PAIRS + pair))
        vq[step] = column_sum(outs[0][...].astype(F32))
        vv[step] = column_sum(outs[2][...].astype(F32))
        dx_out[...] += nn(outs[0][...], wq[...]) + nn(outs[1][...], wk[...]) + nn(outs[2][...], wv[...])

    @pl.when(step == quads)
    def _():
        rows, cols = ROWS_MESH, travel.cols
        width = blocks.shape[2]
        across, depth = width // cols, width // rows
        inputs = joined(x1[...], x2[...])
        for at, (first, second) in enumerate(((gq, gq2), (gk, gk2), (gv, gv2))):
            for quad in range(quads):
                part = slice(QUAD * quad, QUAD * quad + QUAD)
                totals[at, part, :] = nn(joined(first[quad], second[:, part]).T, inputs).astype(BF16)
            advance(quads * PAIRS + at)
        totals[3] = nn(joined(gb1[...], gb2[...]).T, joined(mixed1[...], mixed2[...])).astype(BF16)
        sums = sums1[...] + sums2[...]
        wide = vu1[...] + vu2[...]
        vectors = jnp.concatenate(
            [
                jnp.concatenate([vq[quad] for quad in range(quads)], axis=1) + vq2[...],
                jnp.concatenate([vv[quad] for quad in range(quads)], axis=1) + vv2[...],
            ]
            + [sums[at : at + 1] for at in SUM_ROWS],
            axis=0,
        )
        share = wide.shape[1] // cols // across
        for col in range(cols):
            begin = across * col
            narrow = jnp.concatenate(
                [vectors[:, begin : begin + across]]
                + [wide[:, across * (col * share + at) : across * (col * share + at + 1)] for at in range(share)]
                + [jnp.zeros((LINES - 8 - share, across), F32)],
                axis=0,
            )
            narrow = jnp.pad(narrow, ((0, 0), (0, width - across))).astype(BF16)
            for row in range(rows):
                block = row * cols + col
                blocks[block, :across, :] = jnp.concatenate(
                    [totals[at, begin : begin + across, depth * row : depth * row + depth] for at in range(4)],
                    axis=1,
                )
                blocks[block, across:, :] = narrow
        travel.begin(0)
        for move in late:
            move()
        for which in range(3):
            travel.drain(which)


def last_backward(saved1, saved2, gm, dfirst, weights, grads1, grads2, upper, lower, cols):
    width = dfirst.shape[1]
    quads = width // QUAD
    length = cols // 2
    across, depth = width // cols, width // ROWS_MESH
    units = upper.shape[1]
    sizes = ((across + LINES, width), (depth, units // cols), (across, units // ROWS_MESH))
    kinds = (3, SHARE + ROWS_MESH, length)

    def once(array):
        return pl.BlockSpec(array.shape, lambda i: (0,) * array.ndim, pipeline_mode=pl.Buffered(1))

    def turn(i):
        return jnp.minimum(i, quads - 1)

    rows_block = pl.BlockSpec((ROWS, QUAD), lambda i: (0, turn(i)))
    row_block = pl.BlockSpec((QUAD, width), lambda i: (turn(i), 0))
    anywhere = pl.BlockSpec(memory_space=pl.ANY)
    singles = (
        grads2["gq"], grads2["gk"], grads2["gv"], grads1["gb"], grads2["gb"], saved1["x"], saved2["x"],
        saved1["mixed"], saved2["mixed"], grads2["vq"], grads2["vv"],
        grads1["sums"], grads2["sums"], grads1["vu"], grads2["vu"],
    )
    buffers = [
        pltpu.VMEM((*lead, *size), BF16)
        for lead in ((ROWS_MESH * length,), (ROWS_MESH * length,), (length,), (2, length), (2, length))
        for size in sizes
    ][1:]
    shape = jax.ShapeDtypeStruct
    return pl.pallas_call(
        last_backward_kernel,
        grid=(quads + 1,),
        in_specs=[
            rows_block, rows_block, rows_block,
            pl.BlockSpec((4, ROWS, MAIN), lambda i: (turn(i), 0, 0)),
            pl.BlockSpec((4, ROWS - MAIN, LAST), lambda i: (turn(i), 0, 0)),
            once(saved1["total"]), rows_block, rows_block, once(dfirst), row_block, row_block, row_block,
            *(once(item) for item in singles), anywhere, anywhere,
        ],
        out_specs=[whole((ROWS, width)), *(whole(size) for size in sizes)],
        out_shape=[shape((ROWS, width), F32), *(shape(size, F32) for size in sizes)],
        scratch_shapes=[
            pltpu.VMEM((KEYS, QUAD), BF16), pltpu.VMEM((KEYS, QUAD), BF16),
            *[pltpu.VMEM((quads, ROWS, QUAD), BF16)] * 3, *[pltpu.VMEM((quads, 1, QUAD), F32)] * 2,
            pltpu.VMEM((4, width, width), BF16),
            pltpu.VMEM((ROWS_MESH * cols, *sizes[0]), BF16),
            *buffers,
            pltpu.SemaphoreType.DMA(kinds), pltpu.SemaphoreType.DMA(kinds),
            pltpu.SemaphoreType.DMA((2, ROWS_MESH * length)),
        ],
        compiler_params=pltpu.CompilerParams(
            dimension_semantics=("arbitrary",), collective_id=1, has_side_effects=True,
            vmem_limit_bytes=63 * 1024 * 1024,
        ),
        name="last_backward",
    )(
        saved1["q"], saved1["k"], saved1["v"], saved1["e"], saved1["last"], saved1["total"], saved1["mixed"],
        gm, dfirst, weights["q"], weights["k"], weights["v"], *singles, upper, lower,
    )


def gather_all(part):
    return lax.all_gather(part, ("row", "col"), axis=0, tiled=False)


def fetch(arguments):
    matrices, vectors = arguments[:6], arguments[6:]
    rows, cols = lax.axis_size("row"), lax.axis_size("col")
    depth, across = matrices[0].shape
    width = depth * rows
    names = ("q", "k", "v", "o")
    square = jnp.concatenate([item.T for item in matrices[:4]], axis=1)
    upper = matrices[4].T.reshape(4, across, depth).transpose(1, 0, 2).reshape(across, 4 * depth)
    lower = matrices[5].T
    line = jnp.concatenate(vectors)
    extra = -(-line.shape[0] // (4 * depth))
    extra += -(across + extra) % 16
    line = jnp.pad(line, (0, extra * 4 * depth - line.shape[0])).reshape(extra, 4 * depth)
    first = gather_all(jnp.concatenate([square, line], axis=0))
    second = gather_all(upper)
    third = gather_all(lower)
    whole_square = (
        first[:, :across].reshape(rows, cols, across, 4, depth)
        .transpose(3, 1, 2, 0, 4).reshape(4, width, width)
    )
    weights = {name: whole_square[at] for at, name in enumerate(names)}
    weights["u"] = (
        second.reshape(rows, cols, across, 4, depth)
        .transpose(0, 4, 1, 3, 2).reshape(width, 4 * width)
    )
    weights["d"] = third.reshape(rows, cols, across, 4 * depth).transpose(1, 2, 0, 3).reshape(width, 4 * width)
    lines = first[:cols, across:].reshape(cols, -1).astype(F32)
    at = 0
    for name, item in zip(("vq", "vv", "vo", "ag", "as", "vu", "vd", "og", "os"), vectors):
        weights[name] = lines[:, at : at + item.shape[0]].reshape(1, -1)
        at += item.shape[0]
    return weights


def scatter_all(terms):
    return lax.psum_scatter(terms, ("row", "col"), scatter_dimension=0, tiled=False)


def scatter(square, upper, lower, lines):
    rows, cols = lax.axis_size("row"), lax.axis_size("col")
    width = square.shape[1]
    depth, across = width // rows, width // cols
    square = square.reshape(4, cols, across, rows, depth).transpose(3, 1, 2, 0, 4)
    square = square.reshape(rows, cols, across, 4 * depth)
    count = lines.shape[1]
    extra = -(-count // (4 * depth))
    extra += -(across + extra) % 16
    lines = jnp.pad(lines, ((0, 0), (0, extra * 4 * depth - count))).astype(BF16)
    lines = jnp.broadcast_to(lines.reshape(1, cols, extra, 4 * depth), (rows, cols, extra, 4 * depth))
    square = jnp.concatenate([square, lines], axis=2)
    square = scatter_all(square.reshape(rows * cols, across + extra, 4 * depth)).astype(F32)
    upper = upper.reshape(rows, depth, cols, 4 * across).transpose(0, 2, 1, 3)
    upper = scatter_all(upper.reshape(rows * cols, depth, 4 * across)).astype(F32)
    lower = lower.reshape(cols, across, rows, 4 * depth).transpose(2, 0, 1, 3)
    lower = scatter_all(lower.reshape(rows * cols, across, 4 * depth)).astype(F32)
    return square[:across], upper, lower, square[across:].reshape(-1)[:count]


def solution_body(
    text, memory, tail_lengths, picture_starts, grad_out, *parameters
):
    rows, cols = lax.axis_size("row"), lax.axis_size("col")
    depth, across = parameters[0].shape
    width = depth * rows
    by_kernel = rows == ROWS_MESH and cols % 2 == 0 and depth % 32 == 0 and across % 32 == 0
    by_kernel = by_kernel and 4 * across % 128 == 0
    weights = fetch_by_kernel(parameters) if by_kernel else fetch(parameters)
    words = jnp.pad(text[0].astype(F32), ((0, 0), (MEMORY, ROWS - MEMORY - TEXT), (0, 0)))

    def forward(segment, edge):
        q, k, v, e, last, total, mixed, hidden, normed1, inverse1, xb, hb = attention_forward(
            segment, tail_lengths, picture_starts, words, edge, weights
        )
        act, slope, y, edge, normed2, inverse2 = feed_forward(hidden, hb, weights)
        saved = dict(
            x=xb, q=q, k=k, v=v, e=e, last=last, total=total, mixed=mixed, hidden=hb,
            normed1=normed1, inverse1=inverse1, act=act, slope=slope, normed2=normed2, inverse2=inverse2,
        )
        return y, edge, saved

    def paired(first, second, begin, count):
        which = lax.broadcasted_iota(jnp.int32, (count, 2, width), 1)
        first, second = (item[begin : begin + count, None, :] for item in (first, second))
        return jnp.where(which == 0, first, second).astype(BF16).transpose(1, 0, 2)[None]

    y1, edge1, saved1 = forward(0, memory[0])
    y2, edge2, saved2 = forward(1, edge1)
    layer_output = paired(y1, y2, 0, SEG_ROWS)

    def feed(segment, later, saved):
        gd, gu, gb, dfirst, gm, vu, sums = feed_backward(segment, cotangent, later, saved, weights)
        return gm, dfirst, dict(gd=gd, gu=gu, gb=gb, vu=vu, sums=sums)

    def attend(saved, gm, dfirst):
        gq, gk, gv, dx, vq, vv = attention_backward(saved, gm, dfirst, weights)
        return dx, dict(gq=gq, gk=gk, gv=gv, vq=vq, vv=vv)

    cotangent = jnp.pad(grad_out[0].astype(F32), ((0, 0), (0, ROWS - SEG_ROWS), (0, 0)))
    gm2, dfirst2, grads2 = feed(1, saved2["normed2"], saved2)
    dx2, more = attend(saved2, gm2, dfirst2)
    grads2.update(more)
    gm1, dfirst1, grads1 = feed(0, dx2, saved1)
    upper = product_t(saved1["hidden"], saved2["hidden"], grads1["gu"], grads2["gu"])
    lower = product_t(grads1["gd"], grads2["gd"], saved1["act"], saved2["act"])
    if by_kernel:
        dx1, square, upper, lower = last_backward(
            saved1, saved2, gm1, dfirst1, weights, grads1, grads2, upper, lower, cols
        )
        table = square[across : across + LINES, :across]
        square = square[:across]
        lines = [table[at] for at in range(8)]
        lines.insert(5, table[8 : 8 + upper.shape[1] // across].reshape(-1))
    else:
        dx1, more = attend(saved1, gm1, dfirst1)
        grads1.update(more)
        square = jnp.stack(
            [
                product_t(grads1["gq"], grads2["gq"], saved1["x"], saved2["x"]),
                product_t(grads1["gk"], grads2["gk"], saved1["x"], saved2["x"]),
                product_t(grads1["gv"], grads2["gv"], saved1["x"], saved2["x"]),
                product_t(grads1["gb"], grads2["gb"], saved1["mixed"], saved2["mixed"]),
            ]
        )
        sums = grads1["sums"] + grads2["sums"]
        wide = grads1["vu"] + grads2["vu"]
        parts = (grads1["vq"] + grads2["vq"], grads1["vv"] + grads2["vv"])
        vectors = jnp.concatenate([*parts, *(sums[at : at + 1] for at in SUM_ROWS)], axis=0)
        table = jnp.concatenate(
            [vectors.reshape(8, cols, across).transpose(1, 0, 2).reshape(cols, -1), wide.reshape(cols, -1)],
            axis=1,
        )
        square, upper, lower, line = scatter(square, upper, lower, table)
        lines = [line[at * across : at * across + across] for at in range(8)]
        lines.insert(5, line[8 * across :])
    memory_grad = (dx1[:MEMORY] + dx1[MEMORY + TEXT : SEG_ROWS]).astype(BF16)[None]
    text_grad = paired(dx1, dx2, MEMORY, TEXT)
    own = square.reshape(across, 4, depth)
    result = [own[:, at].T for at in range(4)] + [upper, lower.T]
    return (layer_output, text_grad, memory_grad, *result, *lines)


def solution(mesh):
    batch, matrix, vector = P(("row", "col")), P("row", "col"), P("col")
    return jax.shard_map(
        solution_body,
        mesh=mesh,
        in_specs=(batch,) * 5 + (matrix,) * 6 + (vector,) * 9,
        out_specs=(batch,) * 3 + (matrix,) * 6 + (vector,) * 9,
        check_vma=False,
    )
```

```python
import functools

import jax
import jax.numpy as jnp
from jax import lax
from jax.experimental import pallas as pl
from jax.experimental.pallas import tpu as pltpu
from jax.sharding import PartitionSpec as P

HEADS = 12
HEAD_DIM = 64
MEMORY = 10
TEXT = 502
PICTURE = 256
SEG_ROWS = 522
ROWS = 528
MAIN = 512
LAST = 128
KEYS = MAIN + LAST
QUAD = 256
UNITS = 512
F32 = jnp.float32
BF16 = jnp.bfloat16

EPSILON = 1e-06
MASKED = -1e30
LOG2E = 1.4426950408889634

ERFC_SLOPE = 0.4 * 0.7071067811865476
ERFC_POLY = (0.22562816739082336, 0.2265406847000122, 0.20122945308685303, 0.19582846760749817, 0.07433333992958069, 0.09543049335479736, 0.07776277512311935, -0.1374378800392151, 0.040684547275304794)


def nn(left, right):
    return lax.dot_general(left, right, (((1,), (0,)), ((), ())), preferred_element_type=F32)


def nt(left, right):
    return lax.dot_general(left, right, (((1,), (1,)), ((), ())), preferred_element_type=F32)


def norm_forward(inputs, gain, shift):
    center = jnp.mean(inputs, axis=-1, keepdims=True)
    centred = inputs - center
    spread = jnp.mean(centred * centred, axis=-1, keepdims=True)
    inverse = lax.rsqrt(spread + EPSILON)
    normed = centred * inverse
    return normed * gain + shift, normed, inverse


def norm_backward(grad, normed, inverse, gain):
    scaled = grad * gain
    first = jnp.mean(scaled, axis=-1, keepdims=True)
    second = jnp.mean(scaled * normed, axis=-1, keepdims=True)
    return (scaled - first - normed * second) * inverse


def column_sum(values):
    return jnp.sum(values, axis=0, keepdims=True)


def gelu_pair(upward):
    size = jnp.abs(upward)
    t = 1.0 / (1.0 + ERFC_SLOPE * size)
    poly = jnp.full_like(t, ERFC_POLY[-1])
    for coefficient in ERFC_POLY[-2::-1]:
        poly = poly * t + coefficient
    bell = jnp.exp2(upward * upward * (-0.5 * LOG2E))
    tail = 0.5 * bell * t * poly
    phi = jnp.where(upward < 0.0, tail, 1.0 - tail)
    return upward * phi, phi + upward * (bell * 0.3989422804014327)


def plus_last(values, last):
    return jnp.concatenate([values[:MAIN], values[MAIN:] + last], axis=0)


def write_masks(length, start, bias, last_bias):
    low, high = start + MEMORY, start + MEMORY + PICTURE
    row = lax.broadcasted_iota(jnp.int32, (ROWS, MAIN), 0)
    col = lax.broadcasted_iota(jnp.int32, (ROWS, MAIN), 1)
    usable = (col < MEMORY) | (col < MEMORY + length)
    inside = (row >= low) & (row < high) & (col >= low) & (col < high)
    bias[...] = jnp.where(usable & ((col <= row) | inside), 0.0, MASKED)
    row = lax.broadcasted_iota(jnp.int32, (ROWS - MAIN, LAST), 0)
    col = lax.broadcasted_iota(jnp.int32, (ROWS - MAIN, LAST), 1)
    last_bias[...] = jnp.where((col < SEG_ROWS - MAIN) & (col <= row), 0.0, MASKED)


def forward_open(segment, tails, starts, words, edge, total_out, narrow, x, bias, last_bias, k_pad, v_pad, branch):
    x[...] = words[0]
    x[:MEMORY, :] = edge[:MEMORY, :].astype(F32)
    x[MEMORY + TEXT : SEG_ROWS, :] = edge[:MEMORY, :].astype(F32)
    narrow[...] = x[...].astype(BF16)
    branch[...] = jnp.zeros_like(branch)
    total_out[...] = jnp.ones_like(total_out)
    k_pad[...] = jnp.zeros_like(k_pad)
    v_pad[...] = jnp.zeros_like(v_pad)
    write_masks(TEXT if segment == 0 else tails[0], starts[0, segment], bias, last_bias)


def forward_project(narrow, wq, wk, wv, vq, vv, q_out, k_out, v_out, k_pad, v_pad):
    xb = narrow[...]
    q_out[...] = ((nt(xb, wq) + vq).astype(BF16).astype(F32) * HEAD_DIM**-0.5).astype(BF16)
    k_pad[:ROWS, :] = nt(xb, wk).astype(BF16)
    v_pad[:ROWS, :] = (nt(xb, wv) + vv).astype(BF16)
    k_out[...] = k_pad[:ROWS, :]
    v_out[...] = v_pad[:ROWS, :]


def forward_pair(pair, step, q, bias, last_bias, k_pad, v_pad, e_out, last_out, total_out, mixed_out):
    lane = lax.broadcasted_iota(jnp.int32, (ROWS, 128), 1)
    at = slice(128 * pair, 128 * pair + 128)
    totals = total_out[...]
    halves = []
    for half in range(2):
        mine = (lane < HEAD_DIM) if half == 0 else (lane >= HEAD_DIM)
        qm = jnp.where(mine, q[:, at], jnp.zeros((), BF16))
        scores = nt(qm, k_pad[:MAIN, at]) + bias[...]
        last = nt(qm[MAIN:], k_pad[MAIN:, at]) + last_bias[...]
        peak = jnp.max(scores, axis=-1, keepdims=True)
        last_peak = jnp.maximum(peak[MAIN:], jnp.max(last, axis=-1, keepdims=True))
        peak = jnp.concatenate([peak[:MAIN], last_peak], axis=0)
        expos = jnp.exp2((scores - peak) * LOG2E)
        last = jnp.exp2((last - last_peak) * LOG2E)
        total = plus_last(jnp.sum(expos, axis=-1, keepdims=True), jnp.sum(last, axis=-1, keepdims=True))
        narrow_e, last = expos.astype(BF16), last.astype(BF16)
        e_out[2 * pair + half] = narrow_e
        last_out[2 * pair + half] = last
        weighted = plus_last(nn(narrow_e, v_pad[:MAIN, at]), nn(last, v_pad[MAIN:, at]))
        totals = jnp.where(lane == step * 4 + 2 * pair + half, total, totals)
        halves.append(weighted / total)
    mixed_out[:, at] = jnp.where(lane < HEAD_DIM, halves[0], halves[1]).astype(BF16)
    total_out[...] = totals


def forward_close(x, branch, vo, gain, shift, hidden_out, normed_out, inverse_out, narrow_hidden):
    hidden, normed, inverse = norm_forward(x[...] + (branch[...] + vo), gain, shift)
    hidden_out[...] = hidden
    narrow_hidden[...] = hidden.astype(BF16)
    normed_out[...] = normed
    inverse_out[...] = jnp.broadcast_to(inverse, inverse_out.shape)


def attention_forward_kernel(
    segment, tails, starts, words, edge, wq, wk, wv, wo, vq, vv, vo, gain, shift,
    q_out, k_out, v_out, e_out, last_out, total_out, mixed_out, hidden_out, normed_out, inverse_out,
    narrow, narrow_hidden, x, bias, last_bias, k_pad, v_pad, branch,
):
    step = pl.program_id(0)

    @pl.when(step == 0)
    def _():
        forward_open(
            segment, tails, starts, words, edge, total_out, narrow, x, bias, last_bias, k_pad, v_pad, branch
        )

    forward_project(narrow, wq[...], wk[...], wv[...], vq[...], vv[...], q_out, k_out, v_out, k_pad, v_pad)
    for pair in range(2):
        forward_pair(pair, step, q_out, bias, last_bias, k_pad, v_pad, e_out, last_out, total_out, mixed_out)
    branch[...] += nt(mixed_out[...], wo[...])

    @pl.when(step == pl.num_programs(0) - 1)
    def _():
        forward_close(
            x, branch, vo[...], gain[...], shift[...], hidden_out, normed_out, inverse_out, narrow_hidden
        )


def whole(shape):
    return pl.BlockSpec(shape, lambda i: (0,) * len(shape))


def params(limit=58):
    return pltpu.CompilerParams(
        dimension_semantics=("arbitrary",), vmem_limit_bytes=limit * 1024 * 1024
    )


def attention_forward(segment, tails, starts, words, edge, weights):
    width = words.shape[2]
    steps = width // QUAD
    row_block = pl.BlockSpec((QUAD, width), lambda i: (i, 0))
    col_block = pl.BlockSpec((width, QUAD), lambda i: (0, i))
    bias_block = pl.BlockSpec((1, QUAD), lambda i: (0, i))
    rows_block = pl.BlockSpec((ROWS, QUAD), lambda i: (0, i))
    vector = whole((1, width))
    full = whole((ROWS, width))
    stats = whole((ROWS, 128))
    shape = jax.ShapeDtypeStruct
    return pl.pallas_call(
        functools.partial(attention_forward_kernel, segment),
        grid=(steps,),
        in_specs=[
            pl.BlockSpec(memory_space=pltpu.SMEM), pl.BlockSpec(memory_space=pltpu.SMEM),
            pl.BlockSpec((1, ROWS, width), lambda i: (segment, 0, 0)), whole(edge.shape), row_block, row_block, row_block, col_block,
            bias_block, bias_block, vector, vector, vector,
        ],
        out_specs=[
            rows_block, rows_block, rows_block,
            pl.BlockSpec((4, ROWS, MAIN), lambda i: (i, 0, 0)),
            pl.BlockSpec((4, ROWS - MAIN, LAST), lambda i: (i, 0, 0)),
            stats, rows_block, full, full, stats, full, full,
        ],
        out_shape=[
            shape((ROWS, width), BF16), shape((ROWS, width), BF16), shape((ROWS, width), BF16),
            shape((HEADS, ROWS, MAIN), BF16), shape((HEADS, ROWS - MAIN, LAST), BF16),
            shape((ROWS, 128), F32), shape((ROWS, width), BF16),
            shape((ROWS, width), F32), shape((ROWS, width), F32), shape((ROWS, 128), F32),
            shape((ROWS, width), BF16), shape((ROWS, width), BF16),
        ],
        scratch_shapes=[
            pltpu.VMEM((ROWS, width), F32),
            pltpu.VMEM((ROWS, MAIN), F32),
            pltpu.VMEM((ROWS - MAIN, LAST), F32),
            pltpu.VMEM((KEYS, QUAD), BF16),
            pltpu.VMEM((KEYS, QUAD), BF16),
            pltpu.VMEM((ROWS, width), F32),
        ],
        compiler_params=params(),
        name="attention_forward",
    )(
        tails, starts, words, edge, weights["q"], weights["k"], weights["v"], weights["o"],
        weights["vq"], weights["vv"], weights["vo"], weights["ag"], weights["as"],
    )


def feed_forward_kernel(
    hidden, narrow, wu, wd, vu, vd, gain, shift, act_out, slope_out, y_out, edge_out, normed_out, inverse_out,
    total,
):
    step = pl.program_id(0)

    @pl.when(step == 0)
    def _():
        total[...] = jnp.zeros_like(total)

    upward = nn(narrow[...], wu[...]) + vu[...]
    act, slope = gelu_pair(upward)
    act_out[...] = act.astype(BF16)
    slope_out[...] = slope.astype(BF16)
    total[...] += nt(act_out[...], wd[...])

    @pl.when(step == pl.num_programs(0) - 1)
    def _():
        y, normed, inverse = norm_forward(
            hidden[...] + (total[...] + vd[...]), gain[...], shift[...]
        )
        y_out[...] = y.astype(BF16)
        edge_out[...] = y[MEMORY + TEXT :, :]
        normed_out[...] = normed
        inverse_out[...] = jnp.broadcast_to(inverse, inverse_out.shape)


def feed_forward(hidden, narrow, weights):
    width = hidden.shape[1]
    units = weights["u"].shape[1]
    vector = whole((1, width))
    full = whole((ROWS, width))
    block = pl.BlockSpec((ROWS, UNITS), lambda i: (0, i))
    shape = jax.ShapeDtypeStruct
    return pl.pallas_call(
        feed_forward_kernel,
        grid=(units // UNITS,),
        in_specs=[
            full, full,
            pl.BlockSpec((width, UNITS), lambda i: (0, i)),
            pl.BlockSpec((width, UNITS), lambda i: (0, i)),
            pl.BlockSpec((1, UNITS), lambda i: (0, i)),
            vector, vector, vector,
        ],
        out_specs=[block, block, full, whole((ROWS - MEMORY - TEXT, width)), full, whole((ROWS, 128))],
        out_shape=[
            shape((ROWS, units), BF16), shape((ROWS, units), BF16), shape((ROWS, width), BF16),
            shape((ROWS - MEMORY - TEXT, width), F32), shape((ROWS, width), F32), shape((ROWS, 128), F32),
        ],
        scratch_shapes=[pltpu.VMEM((ROWS, width), F32)],
        compiler_params=params(),
        name="feed_forward",
    )(
        hidden, narrow, weights["u"], weights["d"], weights["vu"], weights["vd"],
        weights["og"], weights["os"],
    )


def feed_backward_kernel(
    segment, dy, top, bottom, normed2, inverse2, normed1, inverse1, slope, wd, wu, wo, gain2, gain1,
    gd_out, gu_out, gb_out, dfirst_out, gm_out, vu_out, sums_out,
    dsecond, dhidden,
):
    step = pl.program_id(0)

    @pl.when(step == 0)
    def _():
        dsecond[...] = dy[0]
        if segment == 0:
            dsecond[MEMORY + TEXT : SEG_ROWS, :] += top[:MEMORY, :] + bottom[:MEMORY, :]
        grad, normed = dsecond[...], normed2[...]
        sums_out[0:1, :] = column_sum(grad * normed)
        sums_out[1:2, :] = column_sum(grad)
        second = norm_backward(grad, normed, inverse2[:, 0:1], gain2[...])
        dsecond[...] = second
        narrow = second.astype(BF16)
        gd_out[...] = narrow
        sums_out[2:3, :] = column_sum(narrow.astype(F32))
        dhidden[...] = jnp.zeros_like(dhidden)

    up = (nn(gd_out[...], wd[...]) * slope[...].astype(F32)).astype(BF16)
    gu_out[...] = up
    vu_out[...] = column_sum(up.astype(F32))
    dhidden[...] += nt(up, wu[...])

    @pl.when(step == pl.num_programs(0) - 1)
    def _():
        grad, normed = dhidden[...] + dsecond[...], normed1[...]
        sums_out[3:4, :] = column_sum(grad * normed)
        sums_out[4:5, :] = column_sum(grad)
        first = norm_backward(grad, normed, inverse1[:, 0:1], gain1[...])
        dfirst_out[...] = first
        narrow = first.astype(BF16)
        gb_out[...] = narrow
        sums_out[5:6, :] = column_sum(narrow.astype(F32))
        sums_out[6:8, :] = jnp.zeros((2, narrow.shape[1]), F32)
        gm_out[...] = nn(narrow, wo[...]).astype(BF16)


def feed_backward(segment, dy, later, saved, weights):
    width = dy.shape[2]
    edges = ROWS - MEMORY - TEXT
    units = weights["u"].shape[1]
    vector = whole((1, width))
    full = whole((ROWS, width))
    stats = whole((ROWS, 128))
    block = pl.BlockSpec((ROWS, UNITS), lambda i: (0, i))
    shape = jax.ShapeDtypeStruct
    return pl.pallas_call(
        functools.partial(feed_backward_kernel, segment),
        grid=(units // UNITS,),
        in_specs=[
            pl.BlockSpec((1, ROWS, width), lambda i: (segment, 0, 0)),
            pl.BlockSpec((edges, width), lambda i: (0, 0)),
            pl.BlockSpec((edges, width), lambda i: ((MEMORY + TEXT) // edges, 0)),
            full, stats, full, stats, block,
            pl.BlockSpec((width, UNITS), lambda i: (0, i)),
            pl.BlockSpec((width, UNITS), lambda i: (0, i)),
            whole((width, width)), vector, vector,
        ],
        out_specs=[
            full, block, full, full, full,
            pl.BlockSpec((1, UNITS), lambda i: (0, i)), whole((8, width)),
        ],
        out_shape=[
            shape((ROWS, width), BF16), shape((ROWS, units), BF16), shape((ROWS, width), BF16),
            shape((ROWS, width), F32), shape((ROWS, width), BF16),
            shape((1, units), F32), shape((8, width), F32),
        ],
        scratch_shapes=[pltpu.VMEM((ROWS, width), F32), pltpu.VMEM((ROWS, width), F32)],
        compiler_params=params(),
        name="feed_backward",
    )(
        dy, later, later, saved["normed2"], saved["inverse2"], saved["normed1"], saved["inverse1"],
        saved["slope"], weights["d"], weights["u"], weights["o"], weights["og"], weights["ag"],
    )


def backward_pair(pair, step, q, e, last, total, mixed, gm, k_pad, v_pad, gq_out, gk_out, gv_out):
    lane = lax.broadcasted_iota(jnp.int32, (ROWS, 128), 1)
    at = slice(128 * pair, 128 * pair + 128)
    grad = gm[:, at].astype(F32)
    product = grad * mixed[:, at].astype(F32)
    totals = total[...]
    rates, inners = [], []
    for half in range(2):
        mine = (lane < HEAD_DIM) if half == 0 else (lane >= HEAD_DIM)
        head = step * 4 + 2 * pair + half
        rate = 1.0 / jnp.sum(jnp.where(lane == head, totals, 0.0), axis=-1, keepdims=True)
        rates.append(rate)
        inners.append(jnp.sum(jnp.where(mine, product, 0.0), axis=-1, keepdims=True) * rate)
    scaled = (grad * jnp.where(lane < HEAD_DIM, rates[0], rates[1])).astype(BF16)
    scaled_t = scaled.T
    query_t = q[:, at].T
    gq, gk, gv = [], [], []
    for half in range(2):
        mine = (lane < HEAD_DIM) if half == 0 else (lane >= HEAD_DIM)
        rows = slice(HEAD_DIM * half, HEAD_DIM * half + HEAD_DIM)
        inner = inners[half]
        gmm = jnp.where(mine, scaled, jnp.zeros((), BF16))
        dp = nt(gmm, v_pad[:MAIN, at])
        last_dp = nt(gmm[MAIN:], v_pad[MAIN:, at])
        narrow_e, narrow_last = e[2 * pair + half], last[2 * pair + half]
        ds = (narrow_e.astype(F32) * (dp - inner)).astype(BF16)
        last_ds = (narrow_last.astype(F32) * (last_dp - inner[MAIN:])).astype(BF16)
        gq.append(plus_last(nn(ds, k_pad[:MAIN, at]), nn(last_ds, k_pad[MAIN:, at])))
        gk.append(jnp.concatenate([nn(query_t[rows, :], ds), nn(query_t[rows, MAIN:], last_ds)], axis=1))
        gv.append(
            jnp.concatenate([nn(scaled_t[rows, :], narrow_e), nn(scaled_t[rows, MAIN:], narrow_last)], axis=1)
        )
    gq_pair = jnp.where(lane < HEAD_DIM, gq[0], gq[1]) * HEAD_DIM**-0.5
    gq_out[:, at] = gq_pair.astype(BF16)
    gk_out[:, at] = jnp.concatenate(gk, axis=0).T[:ROWS].astype(BF16)
    gv_out[:, at] = jnp.concatenate(gv, axis=0).T[:ROWS].astype(BF16)


def attention_backward_kernel(
    q, k, v, e, last, total, mixed, gm, dfirst, wq, wk, wv,
    gq_out, gk_out, gv_out, dx_out, vq_out, vv_out,
    k_pad, v_pad,
):
    step = pl.program_id(0)

    @pl.when(step == 0)
    def _():
        dx_out[...] = dfirst[...]
        k_pad[...] = jnp.zeros_like(k_pad)
        v_pad[...] = jnp.zeros_like(v_pad)

    k_pad[:ROWS, :] = k[...]
    v_pad[:ROWS, :] = v[...]
    for pair in range(2):
        backward_pair(pair, step, q, e, last, total, mixed, gm, k_pad, v_pad, gq_out, gk_out, gv_out)
    vq_out[...] = column_sum(gq_out[...].astype(F32))
    vv_out[...] = column_sum(gv_out[...].astype(F32))
    dx_out[...] += (
        nn(gq_out[...], wq[...]) + nn(gk_out[...], wk[...]) + nn(gv_out[...], wv[...])
    )


def attention_backward(saved, gm, dfirst, weights):
    width = dfirst.shape[1]
    row_block = pl.BlockSpec((QUAD, width), lambda i: (i, 0))
    rows_block = pl.BlockSpec((ROWS, QUAD), lambda i: (0, i))
    full = whole((ROWS, width))
    sums = pl.BlockSpec((1, QUAD), lambda i: (0, i))
    shape = jax.ShapeDtypeStruct
    return pl.pallas_call(
        attention_backward_kernel,
        grid=(width // QUAD,),
        in_specs=[
            rows_block, rows_block, rows_block,
            pl.BlockSpec((4, ROWS, MAIN), lambda i: (i, 0, 0)),
            pl.BlockSpec((4, ROWS - MAIN, LAST), lambda i: (i, 0, 0)),
            whole((ROWS, 128)), rows_block, rows_block, full, row_block, row_block, row_block,
        ],
        out_specs=[rows_block, rows_block, rows_block, full, sums, sums],
        out_shape=[
            shape((ROWS, width), BF16), shape((ROWS, width), BF16), shape((ROWS, width), BF16),
            shape((ROWS, width), F32), shape((1, width), F32), shape((1, width), F32),
        ],
        scratch_shapes=[pltpu.VMEM((KEYS, QUAD), BF16), pltpu.VMEM((KEYS, QUAD), BF16)],
        compiler_params=params(),
        name="attention_backward",
    )(
        saved["q"], saved["k"], saved["v"], saved["e"], saved["last"], saved["total"], saved["mixed"],
        gm, dfirst, weights["q"], weights["k"], weights["v"],
    )


ROWS_MESH = 4
LINES = 16
MESH_IDS = pl.DeviceIdType.MESH
Z_UP, Z_DOWN, ACROSS, ALONG, HALF_ACROSS, HALF_ALONG = range(6)
SHARE = 6


class Place:
    def __init__(self, cols):
        self.row, self.col = lax.axis_index("row"), lax.axis_index("col")
        self.length = cols // 2
        self.core = lax.rem(self.col, 2)
        self.line = lax.div(self.col, 2)
        self.across_row = self.row + 1 - 2 * lax.rem(self.row, 2)
        self.along_row = self.row + 2 - 4 * lax.div(self.row, 2)
        self.corner_row = 3 - self.row
        self.across = (self.across_row, self.col)
        self.along = (self.along_row, self.col)
        self.up = (self.row, self.col + 2)
        self.down = (self.row, self.col - 2)
        self.other_core = 1 - self.core
        self.partner = (self.row, self.col + 1 - 2 * self.core)

    def greet(self):
        barrier = pltpu.get_barrier_semaphore()

        def signal(device):
            pl.semaphore_signal(barrier, inc=1, device_id=device, device_id_type=MESH_IDS)

        signal(self.across)
        signal(self.along)
        signal(self.partner)
        pl.when(self.line > 0)(lambda: signal(self.down))
        pl.when(self.line < self.length - 1)(lambda: signal(self.up))
        has_down = lax.div(self.line + self.length - 1, self.length)
        has_up = lax.div(2 * self.length - 2 - self.line, self.length)
        pl.semaphore_wait(barrier, 3 + has_down + has_up)

    def at_distance(self, distance, visit):
        if distance == 0:
            visit(self.line, None)
        else:
            below, above = self.line - distance, self.line + distance
            pl.when(below >= 0)(lambda: visit(below, True))
            pl.when(above < self.length)(lambda: visit(above, False))


def splits(count):
    first = count // 32 * 16
    return ((0, first), (first, count - first))


def first_forward_kernel(square, upper, lower, tails, starts, words, edge, wq, wk, wv, wo, *rest):
    vectors, (whole_upper, whole_lower) = rest[:9], rest[9:11]
    (
        q_out, k_out, v_out, e_out, last_out, total_out, mixed_out, hidden_out, normed_out, inverse_out,
        narrow, narrow_hidden, gathered, send, recv, own, x, bias, last_bias, k_pad, v_pad, branch,
    ) = rest[11:]
    turn = pl.program_id(0)
    rows, cols = ROWS_MESH, wq.shape[0] // lower.shape[0]
    quads = wq.shape[0] // QUAD
    place = Place(cols)
    depth, across = upper.shape[0], lower.shape[0]
    sources = (square, upper, lower)

    def target(which, row, col, part=None):
        if which == 0:
            view, count = gathered.at[row * cols + col], square.shape[0]
            begin, size = part if part else (0, count)
            return view.at[pl.ds(begin, size)]
        count, wide = sources[which].shape
        array, high, side = (whole_upper, row, col) if which == 1 else (whole_lower, col, row)
        begin, size = part if part else (0, count)
        return array.at[
            pl.ds(pl.multiple_of(high * count + begin, 16), size),
            pl.ds(pl.multiple_of(side * wide, 128), wide),
        ]

    def copy(which, kind, row, line, device, part=None, mine=None, arrival=None):
        col = 2 * line + (place.core if mine is None else mine)
        there = target(which, row, col, part)
        here = there if arrival is None else sources[which]
        return pltpu.make_async_remote_copy(
            src_ref=here, dst_ref=there,
            send_sem=send.at[which, kind, line], recv_sem=recv.at[which, kind, line],
            device_id=device, device_id_type=MESH_IDS,
        )

    def keep(which):
        return pltpu.make_async_copy(
            sources[which], target(which, place.row, place.col), own.at[which]
        )

    def both(which):
        return splits(sources[which].shape[0])

    def by_line(which, distance):
        def visit(line, upward):
            first = True if upward is None else None
            args = (place.row, line)
            if upward is not None:
                kind = Z_UP if upward else Z_DOWN
                copy(which, kind, *args, place.down).wait_recv()
            if upward is None or upward:
                pl.when(place.line < place.length - 1)(
                    lambda: copy(which, Z_UP, *args, place.up, arrival=first).start()
                )
            if upward is None or not upward:
                pl.when(place.line > 0)(
                    lambda: copy(which, Z_DOWN, *args, place.down, arrival=first).start()
                )
            copy(which, ACROSS, *args, place.across, arrival=first).start()
            copy(which, ALONG, *args, place.along, arrival=first).start()
            copy(which, SHARE, *args, place.partner, arrival=first).start()

        place.at_distance(distance, visit)

    def by_side(which, distance):
        halves = both(which)

        def visit(line, upward):
            copy(which, ACROSS, place.across_row, line, place.across).wait_recv()
            copy(which, HALF_ALONG, place.across_row, line, place.along, halves[1]).start()
            copy(which, SHARE + 1, place.across_row, line, place.partner).start()
            copy(which, ALONG, place.along_row, line, place.along).wait_recv()
            copy(which, HALF_ACROSS, place.along_row, line, place.across, halves[0]).start()
            copy(which, SHARE + 2, place.along_row, line, place.partner).start()

        place.at_distance(distance, visit)

    def by_corner(which, distance):
        halves = both(which)

        def visit(line, upward):
            copy(which, HALF_ACROSS, place.corner_row, line, place.across, halves[0]).wait_recv()
            copy(which, SHARE + 3, place.corner_row, line, place.partner, halves[0]).start()
            copy(which, HALF_ALONG, place.corner_row, line, place.along, halves[1]).wait_recv()
            copy(which, SHARE + 4, place.corner_row, line, place.partner, halves[1]).start()

        place.at_distance(distance, visit)

    def from_partner(which):
        halves = both(which)
        for distance in range(place.length):

            def visit(line, upward):
                mine = place.other_core
                for kind, row, part in (
                    (0, place.row, None), (1, place.across_row, None), (2, place.along_row, None),
                    (3, place.corner_row, halves[0]), (4, place.corner_row, halves[1]),
                ):
                    copy(which, SHARE + kind, row, line, place.partner, part, mine=mine).wait_recv()

            place.at_distance(distance, visit)

    def drain(which):
        halves = both(which)
        for distance in range(place.length):

            def visit(line, upward):
                args = (place.row, line)
                first = True if upward is None else None
                if upward is None or upward:
                    pl.when(place.line < place.length - 1)(
                        lambda: copy(which, Z_UP, *args, place.up, arrival=first).wait_send()
                    )
                if upward is None or not upward:
                    pl.when(place.line > 0)(
                        lambda: copy(which, Z_DOWN, *args, place.down, arrival=first).wait_send()
                    )
                copy(which, ACROSS, *args, place.across, arrival=first).wait_send()
                copy(which, ALONG, *args, place.along, arrival=first).wait_send()
                copy(which, SHARE, *args, place.partner, arrival=first).wait_send()
                copy(which, HALF_ALONG, place.across_row, line, place.along, halves[1]).wait_send()
                copy(which, HALF_ACROSS, place.along_row, line, place.across, halves[0]).wait_send()
                copy(which, SHARE + 1, place.across_row, line, place.partner).wait_send()
                copy(which, SHARE + 2, place.along_row, line, place.partner).wait_send()
                copy(which, SHARE + 3, place.corner_row, line, place.partner, halves[0]).wait_send()
                copy(which, SHARE + 4, place.corner_row, line, place.partner, halves[1]).wait_send()

            place.at_distance(distance, visit)

    length = place.length

    def advance(which, at):
        if at < length:
            by_line(which, at)
        if 1 <= at < length + 1:
            by_side(which, at - 1)
        if 2 <= at < length + 2:
            by_corner(which, at - 2)

    moves = [(which, at) for at in range(1, length + 2) for which in (1, 2)]
    slots = [3 * (at // 2) + 2 * (at % 2) for at in range(6)]

    def slot(at):
        if at in slots:
            advance(*moves[slots.index(at)])

    @pl.when(turn == 0)
    def _():
        place.greet()
        for which in range(3):
            keep(which).start()
        advance(0, 0)
        forward_open(
            0, tails, starts, words, edge, total_out, narrow, x, bias, last_bias, k_pad, v_pad, branch
        )
        for at in range(1, length + 2):
            advance(0, at)
            if at in (2, 3):
                advance(at - 1, 0)
        from_partner(0)
        keep(0).wait()
        outs = (wq, wk, wv, wo)
        for col in range(cols):
            for at, out in enumerate(outs):
                out[across * col : across * col + across, :] = jnp.concatenate(
                    [
                        gathered[row * cols + col, :across, depth * at : depth * at + depth]
                        for row in range(rows)
                    ],
                    axis=1,
                )
        lines = [gathered[col, across:, :across].astype(F32) for col in range(cols)]
        table = jnp.concatenate(lines, axis=1)
        for at in range(8):
            vectors[at][...] = table[at : at + 1]
        vectors[8][...] = jnp.concatenate(
            [line[8 + at : 9 + at] for line in lines for at in range(upper.shape[1] // across)], axis=1
        )

    @pl.when(turn > 0)
    def _():
        quad = turn - 1
        part = pl.ds(pl.multiple_of(quad * QUAD, QUAD), QUAD)

        def offer(place_in_quad):
            for at in range(quads):
                if 3 * at + place_in_quad in slots:
                    pl.when(quad == at)(functools.partial(slot, 3 * at + place_in_quad))

        forward_project(
            narrow, wq[part, :], wk[part, :], wv[part, :], vectors[0][:, part], vectors[1][:, part],
            q_out, k_out, v_out, k_pad, v_pad,
        )
        offer(0)
        for pair in range(2):
            forward_pair(pair, quad, q_out, bias, last_bias, k_pad, v_pad, e_out, last_out, total_out, mixed_out)
            offer(1 + pair)
        branch[...] += nt(mixed_out[...], wo[:, part])

    @pl.when(turn == quads)
    def _():
        forward_close(
            x, branch, vectors[2][...], vectors[3][...], vectors[4][...],
            hidden_out, normed_out, inverse_out, narrow_hidden,
        )
        for which, at in moves[len(slots) :]:
            advance(which, at)
        for which in range(1, 3):
            from_partner(which)
            keep(which).wait()
        for which in range(3):
            drain(which)


def pack_kernel(wq, wk, wv, wo, wd, vectors, square, lower):
    across, depth = wq.shape[1], wq.shape[0]
    square[:across, :] = jnp.concatenate(
        [item[...].astype(F32).T for item in (wq, wk, wv, wo)], axis=1
    ).astype(BF16)
    square[across:, :] = jnp.zeros((LINES, square.shape[1]), BF16)
    square[across : across + LINES, :128] = vectors[...]
    lower[...] = wd[...].astype(F32).T.astype(BF16)


def first_forward(arguments, tails, starts, words, edge):
    matrices, vectors = arguments[:6], arguments[6:]
    rows, cols = lax.axis_size("row"), lax.axis_size("col")
    depth, across = matrices[0].shape
    width = depth * rows
    units = matrices[4].shape[1] * cols
    table = jnp.stack([*vectors[:5], *vectors[6:]])
    table = jnp.concatenate([table, vectors[5].reshape(-1, across)], axis=0)
    table = jnp.pad(table, ((0, LINES - table.shape[0]), (0, 128 - across)))
    shape = jax.ShapeDtypeStruct
    square, lower = pl.pallas_call(
        pack_kernel,
        out_shape=[shape((across + LINES, 4 * depth), BF16), shape((across, matrices[5].shape[0]), BF16)],
        in_specs=[pl.BlockSpec(memory_space=pltpu.VMEM)] * 6,
        out_specs=[pl.BlockSpec(memory_space=pltpu.VMEM)] * 2,
        name="pack",
    )(*matrices[:4], matrices[5], table)
    anywhere = pl.BlockSpec(memory_space=pl.ANY)
    kinds = (3, SHARE + 5, cols // 2)
    steps = width // QUAD

    def quad(i):
        return jnp.maximum(i - 1, 0)

    def resident(size):
        return pl.BlockSpec(size, lambda i: (0,) * len(size))

    def once(size, first=0):
        index = (first,) + (0,) * (len(size) - 1)
        return pl.BlockSpec(size, lambda i: index, pipeline_mode=pl.Buffered(1))

    rows_block = pl.BlockSpec((ROWS, QUAD), lambda i: (0, quad(i)))
    full, stats = (ROWS, width), (ROWS, 128)
    names = ("q", "k", "v", "o", "vq", "vv", "vo", "ag", "as", "vd", "og", "os", "vu", "u", "d")
    sizes = [(width, width)] * 4 + [(1, width)] * 8 + [(1, units)]
    results = pl.pallas_call(
        first_forward_kernel,
        grid=(1 + steps,),
        out_shape=[shape(size, BF16 if size[0] > 1 else F32) for size in sizes]
        + [shape((width, units), BF16), shape((width, units), BF16)]
        + [shape(full, BF16)] * 3
        + [shape((HEADS, ROWS, MAIN), BF16), shape((HEADS, ROWS - MAIN, LAST), BF16)]
        + [shape(stats, F32), shape(full, BF16), shape(full, F32), shape(full, F32), shape(stats, F32)]
        + [shape(full, BF16)] * 2,
        in_specs=[anywhere] * 3
        + [pl.BlockSpec(memory_space=pltpu.SMEM)] * 2
        + [once((1, ROWS, width)), once(edge.shape)],
        out_specs=[resident(size) for size in sizes] + [anywhere] * 2 + [
            rows_block, rows_block, rows_block,
            pl.BlockSpec((4, ROWS, MAIN), lambda i: (quad(i), 0, 0)),
            pl.BlockSpec((4, ROWS - MAIN, LAST), lambda i: (quad(i), 0, 0)),
            resident(stats), rows_block, resident(full), resident(full), resident(stats),
            resident(full), resident(full),
        ],
        scratch_shapes=[
            pltpu.VMEM((rows * cols, across + LINES, 4 * depth), BF16),
            pltpu.SemaphoreType.DMA(kinds), pltpu.SemaphoreType.DMA(kinds), pltpu.SemaphoreType.DMA((3,)),
            pltpu.VMEM(full, F32), pltpu.VMEM((ROWS, MAIN), F32), pltpu.VMEM((ROWS - MAIN, LAST), F32),
            pltpu.VMEM((KEYS, QUAD), BF16), pltpu.VMEM((KEYS, QUAD), BF16), pltpu.VMEM(full, F32),
        ],
        compiler_params=pltpu.CompilerParams(
            dimension_semantics=("arbitrary",), collective_id=0, has_side_effects=True,
            vmem_limit_bytes=58 * 1024 * 1024,
        ),
        name="first_forward",
    )(square, matrices[4], lower, tails, starts, words, edge)
    return dict(zip(names, results)), results[len(names) :]


def joined(first, second):
    return jnp.concatenate([first, second], axis=0)


def product_kernel(left1, left2, right1, right2, out, turned):
    @pl.when(pl.program_id(0) == 0)
    def _():
        turned[...] = joined(left1[...], left2[...]).T

    out[...] = nn(turned[...], joined(right1[...], right2[...])).astype(BF16)


def product_t(left1, left2, right1, right2):
    width, units = left1.shape[1], right1.shape[1]
    block = pl.BlockSpec((ROWS, UNITS), lambda i: (0, i))
    return pl.pallas_call(
        product_kernel,
        grid=(units // UNITS,),
        in_specs=[whole((ROWS, width))] * 2 + [block] * 2,
        out_specs=pl.BlockSpec((width, UNITS), lambda i: (0, i)),
        out_shape=jax.ShapeDtypeStruct((width, units), BF16),
        scratch_shapes=[pltpu.VMEM((width, 2 * ROWS), BF16)],
        compiler_params=params(),
        name="weight_gradient",
    )(left1, left2, right1, right2)


SUM_ROWS = (5, 3, 4, 2, 0, 1)


class Scatter:
    def __init__(self, square, upper, lower, outs, scratch):
        self.square, self.upper, self.lower, self.outs = square, upper, lower, outs
        held, self.theirs, self.corner, self.side, self.lined = (
            scratch[:2], scratch[2:5], scratch[5:8], scratch[8:11], scratch[11:14]
        )
        self.held = (None, *held)
        self.send, self.recv, self.own = scratch[14:]
        self.cols = square.shape[0] // ROWS_MESH
        self.place = Place(self.cols)
        self.length = self.place.length

    def source(self, which, row, col):
        count, wide = self.outs[which].shape
        if which == 0:
            return self.square.at[row * self.cols + col]
        array, high, level = (self.upper, row, col) if which == 1 else (self.lower, col, row)
        return array.at[
            pl.ds(pl.multiple_of(high * count, 16), count),
            pl.ds(pl.multiple_of(level * wide, 128), wide),
        ]

    def mine(self, which, row, line, part=None):
        if which == 0:
            array, at = self.square, row * self.cols + 2 * line + self.place.core
        else:
            array, at = self.held[which], row * self.length + line
        return array.at[at] if part is None else array.at[at, pl.ds(*part)]

    def load(self, which, row, line):
        at = row * self.length + line
        return pltpu.make_async_copy(
            self.source(which, row, 2 * line + self.place.core),
            self.held[which].at[at], self.own.at[which - 1, at],
        )

    def remote(self, which, kind, line, here, there, device):
        return pltpu.make_async_remote_copy(
            src_ref=here, dst_ref=there,
            send_sem=self.send.at[which, kind, line], recv_sem=self.recv.at[which, kind, line],
            device_id=device, device_id_type=MESH_IDS,
        )

    def share(self, which, row, line, core):
        here = self.source(which, row, 2 * line + core)
        there = self.theirs[which].at[row * self.length + line]
        return self.remote(which, SHARE + row, line, here, there, self.place.partner)

    def corner_copy(self, which, kind, line):
        part = splits(self.outs[which].shape[0])[kind - HALF_ACROSS]
        here = self.mine(which, self.place.corner_row, line, part)
        there = self.corner[which].at[line, pl.ds(*part)]
        device = self.place.across if kind == HALF_ACROSS else self.place.along
        return self.remote(which, kind, line, here, there, device)

    def side_copy(self, which, kind, line):
        place = self.place
        row, device = (place.across_row, place.across) if kind == ACROSS else (place.along_row, place.along)
        there = self.side[which].at[kind - ACROSS, line]
        return self.remote(which, kind, line, self.mine(which, row, line), there, device)

    def line_copy(self, which, kind, line):
        device = self.place.up if kind == Z_UP else self.place.down
        here = self.mine(which, self.place.row, line)
        return self.remote(which, kind, line, here, self.lined[which].at[kind, line], device)

    def add(self, block, arrived):
        block[...] = (block[...].astype(F32) + arrived[...].astype(F32)).astype(BF16)

    def begin(self, which):
        place = self.place
        for distance in range(self.length - 1, -1, -1):

            def visit(line, downward):
                for row in (place.corner_row, place.across_row, place.along_row, place.row):
                    if which:
                        self.load(which, row, line).start()
                    self.share(which, row, line, place.other_core).start()

            place.at_distance(distance, visit)

    def merge(self, which, row, line):
        if which:
            self.load(which, row, line).wait()
        self.share(which, row, line, self.place.core).wait_recv()
        self.add(self.mine(which, row, line), self.theirs[which].at[row * self.length + line])

    def cores(self, which, distance):
        place = self.place

        def visit(line, downward):
            self.merge(which, place.corner_row, line)
            self.merge(which, place.across_row, line)
            self.corner_copy(which, HALF_ACROSS, line).start()
            self.corner_copy(which, HALF_ALONG, line).start()
            self.merge(which, place.along_row, line)
            self.merge(which, place.row, line)

        place.at_distance(distance, visit)

    def corners(self, which, distance):
        place = self.place
        first, second = splits(self.outs[which].shape[0])

        def visit(line, downward):
            for kind, row, part in (
                (HALF_ACROSS, place.along_row, first), (HALF_ALONG, place.across_row, second)
            ):
                self.corner_copy(which, kind, line).wait_recv()
                self.add(self.mine(which, row, line, part), self.corner[which].at[line, pl.ds(*part)])
            self.side_copy(which, ALONG, line).start()
            self.side_copy(which, ACROSS, line).start()

        place.at_distance(distance, visit)

    def sides(self, which, distance):
        def visit(line, downward):
            for kind in (ACROSS, ALONG):
                self.side_copy(which, kind, line).wait_recv()
                self.add(self.mine(which, self.place.row, line), self.side[which].at[kind - ACROSS, line])

        self.place.at_distance(distance, visit)

    def lines(self, which, distance):
        place = self.place

        def visit(line, downward):
            kind = Z_DOWN if downward else Z_UP
            onward = place.line < self.length - 1 if downward else place.line > 0

            @pl.when(onward)
            def _():
                self.line_copy(which, kind, line).wait_recv()
                self.add(self.mine(which, place.row, line), self.lined[which].at[kind, line])

            self.line_copy(which, kind, line).start()

        place.at_distance(distance, visit)

    def result(self, which):
        place = self.place
        block = self.mine(which, place.row, place.line)
        for kind, there in ((Z_UP, place.line > 0), (Z_DOWN, place.line < self.length - 1)):

            @pl.when(there)
            def _():
                self.line_copy(which, kind, place.line).wait_recv()
                self.add(block, self.lined[which].at[kind, place.line])

        self.outs[which][...] = block[...].astype(F32)

    def all_cores(self, which):
        for distance in range(self.length - 1, -1, -1):
            self.cores(which, distance)

    def all_corners(self, which):
        for distance in range(self.length - 1, -1, -1):
            self.corners(which, distance)

    def step(self, which, at):
        if at < self.length:
            self.sides(which, self.length - 1 - at)
        if 1 <= at < self.length:
            self.lines(which, self.length - at)
        if at == self.length:
            self.result(which)

    def drain(self, which):
        for distance in range(self.length):

            def visit(line, downward):
                for row in range(ROWS_MESH):
                    self.share(which, row, line, self.place.other_core).wait_send()
                for kind in (HALF_ACROSS, HALF_ALONG):
                    self.corner_copy(which, kind, line).wait_send()
                for kind in (ACROSS, ALONG):
                    self.side_copy(which, kind, line).wait_send()
                if downward is not None:
                    self.line_copy(which, Z_DOWN if downward else Z_UP, line).wait_send()

            self.place.at_distance(distance, visit)


PAIRS = QUAD // 128


def last_backward_kernel(
    q, k, v, e, last, total, mixed, gm, dfirst, wq, wk, wv,
    gq2, gk2, gv2, gb1, gb2, x1, x2, mixed1, mixed2, vq2, vv2, sums1, sums2, vu1, vu2, upper, lower,
    dx_out, square_out, upper_out, lower_out,
    k_pad, v_pad, gq, gk, gv, vq, vv, totals, blocks, *scratch,
):
    step = pl.program_id(0)
    quads = gq.shape[0]
    travel = Scatter(blocks, upper, lower, (square_out, upper_out, lower_out), scratch)
    length = travel.length
    steps = [functools.partial(travel.step, which, at) for which in (1, 2) for at in range(length + 1)]
    early = {
        0: (functools.partial(travel.all_cores, 1),), 1: (functools.partial(travel.all_cores, 2),),
        2: (functools.partial(travel.all_corners, 1),), 4: (functools.partial(travel.all_corners, 2),),
    }
    taken = 0
    for slot in range(quads * PAIRS, quads * PAIRS + 3):
        early[slot], taken = (steps[taken],), taken + 1
    squares = [functools.partial(travel.all_cores, 0), functools.partial(travel.all_corners, 0)]
    squares += [functools.partial(travel.step, 0, at) for at in range(length + 1)]
    late = []
    while steps[taken:] or squares:
        late += steps[taken : taken + 2] if len(squares) > length else steps[taken : taken + 1]
        taken += 2 if len(squares) > length else 1
        late += squares[:1]
        squares = squares[1:]

    def advance(slot):
        for move in early.get(slot, ()):
            move()

    @pl.when(step == 0)
    def _():
        travel.place.greet()
        travel.begin(1)
        travel.begin(2)
        dx_out[...] = dfirst[...]
        k_pad[...] = jnp.zeros_like(k_pad)
        v_pad[...] = jnp.zeros_like(v_pad)

    @pl.when(step < quads)
    def _():
        outs = gq.at[step], gk.at[step], gv.at[step]
        k_pad[:ROWS, :] = k[...]
        v_pad[:ROWS, :] = v[...]
        for pair in range(PAIRS):
            backward_pair(pair, step, q, e, last, total, mixed, gm, k_pad, v_pad, *outs)
            for at in range(quads):
                pl.when(step == at)(functools.partial(advance, at * PAIRS + pair))
        vq[step] = column_sum(outs[0][...].astype(F32))
        vv[step] = column_sum(outs[2][...].astype(F32))
        dx_out[...] += nn(outs[0][...], wq[...]) + nn(outs[1][...], wk[...]) + nn(outs[2][...], wv[...])

    @pl.when(step == quads)
    def _():
        rows, cols = ROWS_MESH, travel.cols
        width = blocks.shape[2]
        across, depth = width // cols, width // rows
        inputs = joined(x1[...], x2[...])
        for at, (first, second) in enumerate(((gq, gq2), (gk, gk2), (gv, gv2))):
            for quad in range(quads):
                part = slice(QUAD * quad, QUAD * quad + QUAD)
                totals[at, part, :] = nn(joined(first[quad], second[:, part]).T, inputs).astype(BF16)
            advance(quads * PAIRS + at)
        totals[3] = nn(joined(gb1[...], gb2[...]).T, joined(mixed1[...], mixed2[...])).astype(BF16)
        sums = sums1[...] + sums2[...]
        wide = vu1[...] + vu2[...]
        vectors = jnp.concatenate(
            [
                jnp.concatenate([vq[quad] for quad in range(quads)], axis=1) + vq2[...],
                jnp.concatenate([vv[quad] for quad in range(quads)], axis=1) + vv2[...],
            ]
            + [sums[at : at + 1] for at in SUM_ROWS],
            axis=0,
        )
        share = wide.shape[1] // cols // across
        for col in range(cols):
            begin = across * col
            narrow = jnp.concatenate(
                [vectors[:, begin : begin + across]]
                + [wide[:, across * (col * share + at) : across * (col * share + at + 1)] for at in range(share)]
                + [jnp.zeros((LINES - 8 - share, across), F32)],
                axis=0,
            )
            narrow = jnp.pad(narrow, ((0, 0), (0, width - across))).astype(BF16)
            for row in range(rows):
                block = row * cols + col
                blocks[block, :across, :] = jnp.concatenate(
                    [totals[at, begin : begin + across, depth * row : depth * row + depth] for at in range(4)],
                    axis=1,
                )
                blocks[block, across:, :] = narrow
        travel.begin(0)
        for move in late:
            move()
        for which in range(3):
            travel.drain(which)


def last_backward(saved1, saved2, gm, dfirst, weights, grads1, grads2, upper, lower, cols):
    width = dfirst.shape[1]
    quads = width // QUAD
    length = cols // 2
    across, depth = width // cols, width // ROWS_MESH
    units = upper.shape[1]
    sizes = ((across + LINES, width), (depth, units // cols), (across, units // ROWS_MESH))
    kinds = (3, SHARE + ROWS_MESH, length)

    def once(array):
        return pl.BlockSpec(array.shape, lambda i: (0,) * array.ndim, pipeline_mode=pl.Buffered(1))

    def turn(i):
        return jnp.minimum(i, quads - 1)

    rows_block = pl.BlockSpec((ROWS, QUAD), lambda i: (0, turn(i)))
    row_block = pl.BlockSpec((QUAD, width), lambda i: (turn(i), 0))
    anywhere = pl.BlockSpec(memory_space=pl.ANY)
    singles = (
        grads2["gq"], grads2["gk"], grads2["gv"], grads1["gb"], grads2["gb"], saved1["x"], saved2["x"],
        saved1["mixed"], saved2["mixed"], grads2["vq"], grads2["vv"],
        grads1["sums"], grads2["sums"], grads1["vu"], grads2["vu"],
    )
    buffers = [
        pltpu.VMEM((*lead, *size), BF16)
        for lead in ((ROWS_MESH * length,), (ROWS_MESH * length,), (length,), (2, length), (2, length))
        for size in sizes
    ][1:]
    shape = jax.ShapeDtypeStruct
    return pl.pallas_call(
        last_backward_kernel,
        grid=(quads + 1,),
        in_specs=[
            rows_block, rows_block, rows_block,
            pl.BlockSpec((4, ROWS, MAIN), lambda i: (turn(i), 0, 0)),
            pl.BlockSpec((4, ROWS - MAIN, LAST), lambda i: (turn(i), 0, 0)),
            once(saved1["total"]), rows_block, rows_block, once(dfirst), row_block, row_block, row_block,
            *(once(item) for item in singles), anywhere, anywhere,
        ],
        out_specs=[whole((ROWS, width)), *(whole(size) for size in sizes)],
        out_shape=[shape((ROWS, width), F32), *(shape(size, F32) for size in sizes)],
        scratch_shapes=[
            pltpu.VMEM((KEYS, QUAD), BF16), pltpu.VMEM((KEYS, QUAD), BF16),
            *[pltpu.VMEM((quads, ROWS, QUAD), BF16)] * 3, *[pltpu.VMEM((quads, 1, QUAD), F32)] * 2,
            pltpu.VMEM((4, width, width), BF16),
            pltpu.VMEM((ROWS_MESH * cols, *sizes[0]), BF16),
            *buffers,
            pltpu.SemaphoreType.DMA(kinds), pltpu.SemaphoreType.DMA(kinds),
            pltpu.SemaphoreType.DMA((2, ROWS_MESH * length)),
        ],
        compiler_params=pltpu.CompilerParams(
            dimension_semantics=("arbitrary",), collective_id=1, has_side_effects=True,
            vmem_limit_bytes=63 * 1024 * 1024,
        ),
        name="last_backward",
    )(
        saved1["q"], saved1["k"], saved1["v"], saved1["e"], saved1["last"], saved1["total"], saved1["mixed"],
        gm, dfirst, weights["q"], weights["k"], weights["v"], *singles, upper, lower,
    )


def gather_all(part):
    return lax.all_gather(part, ("row", "col"), axis=0, tiled=False)


def fetch(arguments):
    matrices, vectors = arguments[:6], arguments[6:]
    rows, cols = lax.axis_size("row"), lax.axis_size("col")
    depth, across = matrices[0].shape
    width = depth * rows
    names = ("q", "k", "v", "o")
    square = jnp.concatenate([item.T for item in matrices[:4]], axis=1)
    upper = matrices[4].T.reshape(4, across, depth).transpose(1, 0, 2).reshape(across, 4 * depth)
    lower = matrices[5].T
    line = jnp.concatenate(vectors)
    extra = -(-line.shape[0] // (4 * depth))
    extra += -(across + extra) % 16
    line = jnp.pad(line, (0, extra * 4 * depth - line.shape[0])).reshape(extra, 4 * depth)
    first = gather_all(jnp.concatenate([square, line], axis=0))
    second = gather_all(upper)
    third = gather_all(lower)
    whole_square = (
        first[:, :across].reshape(rows, cols, across, 4, depth)
        .transpose(3, 1, 2, 0, 4).reshape(4, width, width)
    )
    weights = {name: whole_square[at] for at, name in enumerate(names)}
    weights["u"] = (
        second.reshape(rows, cols, across, 4, depth)
        .transpose(0, 4, 1, 3, 2).reshape(width, 4 * width)
    )
    weights["d"] = third.reshape(rows, cols, across, 4 * depth).transpose(1, 2, 0, 3).reshape(width, 4 * width)
    lines = first[:cols, across:].reshape(cols, -1).astype(F32)
    at = 0
    for name, item in zip(("vq", "vv", "vo", "ag", "as", "vu", "vd", "og", "os"), vectors):
        weights[name] = lines[:, at : at + item.shape[0]].reshape(1, -1)
        at += item.shape[0]
    return weights


def scatter_all(terms):
    return lax.psum_scatter(terms, ("row", "col"), scatter_dimension=0, tiled=False)


def scatter(square, upper, lower, lines):
    rows, cols = lax.axis_size("row"), lax.axis_size("col")
    width = square.shape[1]
    depth, across = width // rows, width // cols
    square = square.reshape(4, cols, across, rows, depth).transpose(3, 1, 2, 0, 4)
    square = square.reshape(rows, cols, across, 4 * depth)
    count = lines.shape[1]
    extra = -(-count // (4 * depth))
    extra += -(across + extra) % 16
    lines = jnp.pad(lines, ((0, 0), (0, extra * 4 * depth - count))).astype(BF16)
    lines = jnp.broadcast_to(lines.reshape(1, cols, extra, 4 * depth), (rows, cols, extra, 4 * depth))
    square = jnp.concatenate([square, lines], axis=2)
    square = scatter_all(square.reshape(rows * cols, across + extra, 4 * depth)).astype(F32)
    upper = upper.reshape(rows, depth, cols, 4 * across).transpose(0, 2, 1, 3)
    upper = scatter_all(upper.reshape(rows * cols, depth, 4 * across)).astype(F32)
    lower = lower.reshape(cols, across, rows, 4 * depth).transpose(2, 0, 1, 3)
    lower = scatter_all(lower.reshape(rows * cols, across, 4 * depth)).astype(F32)
    return square[:across], upper, lower, square[across:].reshape(-1)[:count]


def solution_body(
    text, memory, tail_lengths, picture_starts, grad_out, *parameters
):
    rows, cols = lax.axis_size("row"), lax.axis_size("col")
    depth, across = parameters[0].shape
    width = depth * rows
    by_kernel = rows == ROWS_MESH and cols % 2 == 0 and depth % 32 == 0 and across % 32 == 0
    by_kernel = by_kernel and 4 * across % 128 == 0
    words = jnp.pad(text[0].astype(F32), ((0, 0), (MEMORY, ROWS - MEMORY - TEXT), (0, 0)))
    attended = None
    if by_kernel:
        weights, attended = first_forward(parameters, tail_lengths, picture_starts, words, memory[0])
    else:
        weights = fetch(parameters)

    def forward(segment, edge, attended=None):
        if attended is None:
            attended = attention_forward(segment, tail_lengths, picture_starts, words, edge, weights)
        q, k, v, e, last, total, mixed, hidden, normed1, inverse1, xb, hb = attended
        act, slope, y, edge, normed2, inverse2 = feed_forward(hidden, hb, weights)
        saved = dict(
            x=xb, q=q, k=k, v=v, e=e, last=last, total=total, mixed=mixed, hidden=hb,
            normed1=normed1, inverse1=inverse1, act=act, slope=slope, normed2=normed2, inverse2=inverse2,
        )
        return y, edge, saved

    def paired(first, second, begin, count):
        which = lax.broadcasted_iota(jnp.int32, (count, 2, width), 1)
        first, second = (item[begin : begin + count, None, :] for item in (first, second))
        return jnp.where(which == 0, first, second).astype(BF16).transpose(1, 0, 2)[None]

    y1, edge1, saved1 = forward(0, memory[0], attended)
    y2, edge2, saved2 = forward(1, edge1)
    layer_output = paired(y1, y2, 0, SEG_ROWS)

    def feed(segment, later, saved):
        gd, gu, gb, dfirst, gm, vu, sums = feed_backward(segment, cotangent, later, saved, weights)
        return gm, dfirst, dict(gd=gd, gu=gu, gb=gb, vu=vu, sums=sums)

    def attend(saved, gm, dfirst):
        gq, gk, gv, dx, vq, vv = attention_backward(saved, gm, dfirst, weights)
        return dx, dict(gq=gq, gk=gk, gv=gv, vq=vq, vv=vv)

    cotangent = jnp.pad(grad_out[0].astype(F32), ((0, 0), (0, ROWS - SEG_ROWS), (0, 0)))
    gm2, dfirst2, grads2 = feed(1, saved2["normed2"], saved2)
    dx2, more = attend(saved2, gm2, dfirst2)
    grads2.update(more)
    gm1, dfirst1, grads1 = feed(0, dx2, saved1)
    upper = product_t(saved1["hidden"], saved2["hidden"], grads1["gu"], grads2["gu"])
    lower = product_t(grads1["gd"], grads2["gd"], saved1["act"], saved2["act"])
    if by_kernel:
        dx1, square, upper, lower = last_backward(
            saved1, saved2, gm1, dfirst1, weights, grads1, grads2, upper, lower, cols
        )
        table = square[across : across + LINES, :across]
        square = square[:across]
        lines = [table[at] for at in range(8)]
        lines.insert(5, table[8 : 8 + upper.shape[1] // across].reshape(-1))
    else:
        dx1, more = attend(saved1, gm1, dfirst1)
        grads1.update(more)
        square = jnp.stack(
            [
                product_t(grads1["gq"], grads2["gq"], saved1["x"], saved2["x"]),
                product_t(grads1["gk"], grads2["gk"], saved1["x"], saved2["x"]),
                product_t(grads1["gv"], grads2["gv"], saved1["x"], saved2["x"]),
                product_t(grads1["gb"], grads2["gb"], saved1["mixed"], saved2["mixed"]),
            ]
        )
        sums = grads1["sums"] + grads2["sums"]
        wide = grads1["vu"] + grads2["vu"]
        parts = (grads1["vq"] + grads2["vq"], grads1["vv"] + grads2["vv"])
        vectors = jnp.concatenate([*parts, *(sums[at : at + 1] for at in SUM_ROWS)], axis=0)
        table = jnp.concatenate(
            [vectors.reshape(8, cols, across).transpose(1, 0, 2).reshape(cols, -1), wide.reshape(cols, -1)],
            axis=1,
        )
        square, upper, lower, line = scatter(square, upper, lower, table)
        lines = [line[at * across : at * across + across] for at in range(8)]
        lines.insert(5, line[8 * across :])
    memory_grad = (dx1[:MEMORY] + dx1[MEMORY + TEXT : SEG_ROWS]).astype(BF16)[None]
    text_grad = paired(dx1, dx2, MEMORY, TEXT)
    own = square.reshape(across, 4, depth)
    result = [own[:, at].T for at in range(4)] + [upper, lower.T]
    return (layer_output, text_grad, memory_grad, *result, *lines)


def solution(mesh):
    batch, matrix, vector = P(("row", "col")), P("row", "col"), P("col")
    return jax.shard_map(
        solution_body,
        mesh=mesh,
        in_specs=(batch,) * 5 + (matrix,) * 6 + (vector,) * 9,
        out_specs=(batch,) * 3 + (matrix,) * 6 + (vector,) * 9,
        check_vma=False,
    )
```
